256 devices in a mesh: seq: 16 (over z_hi, y), head: 4 (over x), prompt: 4 (over z_lo, core).
Axes of the slice: x: 4, y: 4, z: 8 (z_hi: 4, z_lo: 2; z = z_hi * 2 + z_lo), core: 2. Of those that a mesh axis runs over, the one named last changes fastest.
Arguments:
- heads_pre: bfloat16 [8192, 16384], P(('prompt', 'seq'), 'head'), parts along dimension 0, may hold values from -6 to 6
- maps_pre: bfloat16 [8192, 2, 2048], P(('prompt', 'seq'), None, 'head'), parts along dimension 0, may hold values from -6 to 6
- step_prompt: float32 [8192, 256], P(('prompt', 'seq'), 'head'), parts along dimension 0, may hold values from 0 to 0.3, as said below
- head_rate: float32 [256], P('head'), may hold values from 0.5 to 1
- skip_gain: float32 [256], P('head'), may hold values from 0.5 to 1.5
- conv_head_taps: float32 [4, 16384], P(None, 'head'), may hold values from -3 to 3
- conv_head_bias: float32 [16384], P('head'), may hold values from -3 to 3
- conv_map_taps: float32 [4, 2, 2048], P(None, None, 'head'), may hold values from -3 to 3
- filter_mapping_offset: float32 [2, 2048], P(None, 'head'), may hold values from -3 to 3
- heads_dec: bfloat16 [64, 4, 16384], P(('prompt', 'seq'), None, 'head'), parts along dimension 0, may hold values from -6 to 6
- maps_dec: bfloat16 [64, 4, 2, 2048], P(('prompt', 'seq'), None, None, 'head'), parts along dimension 0, may hold values from -6 to 6
- step_dec: float32 [64, 4, 256], P(('prompt', 'seq'), None, 'head'), parts along dimension 0, may hold values from 0.01 to 0.3
Outputs:
- prompt_out: bfloat16 [8192, 16384], P(('prompt', 'seq'), 'head'), parts along dimension 0
- sample_out: bfloat16 [64, 4, 16384], P(('prompt', 'seq'), None, 'head'), parts along dimension 0
The draws below stay inside these ranges and needn't reach their ends.
There are 4 independent parts, one for each index of `prompt`. The reference program is written for one: setup_inputs(seed, part) draws one part's arguments, and reference() takes and returns one part's arrays. A program takes and returns all parts, laid end to end along the dimension named above; an argument that names none is the same for every part. Nothing has to cross between parts.
Inputs may be any that keep to these rules, and one draw needn't show every extreme that they name: `step_prompt`: step sizes, all positive.
All inputs are finite; a program needn't handle non-finite values.
Results may differ from the reference program's by a relative error of at most 0.0035.
Values may be sent and summed in bfloat16 or wider, within the bound.
A program may use at most 192 MiB of HBM per device.

```python
import math
import jax
import jax.numpy as jnp
from jax import lax

HEADS = 256
HEAD_DIM = 64
STATE = 256
GROUPS = 8
CONV = 4
BLOCK_TOKENS = 128
STEPS = 4
QUERY_WORDS = 2048
SAMPLES = 16


def draw_step_prompt(key, part):
    random_subkeys = jax.random.split(key, 5)
    slow_share = 0.5
    is_slow = jax.random.bernoulli(random_subkeys[0], slow_share, (HEADS,))
    spread = jax.random.uniform(random_subkeys[1], (HEADS,), jnp.float32)
    gradual_baseline = 0.05 / QUERY_WORDS * jnp.exp(spread * math.log(3.0))
    fast_base = 0.03 * jnp.exp(spread * math.log(3.0))
    jaggedness_level = jnp.exp(jax.random.uniform(random_subkeys[2], (QUERY_WORDS, HEADS), jnp.float32, math.log(0.5), math.log(2.0)))
    block_count = QUERY_WORDS // BLOCK_TOKENS
    quiet_factor = jnp.exp(jax.random.uniform(random_subkeys[3], (block_count, HEADS), jnp.float32, math.log(0.02), 0.0))
    quiet_rows = jnp.repeat(quiet_factor, BLOCK_TOKENS, axis=0)
    spike_length = max(3 * BLOCK_TOKENS // 8, 8)
    half_vocabulary = QUERY_WORDS // 2
    spike_offsets = jax.random.randint(random_subkeys[4], (2,), 0, half_vocabulary - spike_length + 1)
    spike_starts = spike_offsets + jnp.array([0, half_vocabulary], jnp.int32)
    token_positions = jnp.arange(QUERY_WORDS)[:, None]
    within_spike = jnp.any((token_positions >= spike_starts[None, :]) & (token_positions < spike_starts[None, :] + spike_length), axis=1).astype(jnp.float32)
    spike_step = 0.65 / (spike_length * 1.082)
    gradual_steps = (gradual_baseline[None, :] + spike_step * within_spike[:, None]) * jaggedness_level
    fast_steps = fast_base[None, :] * quiet_rows * jaggedness_level
    return jnp.where(is_slow[None, :], gradual_steps, fast_steps)


def shard_levels(key, extent, cuts, smallest, high):
    level = 1.0
    for dim, parts in cuts:
        draws = jax.random.uniform(jax.random.fold_in(jax.random.fold_in(key, 6), dim), (parts,), jnp.float32, smallest / len(cuts), high / len(cuts))
        level = level * jnp.repeat(jnp.exp(draws), extent[dim] // parts).reshape((-1,) + (1,) * (len(extent) - 1 - dim))
    return level


def bell_draw(stream_key, dims, scale, bound, shards=(), dtype=jnp.bfloat16):
    factor_of = shard_levels(stream_key, dims, shards, -0.22, 0.18) if shards else 1.0
    values = jax.random.normal(stream_key, dims, jnp.float32) * scale * factor_of
    return jnp.minimum(jnp.maximum(values, -bound), bound).astype(dtype)


def setup_inputs(seed: int = 0, part: int = 0) -> dict:
    arg_keys = jax.random.split(jax.random.key(seed), 13)
    part_keys = jax.random.split(jax.random.fold_in(arg_keys[12], part), 13)
    return {
        "heads_pre": bell_draw(part_keys[0], (QUERY_WORDS, HEADS * HEAD_DIM), 1.0, 6.0, ((0, 16), (1, 4))),
        "maps_pre": bell_draw(part_keys[1], (QUERY_WORDS, 2, GROUPS * STATE), 1.0, 6.0, ((0, 16), (2, 4))),
        "step_prompt": draw_step_prompt(jax.random.fold_in(jax.random.fold_in(arg_keys[12], part), 71), part),
        "head_rate": jnp.clip(jnp.exp(math.log(1.0) - 0.6931472 * jax.random.uniform(arg_keys[3], (HEADS,), jnp.float32) ** shard_levels(arg_keys[3], (HEADS,), ((0, 4),), -0.2, 0.2)), 0.5, 1.0),
        "skip_gain": jnp.clip(0.5 + 1.0 * jax.random.uniform(arg_keys[4], (HEADS,), jnp.float32) ** shard_levels(arg_keys[4], (HEADS,), ((0, 4),), -0.2, 0.2), 0.5, 1.5),
        "conv_head_taps": bell_draw(arg_keys[5], (CONV, HEADS * HEAD_DIM), CONV ** -0.5, 3.0, ((1, 4),), jnp.float32),
        "conv_head_bias": bell_draw(arg_keys[6], (HEADS * HEAD_DIM,), 0.5, 3.0, ((0, 4),), jnp.float32),
        "conv_map_taps": bell_draw(arg_keys[7], (CONV, 2, GROUPS * STATE), CONV ** -0.5, 3.0, ((2, 4),), jnp.float32),
        "filter_mapping_offset": bell_draw(arg_keys[8], (2, GROUPS * STATE), 0.5, 3.0, ((1, 4),), jnp.float32),
        "heads_dec": bell_draw(part_keys[9], (SAMPLES, STEPS, HEADS * HEAD_DIM), 1.0, 6.0, ((0, 16), (2, 4))),
        "maps_dec": bell_draw(part_keys[10], (SAMPLES, STEPS, 2, GROUPS * STATE), 1.0, 6.0, ((0, 16), (3, 4))),
        "step_dec": jnp.clip(jnp.exp(math.log(0.3) - 3.4011974 * jax.random.uniform(part_keys[11], (SAMPLES, STEPS, HEADS), jnp.float32) ** shard_levels(part_keys[11], (SAMPLES, STEPS, HEADS), ((0, 16), (2, 4)), -0.2, 0.2)), 0.01, 0.3),
    }


def conv_silu(padded, conv_weight, conv_bias, sequence_length):
    summed = conv_bias + conv_weight[0] * padded[0:sequence_length].astype(jnp.float32)
    for offset in range(1, CONV):
        summed = summed + conv_weight[offset] * padded[offset:offset + sequence_length].astype(jnp.float32)
    return jax.nn.silu(summed).astype(jnp.bfloat16)


def rounded(value):
    return lax.optimization_barrier(value.astype(jnp.bfloat16)).astype(jnp.float32)


def reference(heads_pre, maps_pre, step_prompt, head_rate, skip_gain, conv_head_taps, conv_head_bias, conv_map_taps, filter_mapping_offset, heads_dec, maps_dec, step_dec):
    per_group = HEADS // GROUPS
    x_conv = conv_silu(jnp.concatenate([jnp.zeros((CONV - 1, HEADS * HEAD_DIM), jnp.bfloat16), heads_pre], 0), conv_head_taps, conv_head_bias, QUERY_WORDS)
    bc_conv = conv_silu(jnp.concatenate([jnp.zeros((CONV - 1, 2, GROUPS * STATE), jnp.bfloat16), maps_pre], 0), conv_map_taps, filter_mapping_offset, QUERY_WORDS)
    blocks = QUERY_WORDS // BLOCK_TOKENS
    x_blocks = x_conv.reshape(blocks, BLOCK_TOKENS, GROUPS, per_group, HEAD_DIM)
    in_maps = bc_conv[:, 0].reshape(blocks, BLOCK_TOKENS, GROUPS, STATE)
    result_mappings = bc_conv[:, 1].reshape(blocks, BLOCK_TOKENS, GROUPS, STATE)
    step_block_list = step_prompt.reshape(blocks, BLOCK_TOKENS, GROUPS, per_group)
    decay_rate = head_rate.reshape(GROUPS, per_group)
    skip_heads = skip_gain.reshape(GROUPS, per_group)
    causal = jnp.arange(BLOCK_TOKENS)[:, None] >= jnp.arange(BLOCK_TOKENS)[None, :]

    def one_block(ssm_state, pieces):
        x_block, in_map, out_map, step_size = pieces
        log_decay = jnp.cumsum(-step_size * decay_rate, axis=0)
        log_columns = jnp.moveaxis(log_decay, 0, -1)
        logarithmic_spacings = log_columns[..., :, None] - log_columns[..., None, :]
        decay_mat = jnp.exp(jnp.where(causal, logarithmic_spacings, -jnp.inf))
        scores = jnp.einsum('qgn,sgn->gqs', out_map.astype(jnp.float32), in_map.astype(jnp.float32))
        mixing = rounded(scores[:, None] * decay_mat * jnp.moveaxis(step_size, 0, -1)[..., None, :])
        x_wide = x_block.astype(jnp.float32)
        y_inner = jnp.einsum('gjqs,sgjp->qgjp', mixing, x_wide)
        entry_low = rounded(ssm_state)
        y_cross = jnp.exp(log_decay)[..., None] * jnp.einsum('qgn,gjpn->qgjp', out_map.astype(jnp.float32), entry_low)
        output = (y_inner + y_cross + skip_heads[..., None] * x_wide).astype(jnp.bfloat16)
        weights = jnp.exp(log_decay[-1] - log_decay) * step_size
        weighted = rounded(x_wide * weights[..., None])
        block_state = jnp.einsum('qgjp,qgn->gjpn', weighted, in_map.astype(jnp.float32))
        ssm_state = jnp.exp(log_decay[-1])[..., None, None] * ssm_state + block_state
        return ssm_state, output

    start_state = jnp.zeros((GROUPS, per_group, HEAD_DIM, STATE), jnp.float32)
    final_state, outputs = lax.scan(one_block, start_state, (x_blocks, in_maps, result_mappings, step_block_list))
    prompt_out = outputs.reshape(QUERY_WORDS, HEADS * HEAD_DIM)
    tail_x = heads_pre[QUERY_WORDS - CONV + 1:]
    tail_bc = maps_pre[QUERY_WORDS - CONV + 1:]

    def one_sample(x_new, bc_new, step_new):
        dx_conv = conv_silu(jnp.concatenate([tail_x, x_new], 0), conv_head_taps, conv_head_bias, STEPS)
        dbc_conv = conv_silu(jnp.concatenate([tail_bc, bc_new], 0), conv_map_taps, filter_mapping_offset, STEPS)
        ssm_state = final_state
        rows_out = []
        for position in range(STEPS):
            x_step = dx_conv[position].reshape(GROUPS, per_group, HEAD_DIM).astype(jnp.float32)
            in_step = dbc_conv[position, 0].reshape(GROUPS, STATE).astype(jnp.float32)
            out_step = dbc_conv[position, 1].reshape(GROUPS, STATE).astype(jnp.float32)
            step_size = step_new[position].reshape(GROUPS, per_group)
            ssm_state = jnp.exp(-step_size * decay_rate)[..., None, None] * ssm_state + (step_size[..., None] * x_step)[..., None] * in_step[:, None, None, :]
            output = jnp.sum(ssm_state * out_step[:, None, None, :], axis=-1) + skip_heads[..., None] * x_step
            rows_out.append(output.astype(jnp.bfloat16).reshape(HEADS * HEAD_DIM))
        return jnp.stack(rows_out)

    sample_out = jax.vmap(one_sample)(heads_dec, maps_dec, step_dec)
    return prompt_out, sample_out
```

```python
import functools

import jax
import jax.numpy as jnp
from jax import lax
from jax.experimental import pallas as pl
from jax.experimental.pallas import tpu as pltpu
from jax.sharding import PartitionSpec as P

HEAD_DIM = 64
STATE = 256
CONV = 4
BLOCK = 128
STEPS = 4
ROW = 4
RING = 16
HEADS_Q = 16
CHAN_Q = HEADS_Q * HEAD_DIM
CHUNKS = 4
WIDTH = CHAN_Q // CHUNKS
HALO = 16
MESH = pl.DeviceIdType.MESH
F32 = jnp.float32
BF16 = jnp.bfloat16
HIGH = lax.Precision.HIGHEST


def silu(v):
    return v * (1.0 / (1.0 + jnp.exp(-v)))


def iota(shape, dim):
    return lax.broadcasted_iota(jnp.int32, shape, dim)


def conv_rows(xin, taps, bias):
    total = bias + taps[0] * pltpu.roll(xin, 3, 0)[HALO:]
    total = total + taps[1] * pltpu.roll(xin, 2, 0)[HALO:]
    total = total + taps[2] * pltpu.roll(xin, 1, 0)[HALO:]
    total = total + taps[3] * xin[HALO:]
    return silu(total)


def conv_cyclic(xin, taps, bias):
    total = bias + taps[0] * pltpu.roll(xin, 3, 0)
    total = total + taps[1] * pltpu.roll(xin, 2, 0)
    total = total + taps[2] * pltpu.roll(xin, 1, 0)
    total = total + taps[3] * xin
    return silu(total)


def kernel(
    x_ref,
    bc_ref,
    st_ref,
    dec_ref,
    decs_ref,
    par_ref,
    parm_ref,
    out_ref,
    dout_ref,
    xbuf,
    bcbuf,
    st_s,
    decbuf,
    decsbuf,
    xc,
    bcc,
    bt,
    scores,
    tri,
    madd,
    cum_t,
    cumcol,
    wexp,
    ecexp,
    yacc,
    local_s,
    total_s,
    cin,
    cout,
    outbuf,
    doutbuf,
    lsem,
    lout_sem,
    sx,
    rx,
    sbc,
    rbc,
    sst,
    rst,
    shalo,
    rhalo,
    sdec,
    rdec,
    scar,
    rcar,
    sout,
    rout,
    sdo,
    rdo,
):
    me = lax.axis_index("seq")
    z = me // ROW
    y = me % ROW
    group = y // 2
    base = ROW * z

    def row_peer(k):
        return lax.rem(y + k, ROW)

    def from_peer(k):
        return lax.rem(y + ROW - k, ROW)

    def rows_of(b):
        return pl.ds(pl.multiple_of(b * BLOCK, BLOCK), BLOCK)

    def in_rows(b):
        return pl.ds(pl.multiple_of(HALO + b * BLOCK, HALO), BLOCK)

    def cols_of(c):
        return pl.ds(pl.multiple_of(c * WIDTH, WIDTH), WIDTH)

    def quarter_cols(q, c):
        return pl.ds(pl.multiple_of(q * CHAN_Q + c * WIDTH, WIDTH), WIDTH)

    def quarter(q):
        return pl.ds(pl.multiple_of(q * CHAN_Q, CHAN_Q), CHAN_Q)

    def remote(src, dst, send, recv, seq):
        return pltpu.make_async_remote_copy(
            src_ref=src,
            dst_ref=dst,
            send_sem=send,
            recv_sem=recv,
            device_id={"seq": seq},
            device_id_type=MESH,
        )

    def x_copy(k, c):
        q = row_peer(k)
        return remote(
            x_ref.at[:, quarter_cols(q, c)],
            xbuf.at[in_rows(y), cols_of(c)],
            sx.at[k, c],
            rx.at[k, c],
            base + q,
        )

    def x_arrival(k, c):
        return remote(
            x_ref.at[:, quarter_cols(y, c)],
            xbuf.at[in_rows(from_peer(k)), cols_of(c)],
            sx.at[k, c],
            rx.at[k, c],
            base + from_peer(k),
        )

    def bc_copy(k):
        q = row_peer(k)
        return remote(bc_ref.at[q // 2], bcbuf.at[in_rows(y)], sbc.at[k], rbc.at[k], base + q)

    def bc_arrival(k):
        src = from_peer(k)
        return remote(bc_ref.at[group], bcbuf.at[in_rows(src)], sbc.at[k], rbc.at[k], base + src)

    def st_copy(k):
        q = row_peer(k)
        return remote(st_ref.at[q], st_s.at[y], sst.at[k], rst.at[k], base + q)

    def st_arrival(k):
        src = from_peer(k)
        return remote(st_ref.at[y], st_s.at[src], sst.at[k], rst.at[k], base + src)

    def halo_x(q, seq):
        return remote(
            x_ref.at[pl.ds(BLOCK - HALO, HALO), quarter(q)],
            xbuf.at[pl.ds(0, HALO)],
            shalo.at[0, q],
            rhalo.at[0],
            seq,
        )

    def halo_bc(q, seq):
        return remote(
            bc_ref.at[q // 2, pl.ds(BLOCK - HALO, HALO)],
            bcbuf.at[pl.ds(0, HALO)],
            shalo.at[1, q],
            rhalo.at[1],
            seq,
        )

    def dec_copy(q, sample):
        return remote(dec_ref.at[q], decbuf.at[sample], sdec.at[0, q], rdec.at[0, sample], 12 + q)

    def decs_copy(q, sample):
        return remote(decs_ref.at[q], decsbuf.at[sample], sdec.at[1, q], rdec.at[1, sample], 12 + q)

    own_dec = pltpu.make_async_copy(dec_ref.at[y], decbuf.at[me], lsem.at[3])
    own_decs = pltpu.make_async_copy(decs_ref.at[y], decsbuf.at[me], lsem.at[4])

    def carry_copy(c, seq):
        return remote(cout.at[c], cin.at[c], scar.at[c], rcar.at[c], seq)

    def out_copy(k, c):
        b = row_peer(k)
        return remote(
            outbuf.at[rows_of(b), cols_of(c)],
            out_ref.at[:, quarter_cols(y, c)],
            sout.at[k, c],
            rout.at[k, c],
            base + b,
        )

    def out_arrival(k, c):
        src = from_peer(k)
        return remote(
            outbuf.at[rows_of(y), cols_of(c)],
            out_ref.at[:, quarter_cols(src, c)],
            sout.at[k, c],
            rout.at[k, c],
            base + src,
        )

    def out_own(c):
        return pltpu.make_async_copy(
            outbuf.at[rows_of(y), cols_of(c)], out_ref.at[:, quarter_cols(y, c)], lout_sem.at[c]
        )

    def dout_copy(sample):
        return remote(
            doutbuf.at[sample], dout_ref.at[:, quarter(y)], sdo.at[sample], rdo.at[y], sample
        )

    def dout_arrival(q):
        return remote(doutbuf.at[me], dout_ref.at[:, quarter(q)], sdo.at[me], rdo.at[q], 12 + q)

    own_dout = pltpu.make_async_copy(doutbuf.at[me], dout_ref.at[:, quarter(y)], lsem.at[5])

    own_x = pltpu.make_async_copy(x_ref.at[:, quarter(y)], xbuf.at[in_rows(y)], lsem.at[0])
    own_bc = pltpu.make_async_copy(bc_ref.at[group], bcbuf.at[in_rows(y)], lsem.at[1])
    own_st = pltpu.make_async_copy(st_ref.at[y], st_s.at[y], lsem.at[2])

    barrier = pltpu.get_barrier_semaphore()
    for k in range(1, RING):
        pl.semaphore_signal(
            barrier, inc=1, device_id={"seq": lax.rem(me + k, RING)}, device_id_type=MESH
        )
    own_st.start()
    own_bc.start()
    own_x.start()

    r_i, c_i = iota((BLOCK, BLOCK), 0), iota((BLOCK, BLOCK), 1)
    same = (r_i // 8) == (c_i // 8)
    tri[0] = jnp.where(r_i <= c_i, 1.0, 0.0).astype(F32)
    tri[1] = jnp.where((r_i <= c_i) & same, 1.0, 0.0).astype(F32)
    madd[0] = jnp.where(r_i >= c_i, 0.0, -1e30).astype(F32)
    madd[1] = jnp.where((r_i >= c_i) & same, 0.0, -1e30).astype(F32)

    pl.semaphore_wait(barrier, RING - 1)

    for k in range(1, ROW):
        st_copy(k).start()
    for k in range(1, ROW):
        bc_copy(k).start()

    @pl.when((y == ROW - 1) & (z < ROW - 1))
    def _():
        for q in range(ROW):
            halo_bc(q, base + ROW + q).start()
            halo_x(q, base + ROW + q).start()

    for c in range(CHUNKS):
        for k in range(1, ROW):
            x_copy(k, c).start()

    for q in range(ROW):

        @pl.when(me != 12 + q)
        def _(q=q):
            dec_copy(q, me).start()
            decs_copy(q, me).start()

    @pl.when(z == ROW - 1)
    def _():
        own_dec.start()
        own_decs.start()

    @pl.when(z == 0)
    def _():
        xbuf[pl.ds(0, HALO)] = jnp.zeros((HALO, CHAN_Q), BF16)
        bcbuf[pl.ds(0, HALO)] = jnp.zeros((HALO, 2 * STATE), BF16)
        cin[...] = jnp.zeros_like(cin)

    lane = iota((BLOCK, BLOCK), 1)
    left = lane < HEAD_DIM

    def steps_of(b, m):
        step = st_s[b, 0:HEADS_Q]
        drop = st_s[b, HEADS_Q : 2 * HEADS_Q]
        cum = jnp.dot(drop, tri[m], precision=HIGH, preferred_element_type=F32)
        cum_t[b] = cum
        weight = jnp.exp(cum[:, BLOCK - 1 : BLOCK] - cum) * step
        stack = jnp.concatenate(
            [cum, weight, jnp.exp(cum), jnp.zeros((BLOCK - 3 * HEADS_Q, BLOCK), F32)], axis=0
        )
        turned = jnp.transpose(stack)
        for c in range(CHUNKS):
            shift = (BLOCK - c * (HEADS_Q // CHUNKS)) % BLOCK
            cumcol[c, b] = pltpu.roll(turned, shift, 1) if shift else turned
        for j in range(HEADS_Q // 2):
            cols = pl.ds(j * BLOCK, BLOCK)

            def pair(first):
                one = jnp.broadcast_to(turned[:, first : first + 1], (BLOCK, BLOCK))
                two = jnp.broadcast_to(turned[:, first + 1 : first + 2], (BLOCK, BLOCK))
                return jnp.where(left, one, two)

            wexp[rows_of(b), cols] = pair(HEADS_Q + 2 * j)
            ecexp[rows_of(b), cols] = pair(2 * HEADS_Q + 2 * j)

    def maps_of(b, conv):
        low = conv.astype(BF16)
        bcc[rows_of(b)] = low
        bt[b] = jnp.transpose(conv[:, 0:STATE]).astype(BF16)
        scores[b] = lax.dot_general(
            low[:, STATE:], low[:, 0:STATE], (((1,), (1,)), ((), ())), preferred_element_type=F32
        )

    own_st.wait()
    for k in range(1, ROW):
        st_arrival(k).wait_recv()

    @pl.loop(0, ROW)
    def _(b):
        steps_of(b, 0)

    own_bc.wait()
    for k in range(1, ROW):
        bc_arrival(k).wait_recv()

    @pl.when(z > 0)
    def _():
        halo_bc(y, me).wait_recv()
        halo_x(y, me).wait_recv()

    map_par = parm_ref[group]
    map_taps = [map_par[j : j + 1] for j in range(CONV)]
    map_bias = map_par[CONV : CONV + 1]

    @pl.loop(0, ROW)
    def _(b):
        rows = pl.ds(pl.multiple_of(b * BLOCK, BLOCK), BLOCK + HALO)
        maps_of(b, conv_rows(bcbuf[rows].astype(F32), map_taps, map_bias))

    own_x.wait()

    def chan_taps(c):
        cols = quarter_cols(y, c)
        return [par_ref[pl.ds(j, 1), cols] for j in range(CONV)], par_ref[pl.ds(CONV, 1), cols]

    def gain(b, cols):
        return ecexp[pl.ds(b * BLOCK + BLOCK - 1, 1), cols]

    @pl.loop(0, CHUNKS)
    def _(c):
        for k in range(1, ROW):
            x_arrival(k, c).wait_recv()
        cols = cols_of(c)
        taps, bias = chan_taps(c)
        state = None
        for b in range(ROW):
            xin = xbuf[pl.ds(b * BLOCK, BLOCK + HALO), cols].astype(F32)
            low = conv_rows(xin, taps, bias).astype(BF16)
            xc[pl.ds(b * BLOCK, BLOCK), cols] = low
            weighted = (low.astype(F32) * wexp[pl.ds(b * BLOCK, BLOCK), cols]).astype(BF16)
            block_state = jnp.dot(bt[b], weighted, preferred_element_type=F32)
            state = block_state if b == 0 else gain(b, cols) * state + block_state
            if b < ROW - 1:
                local_s[b, :, cols] = state
            else:
                total_s[:, cols] = state

        @pl.when(z == 0)
        def _():
            cout[c] = total_s[:, cols].astype(BF16)
            carry_copy(c, me + ROW).start()

    blocks = jnp.where(z == ROW - 1, ROW + 1, ROW)

    @pl.when(z == ROW - 1)
    def _():
        own_dec.wait()
        own_decs.wait()

        @pl.loop(0, RING)
        def _(s):
            @pl.when(s != me)
            def _():
                dec_copy(y, s).wait_recv()
                decs_copy(y, s).wait_recv()

        new_rows = (iota((RING, 8, 1), 1)) < STEPS

        def with_tail(new, tail):
            full = jnp.where(new_rows, new, tail[None])
            return full.reshape(BLOCK, full.shape[-1])

        st_s[ROW] = jnp.transpose(decsbuf[...].reshape(BLOCK, BLOCK))[0 : 2 * HEADS_Q]
        steps_of(ROW, 1)
        tail = bcbuf[pl.ds(ROW * BLOCK, HALO)].astype(F32)[8:16]
        maps_of(
            ROW,
            conv_cyclic(
                with_tail(decbuf[:, :, pl.ds(CHAN_Q, 2 * STATE)].astype(F32), tail), map_taps, map_bias
            ),
        )

        @pl.loop(0, CHUNKS)
        def _(c):
            cols = cols_of(c)
            taps, bias = chan_taps(c)
            tail = xbuf[pl.ds(ROW * BLOCK, HALO), cols].astype(F32)[8:16]
            conv = conv_cyclic(with_tail(decbuf[:, :, cols].astype(F32), tail), taps, bias)
            xc[pl.ds(ROW * BLOCK, BLOCK), cols] = conv.astype(BF16)

    @pl.loop(0, CHUNKS)
    def _(c):
        @pl.loop(0, blocks)
        def _(b):
            m = b // ROW
            mask = madd[m]
            score = scores[b]
            columns = cumcol[c, b]
            for pair in range(2):
                mixes = []
                for j in (2 * pair, 2 * pair + 1):
                    head = c * (HEADS_Q // CHUNKS) + j
                    row = cum_t[b, pl.ds(head, 1)]
                    step = st_s[b, pl.ds(head, 1)]
                    gap = columns[:, j : j + 1] - row + mask
                    mixes.append((score * jnp.exp(gap) * step).astype(BF16))
                mixing = jnp.concatenate(mixes, axis=1)
                cols = pl.ds(pl.multiple_of(c * WIDTH + pair * BLOCK, BLOCK), BLOCK)
                xp = xc[rows_of(b), cols].astype(F32)
                blockdiag = jnp.concatenate(
                    [jnp.where(left, xp, 0.0).astype(BF16), jnp.where(left, 0.0, xp).astype(BF16)],
                    axis=0,
                )
                inner = jnp.dot(mixing, blockdiag, preferred_element_type=F32)
                skip_cols = pl.ds(
                    pl.multiple_of(y * CHAN_Q + c * WIDTH + pair * BLOCK, BLOCK), BLOCK
                )
                yacc[rows_of(b), cols] = inner + par_ref[pl.ds(CONV + 1, 1), skip_cols] * xp

    @pl.loop(0, CHUNKS)
    def _(c):
        cols = cols_of(c)

        @pl.when(z > 0)
        def _():
            carry_copy(c, me).wait_recv()

        carry = cin[c].astype(F32)
        gains = [gain(b, cols) for b in range(ROW)]
        leads = [gains[0]]
        for b in range(1, ROW):
            leads.append(leads[-1] * gains[b])

        @pl.when((z > 0) & (z < ROW - 1))
        def _():
            cout[c] = (total_s[:, cols] + leads[ROW - 1] * carry).astype(BF16)
            carry_copy(c, me + ROW).start()

        for b in range(ROW):
            rows = pl.ds(b * BLOCK, BLOCK)
            if b == 0:
                entry = cin[c]
            else:
                entry = (local_s[b - 1, :, cols] + leads[b - 1] * carry).astype(BF16)
            cross = jnp.dot(bcc[rows, STATE:], entry, preferred_element_type=F32)
            outbuf[rows, cols] = (yacc[rows, cols] + ecexp[rows, cols] * cross).astype(BF16)
        out_own(c).start()
        for k in range(1, ROW):
            out_copy(k, c).start()

        @pl.when(z == ROW - 1)
        def _():
            final = total_s[:, cols] + leads[ROW - 1] * carry
            high = final.astype(BF16)
            rest = (final - high.astype(F32)).astype(BF16)
            rows = pl.ds(ROW * BLOCK, BLOCK)
            maps = bcc[rows, STATE:]
            cross = jnp.dot(maps, high, preferred_element_type=F32) + jnp.dot(
                maps, rest, preferred_element_type=F32
            )
            result = yacc[rows, cols] + ecexp[rows, cols] * cross
            doutbuf[:, :, cols] = result.reshape(RING, 8, WIDTH).astype(BF16)

    @pl.when(z == ROW - 1)
    def _():
        own_dout.start()

        @pl.loop(0, RING)
        def _(s):
            @pl.when(s != me)
            def _():
                dout_copy(s).start()

    for c in range(CHUNKS):
        out_own(c).wait()
        for k in range(1, ROW):
            out_arrival(k, c).wait_recv()
    for q in range(ROW):

        @pl.when(me != 12 + q)
        def _(q=q):
            dout_arrival(q).wait_recv()

    for k in range(1, ROW):
        st_copy(k).wait_send()
        bc_copy(k).wait_send()
        for c in range(CHUNKS):
            x_copy(k, c).wait_send()
            out_copy(k, c).wait_send()

    @pl.when((y == ROW - 1) & (z < ROW - 1))
    def _():
        for q in range(ROW):
            halo_bc(q, base + ROW + q).wait_send()
            halo_x(q, base + ROW + q).wait_send()

    for q in range(ROW):

        @pl.when(me != 12 + q)
        def _(q=q):
            dec_copy(q, me).wait_send()
            decs_copy(q, me).wait_send()

    @pl.when(z < ROW - 1)
    def _():
        for c in range(CHUNKS):
            carry_copy(c, me + ROW).wait_send()

    @pl.when(z == ROW - 1)
    def _():
        own_dout.wait()

        @pl.loop(0, RING)
        def _(s):
            @pl.when(s != me)
            def _():
                dout_copy(s).wait_send()


def local(
    heads_pre,
    maps_pre,
    step_prompt,
    head_rate,
    skip_gain,
    conv_head_taps,
    conv_head_bias,
    conv_map_taps,
    filter_mapping_offset,
    heads_dec,
    maps_dec,
    step_dec,
):
    tokens = heads_pre.shape[0]
    channels = heads_pre.shape[1]
    groups = maps_pre.shape[2] // STATE

    bc = maps_pre.reshape(tokens, 2, groups, STATE).transpose(2, 0, 1, 3)
    bc = bc.reshape(groups, tokens, 2 * STATE)
    drop = -step_prompt * head_rate
    steps = jnp.concatenate(
        [step_prompt.T.reshape(ROW, HEADS_Q, tokens), drop.T.reshape(ROW, HEADS_Q, tokens)], axis=1
    )
    skip = jnp.repeat(skip_gain, HEAD_DIM)
    params = jnp.concatenate(
        [conv_head_taps, conv_head_bias[None], skip[None], jnp.zeros((2, channels), F32)], axis=0
    )
    map_params = jnp.concatenate(
        [conv_map_taps, filter_mapping_offset[None], jnp.zeros((3, 2, groups * STATE), F32)], axis=0
    )
    map_params = map_params.reshape(8, 2, groups, STATE).transpose(2, 0, 1, 3)
    map_params = map_params.reshape(groups, 8, 2 * STATE)
    dec_x = heads_dec[0].reshape(STEPS, ROW, CHAN_Q).transpose(1, 0, 2)
    dec_m = maps_dec[0].reshape(STEPS, 2, groups, STATE).transpose(2, 0, 1, 3)
    dec_m = jnp.repeat(dec_m.reshape(groups, STEPS, 2 * STATE), ROW // groups, axis=0)
    dec = jnp.pad(jnp.concatenate([dec_x, dec_m], axis=2), ((0, 0), (0, 8 - STEPS), (0, 0)))
    dec_steps = step_dec[0].reshape(STEPS, ROW, HEADS_Q).transpose(1, 0, 2)
    dec_drop = (-step_dec[0] * head_rate).reshape(STEPS, ROW, HEADS_Q).transpose(1, 0, 2)
    dec_steps = jnp.pad(
        jnp.concatenate([dec_steps, dec_drop], axis=2),
        ((0, 0), (0, 8 - STEPS), (0, BLOCK - 2 * HEADS_Q)),
    )

    any_space = pl.BlockSpec(memory_space=pl.ANY)
    vmem = pl.BlockSpec(memory_space=pltpu.VMEM)
    dma = pltpu.SemaphoreType.DMA
    all_rows = (ROW + 1) * BLOCK
    out, dout = pl.pallas_call(
        kernel,
        out_shape=(
            jax.ShapeDtypeStruct((tokens, channels), BF16),
            jax.ShapeDtypeStruct((8, channels), BF16),
        ),
        in_specs=[any_space] * 5 + [vmem] * 2,
        out_specs=(any_space, any_space),
        scratch_shapes=[
            pltpu.VMEM((HALO + ROW * BLOCK, CHAN_Q), BF16),
            pltpu.VMEM((HALO + ROW * BLOCK, 2 * STATE), BF16),
            pltpu.VMEM((ROW + 1, 2 * HEADS_Q, BLOCK), F32),
            pltpu.VMEM((RING, 8, CHAN_Q + 2 * STATE), BF16),
            pltpu.VMEM((RING, 8, BLOCK), F32),
            pltpu.VMEM((all_rows, CHAN_Q), BF16),
            pltpu.VMEM((all_rows, 2 * STATE), BF16),
            pltpu.VMEM((ROW + 1, STATE, BLOCK), BF16),
            pltpu.VMEM((ROW + 1, BLOCK, BLOCK), F32),
            pltpu.VMEM((2, BLOCK, BLOCK), F32),
            pltpu.VMEM((2, BLOCK, BLOCK), F32),
            pltpu.VMEM((ROW + 1, HEADS_Q, BLOCK), F32),
            pltpu.VMEM((CHUNKS, ROW + 1, BLOCK, BLOCK), F32),
            pltpu.VMEM((all_rows, CHAN_Q), F32),
            pltpu.VMEM((all_rows, CHAN_Q), F32),
            pltpu.VMEM((all_rows, CHAN_Q), F32),
            pltpu.VMEM((ROW - 1, STATE, CHAN_Q), F32),
            pltpu.VMEM((STATE, CHAN_Q), F32),
            pltpu.VMEM((CHUNKS, STATE, WIDTH), BF16),
            pltpu.VMEM((CHUNKS, STATE, WIDTH), BF16),
            pltpu.VMEM((ROW * BLOCK, CHAN_Q), BF16),
            pltpu.VMEM((RING, 8, CHAN_Q), BF16),
            dma((6,)),
            dma((CHUNKS,)),
            dma((ROW, CHUNKS)),
            dma((ROW, CHUNKS)),
            dma((ROW,)),
            dma((ROW,)),
            dma((ROW,)),
            dma((ROW,)),
            dma((2, ROW)),
            dma((2,)),
            dma((2, ROW)),
            dma((2, RING)),
            dma((CHUNKS,)),
            dma((CHUNKS,)),
            dma((ROW, CHUNKS)),
            dma((ROW, CHUNKS)),
            dma((RING,)),
            dma((ROW,)),
        ],
        compiler_params=pltpu.CompilerParams(
            collective_id=0, has_side_effects=True, vmem_limit_bytes=44 << 20
        ),
        name="scan_exchange",
    )(heads_pre, bc, steps, dec, dec_steps, params, map_params)
    return out, dout[None, :STEPS]


def solution(mesh):
    placed = (
        P(("prompt", "seq"), "head"),
        P(("prompt", "seq"), None, "head"),
        P(("prompt", "seq"), "head"),
        P("head"),
        P("head"),
        P(None, "head"),
        P("head"),
        P(None, None, "head"),
        P(None, "head"),
        P(("prompt", "seq"), None, "head"),
        P(("prompt", "seq"), None, None, "head"),
        P(("prompt", "seq"), None, "head"),
    )
    return jax.shard_map(
        local,
        mesh=mesh,
        in_specs=placed,
        out_specs=(P(("prompt", "seq"), "head"), P(("prompt", "seq"), None, "head")),
        check_vma=False,
    )
```

```python
import functools

import jax
import jax.numpy as jnp
from jax import lax
from jax.experimental import pallas as pl
from jax.experimental.pallas import tpu as pltpu
from jax.sharding import PartitionSpec as P

HEAD_DIM = 64
STATE = 256
CONV = 4
BLOCK = 128
STEPS = 4
ROW = 4
RING = 16
HEADS_Q = 16
CHAN_Q = HEADS_Q * HEAD_DIM
CHUNKS = 8
WIDTH = CHAN_Q // CHUNKS
HALO = 8
HEADS_C = HEADS_Q // CHUNKS
MESH = pl.DeviceIdType.MESH
F32 = jnp.float32
BF16 = jnp.bfloat16
HIGH = lax.Precision.HIGHEST


def silu(v):
    return v * (1.0 / (1.0 + jnp.exp(-v)))


def iota(shape, dim):
    return lax.broadcasted_iota(jnp.int32, shape, dim)


def conv_rows(xin, taps, bias):
    total = bias + taps[0] * pltpu.roll(xin, 3, 0)[HALO:]
    total = total + taps[1] * pltpu.roll(xin, 2, 0)[HALO:]
    total = total + taps[2] * pltpu.roll(xin, 1, 0)[HALO:]
    total = total + taps[3] * xin[HALO:]
    return silu(total)


def conv_cyclic(xin, taps, bias):
    total = bias + taps[0] * pltpu.roll(xin, 3, 0)
    total = total + taps[1] * pltpu.roll(xin, 2, 0)
    total = total + taps[2] * pltpu.roll(xin, 1, 0)
    total = total + taps[3] * xin
    return silu(total)


def kernel(
    x_ref,
    bc_ref,
    st_ref,
    dec_ref,
    decs_ref,
    taps_ref,
    bias_ref,
    mtaps_ref,
    mbias_ref,
    rate_ref,
    skip_ref,
    out_ref,
    dout_ref,
    xbuf,
    bcbuf,
    st_s,
    decx,
    decm,
    decs,
    rows8,
    rate_s,
    skip_s,
    turn_s,
    xc,
    bcc,
    bt,
    scores,
    tri,
    madd,
    cum_t,
    cumcol,
    wexp,
    ecexp,
    yacc,
    local_s,
    total_s,
    cin,
    cout,
    outbuf,
    doutbuf,
    lsem,
    lout_sem,
    ldo_sem,
    sx,
    rx,
    sbc,
    rbc,
    sst,
    rst,
    shalo,
    rhalo,
    sdec,
    rdec,
    scar,
    rcar,
    sout,
    rout,
    sdo,
    rdo,
):
    me = lax.axis_index("seq")
    z = me // ROW
    y = me % ROW
    group = y // 2
    base = ROW * z
    last = z == ROW - 1
    lag = jnp.where(last, CHUNKS, 2 * z)

    def row_peer(k):
        return lax.rem(y + k, ROW)

    def from_peer(k):
        return lax.rem(y + ROW - k, ROW)

    def rows_of(b):
        return pl.ds(pl.multiple_of(b * BLOCK, BLOCK), BLOCK)

    def in_rows(b):
        return pl.ds(pl.multiple_of(HALO + b * BLOCK, HALO), BLOCK)

    def cols_of(c):
        return pl.ds(pl.multiple_of(c * WIDTH, WIDTH), WIDTH)

    def quarter_cols(q, c):
        return pl.ds(pl.multiple_of(q * CHAN_Q + c * WIDTH, WIDTH), WIDTH)

    def quarter(q):
        return pl.ds(pl.multiple_of(q * CHAN_Q, CHAN_Q), CHAN_Q)

    def half(m):
        return pl.ds(m * STATE, STATE)

    prompt_rows = pl.ds(0, BLOCK)
    end_rows = pl.ds(BLOCK - HALO, HALO)
    dec_rows = pl.ds(BLOCK, 8)
    before = pl.ds(0, HALO)

    def remote(src, dst, send, recv, seq):
        return pltpu.make_async_remote_copy(
            src_ref=src,
            dst_ref=dst,
            send_sem=send,
            recv_sem=recv,
            device_id={"seq": seq},
            device_id_type=MESH,
        )

    def x_copy(k, c):
        q = row_peer(k)
        return remote(
            x_ref.at[:, quarter_cols(q, c)],
            xbuf.at[in_rows(y), cols_of(c)],
            sx.at[k, c],
            rx.at[k, c],
            base + q,
        )

    def x_arrival(k, c):
        src = from_peer(k)
        return remote(
            x_ref.at[:, quarter_cols(y, c)],
            xbuf.at[in_rows(src), cols_of(c)],
            sx.at[k, c],
            rx.at[k, c],
            base + src,
        )

    def bc_copy(k, m):
        q = row_peer(k)
        return remote(
            bc_ref.at[q // 2, prompt_rows, half(m)],
            bcbuf.at[in_rows(y), half(m)],
            sbc.at[k, m],
            rbc.at[k, m],
            base + q,
        )

    def bc_arrival(k, m):
        src = from_peer(k)
        return remote(
            bc_ref.at[group, prompt_rows, half(m)],
            bcbuf.at[in_rows(src), half(m)],
            sbc.at[k, m],
            rbc.at[k, m],
            base + src,
        )

    def st_copy(k):
        q = row_peer(k)
        return remote(st_ref.at[q], st_s.at[y], sst.at[k], rst.at[k], base + q)

    def st_arrival(k):
        src = from_peer(k)
        return remote(st_ref.at[y], st_s.at[src], sst.at[k], rst.at[k], base + src)

    def halo_x(q, seq):
        return remote(
            x_ref.at[end_rows, quarter(q)], xbuf.at[before], shalo.at[0, q], rhalo.at[0], seq
        )

    def halo_bc(q, seq):
        return remote(
            bc_ref.at[q // 2, end_rows], bcbuf.at[before], shalo.at[1, q], rhalo.at[1], seq
        )

    def dec_copies(q, sample):
        parts = (
            (dec_ref.at[:, quarter(q)], decx.at[sample]),
            (bc_ref.at[q // 2, dec_rows], decm.at[sample]),
            (decs_ref, decs.at[sample]),
        )
        return [
            remote(src, dst, sdec.at[i, q], rdec.at[i, sample], 12 + q)
            for i, (src, dst) in enumerate(parts)
        ]

    own_dec = [
        pltpu.make_async_copy(dec_ref.at[:, quarter(y)], decx.at[me], lsem.at[3]),
        pltpu.make_async_copy(bc_ref.at[group, dec_rows], decm.at[me], lsem.at[4]),
        pltpu.make_async_copy(decs_ref, decs.at[me], lsem.at[5]),
    ]

    def carry_copy(c, seq):
        return remote(cout.at[c], cin.at[c], scar.at[c], rcar.at[c], seq)

    def out_copy(k, c):
        b = row_peer(k)
        return remote(
            outbuf.at[rows_of(b), cols_of(c)],
            out_ref.at[:, quarter_cols(y, c)],
            sout.at[k, c],
            rout.at[k, c],
            base + b,
        )

    def out_arrival(k, c):
        src = from_peer(k)
        return remote(
            outbuf.at[rows_of(y), cols_of(c)],
            out_ref.at[:, quarter_cols(src, c)],
            sout.at[k, c],
            rout.at[k, c],
            base + src,
        )

    def out_own(c):
        return pltpu.make_async_copy(
            outbuf.at[rows_of(y), cols_of(c)], out_ref.at[:, quarter_cols(y, c)], lout_sem.at[c]
        )

    def dout_copy(sample, c):
        return remote(
            doutbuf.at[sample, :, cols_of(c)],
            dout_ref.at[:, quarter_cols(y, c)],
            sdo.at[sample, c],
            rdo.at[y, c],
            sample,
        )

    def dout_arrival(q, c):
        return remote(
            doutbuf.at[me, :, cols_of(c)],
            dout_ref.at[:, quarter_cols(q, c)],
            sdo.at[me, c],
            rdo.at[q, c],
            12 + q,
        )

    def dout_own(c):
        return pltpu.make_async_copy(
            doutbuf.at[me, :, cols_of(c)], dout_ref.at[:, quarter_cols(y, c)], ldo_sem.at[c]
        )

    own_x = pltpu.make_async_copy(x_ref.at[:, quarter(y)], xbuf.at[in_rows(y)], lsem.at[0])
    own_bc = pltpu.make_async_copy(bc_ref.at[group, prompt_rows], bcbuf.at[in_rows(y)], lsem.at[1])
    own_st = pltpu.make_async_copy(st_ref.at[y], st_s.at[y], lsem.at[2])

    barrier = pltpu.get_barrier_semaphore()
    for k in range(1, RING):
        pl.semaphore_signal(
            barrier, inc=1, device_id={"seq": lax.rem(me + k, RING)}, device_id_type=MESH
        )
    own_st.start()
    own_bc.start()
    own_x.start()

    @pl.when(last)
    def _():
        for copy in own_dec:
            copy.start()

    r_i, c_i = iota((BLOCK, BLOCK), 0), iota((BLOCK, BLOCK), 1)
    same = (r_i // 8) == (c_i // 8)
    left = c_i < HEAD_DIM
    tri[0] = jnp.where(r_i <= c_i, 1.0, 0.0).astype(F32)
    tri[1] = jnp.where((r_i <= c_i) & same, 1.0, 0.0).astype(F32)
    madd[0] = jnp.where(r_i >= c_i, 0.0, -1e30).astype(F32)
    madd[1] = jnp.where((r_i >= c_i) & same, 0.0, -1e30).astype(F32)

    def spread(ref):
        wide = jnp.broadcast_to(ref[...], (BLOCK, ref.shape[1]))
        return jnp.transpose(jnp.concatenate([wide, wide], axis=1))

    rate_s[...] = spread(rate_ref)
    skip_s[...] = spread(skip_ref)

    @pl.when(z == 0)
    def _():
        xbuf[before] = jnp.zeros((HALO, CHAN_Q), BF16)
        bcbuf[before] = jnp.zeros((HALO, 2 * STATE), BF16)
        cin[...] = jnp.zeros_like(cin)

    pl.semaphore_wait(barrier, RING - 1)

    for k in range(1, ROW):
        st_copy(k).start()
    for k in range(1, ROW):
        bc_copy(k, 0).start()
    for c in range(CHUNKS):
        for k in range(1, ROW):
            x_copy(k, c).start()
        if c == 0:

            @pl.when((y == ROW - 1) & (z < ROW - 1))
            def _():
                for q in range(ROW):
                    halo_bc(q, base + ROW + q).start()
                    halo_x(q, base + ROW + q).start()

        if c == 1:
            for k in range(1, ROW):
                bc_copy(k, 1).start()

    for q in range(ROW):

        @pl.when(me != 12 + q)
        def _(q=q):
            for copy in dec_copies(q, me):
                copy.start()

    def steps_of(b, m):
        step = st_s[b]
        drop = -(step * rate_s[pl.ds(pl.multiple_of(y * HEADS_Q, HEADS_Q), HEADS_Q)])
        cum = jnp.dot(drop, tri[m], precision=HIGH, preferred_element_type=F32)
        cum_t[b] = cum
        weight = jnp.exp(cum[:, BLOCK - 1 : BLOCK] - cum) * step
        stack = jnp.concatenate(
            [cum, weight, jnp.exp(cum), jnp.zeros((BLOCK - 3 * HEADS_Q, BLOCK), F32)], axis=0
        )
        turned = jnp.transpose(stack)
        for c in range(CHUNKS):
            shift = (BLOCK - c * HEADS_C) % BLOCK
            cumcol[c, b] = pltpu.roll(turned, shift, 1) if shift else turned
        for j in range(HEADS_Q // 2):
            cols = pl.ds(j * BLOCK, BLOCK)

            def pair(first):
                one = jnp.broadcast_to(turned[:, first : first + 1], (BLOCK, BLOCK))
                two = jnp.broadcast_to(turned[:, first + 1 : first + 2], (BLOCK, BLOCK))
                return jnp.where(left, one, two)

            wexp[rows_of(b), cols] = pair(HEADS_Q + 2 * j)
            ecexp[rows_of(b), cols] = pair(2 * HEADS_Q + 2 * j)

    map_cols = pl.ds(pl.multiple_of(group * STATE, STATE), STATE)

    def map_taps(m):
        return [mtaps_ref[j, pl.ds(m, 1), map_cols] for j in range(CONV)], mbias_ref[
            pl.ds(m, 1), map_cols
        ]

    def keep_in(b, conv):
        bcc[rows_of(b), half(0)] = conv.astype(BF16)
        bt[b] = jnp.transpose(conv).astype(BF16)

    def keep_out(b, conv):
        low = conv.astype(BF16)
        bcc[rows_of(b), half(1)] = low
        scores[b] = lax.dot_general(
            low, bcc[rows_of(b), half(0)], (((1,), (1,)), ((), ())), preferred_element_type=F32
        )

    def chan_taps(c):
        cols = quarter_cols(y, c)
        return [taps_ref[pl.ds(j, 1), cols] for j in range(CONV)], bias_ref[:, cols]

    def gain(b, cols):
        return ecexp[pl.ds(b * BLOCK + BLOCK - 1, 1), cols]

    def maps(m, keep):
        taps, bias = map_taps(m)

        @pl.loop(0, ROW)
        def _(b):
            rows = pl.ds(pl.multiple_of(b * BLOCK, BLOCK), BLOCK + HALO)
            keep(b, conv_rows(bcbuf[rows, half(m)].astype(F32), taps, bias))

    own_st.wait()
    for k in range(1, ROW):
        st_arrival(k).wait_recv()

    @pl.loop(0, ROW)
    def _(b):
        steps_of(b, 0)

    own_bc.wait()
    for k in range(1, ROW):
        bc_arrival(k, 0).wait_recv()

    @pl.when(z > 0)
    def _():
        halo_bc(y, me).wait_recv()
        halo_x(y, me).wait_recv()

    maps(0, keep_in)
    own_x.wait()

    def block_states(c):
        for k in range(1, ROW):
            x_arrival(k, c).wait_recv()
        cols = cols_of(c)
        taps, bias = chan_taps(c)
        state = None
        for b in range(ROW):
            xin = xbuf[pl.ds(b * BLOCK, BLOCK + HALO), cols].astype(F32)
            low = conv_rows(xin, taps, bias).astype(BF16)
            xc[pl.ds(b * BLOCK, BLOCK), cols] = low
            weighted = (low.astype(F32) * wexp[pl.ds(b * BLOCK, BLOCK), cols]).astype(BF16)
            block_state = jnp.dot(bt[b], weighted, preferred_element_type=F32)
            state = block_state if b == 0 else gain(b, cols) * state + block_state
            if b < ROW - 1:
                local_s[b, :, cols] = state
            else:
                total_s[:, cols] = state

        @pl.when(z == 0)
        def _():
            cout[c] = total_s[:, cols].astype(BF16)
            carry_copy(c, me + ROW).start()

    def with_tail(new, tail):
        width = new.shape[-1]
        rows8[:, 0:STEPS, 0:width] = new
        rows8[:, STEPS:8, 0:width] = jnp.broadcast_to(tail[None], (RING, 8 - STEPS, width))
        return rows8[:, :, 0:width].reshape(BLOCK, width)

    def decode_inputs():
        for copy in own_dec:
            copy.wait()

        @pl.loop(0, RING)
        def _(s):
            @pl.when(s != me)
            def _():
                for copy in dec_copies(y, s):
                    copy.wait_recv()

        rows8[:, :, 0:BLOCK] = jnp.zeros((RING, 8, BLOCK), F32)
        rows8[:, 0:STEPS, 0:64] = decs[...]
        turn_s[...] = jnp.transpose(rows8[:, :, 0:BLOCK].reshape(BLOCK, BLOCK))
        st_s[ROW] = turn_s[pl.ds(pl.multiple_of(y * HEADS_Q, HEADS_Q), HEADS_Q)]
        steps_of(ROW, 1)
        end = pl.ds(ROW * BLOCK, HALO)
        for m, keep in ((0, keep_in), (1, keep_out)):
            taps, bias = map_taps(m)
            new = decm[:, :, m * STATE : (m + 1) * STATE].astype(F32)[:, 0:STEPS]
            tail = bcbuf[end, half(m)].astype(F32)[STEPS:8]
            keep(ROW, conv_cyclic(with_tail(new, tail), taps, bias))

        @pl.loop(0, CHUNKS)
        def _(c):
            cols = cols_of(c)
            taps, bias = chan_taps(c)
            tail = xbuf[end, cols].astype(F32)[STEPS:8]
            conv = conv_cyclic(with_tail(decx[:, :, cols].astype(F32), tail), taps, bias)
            xc[pl.ds(ROW * BLOCK, BLOCK), cols] = conv.astype(BF16)

    blocks = jnp.where(last, ROW + 1, ROW)

    def inner_part(c):
        @pl.loop(0, blocks)
        def _(b):
            m = b // ROW
            mask = madd[m]
            score = scores[b]
            columns = cumcol[c, b]
            for pair in range(HEADS_C // 2):
                mixes = []
                for j in (2 * pair, 2 * pair + 1):
                    head = c * HEADS_C + j
                    row = cum_t[b, pl.ds(head, 1)]
                    step = st_s[b, pl.ds(head, 1)]
                    gap = columns[:, j : j + 1] - row + mask
                    mixes.append((score * jnp.exp(gap) * step).astype(BF16))
                mixing = jnp.concatenate(mixes, axis=1)
                cols = pl.ds(pl.multiple_of(c * WIDTH + pair * BLOCK, BLOCK), BLOCK)
                xp = xc[rows_of(b), cols].astype(F32)
                blockdiag = jnp.concatenate(
                    [jnp.where(left, xp, 0.0).astype(BF16), jnp.where(left, 0.0, xp).astype(BF16)],
                    axis=0,
                )
                inner = jnp.dot(mixing, blockdiag, preferred_element_type=F32)
                head = y * HEADS_Q + c * HEADS_C + 2 * pair
                skip = jnp.where(
                    left[0:1], skip_s[pl.ds(head, 1)], skip_s[pl.ds(head + 1, 1)]
                )
                yacc[rows_of(b), cols] = inner + skip * xp

    def with_carry(c):
        cols = cols_of(c)

        @pl.when(z > 0)
        def _():
            carry_copy(c, me).wait_recv()

        leads = [gain(0, cols)]
        for b in range(1, ROW):
            leads.append(leads[-1] * gain(b, cols))

        @pl.when((z > 0) & (z < ROW - 1))
        def _():
            cout[c] = (total_s[:, cols] + leads[ROW - 1] * cin[c].astype(F32)).astype(BF16)
            carry_copy(c, me + ROW).start()

        inner_part(c)
        carry = cin[c].astype(F32)
        for b in range(ROW):
            rows = pl.ds(b * BLOCK, BLOCK)
            if b == 0:
                entry = cin[c]
            else:
                entry = (local_s[b - 1, :, cols] + leads[b - 1] * carry).astype(BF16)
            cross = jnp.dot(bcc[rows, half(1)], entry, preferred_element_type=F32)
            outbuf[rows, cols] = (yacc[rows, cols] + ecexp[rows, cols] * cross).astype(BF16)
        out_own(c).start()
        for k in range(1, ROW):
            out_copy(k, c).start()

        @pl.when(last)
        def _():
            final = total_s[:, cols] + leads[ROW - 1] * carry
            high = final.astype(BF16)
            rest = (final - high.astype(F32)).astype(BF16)
            rows = pl.ds(ROW * BLOCK, BLOCK)
            out_map = bcc[rows, half(1)]
            cross = jnp.dot(out_map, high, preferred_element_type=F32) + jnp.dot(
                out_map, rest, preferred_element_type=F32
            )
            result = yacc[rows, cols] + ecexp[rows, cols] * cross
            rows8[:, :, 0:WIDTH] = result.reshape(RING, 8, WIDTH)
            doutbuf[:, :, cols] = rows8[:, 0:STEPS, 0:WIDTH].astype(BF16)
            dout_own(c).start()

            @pl.loop(0, RING)
            def _(s):
                @pl.when(s != me)
                def _():
                    dout_copy(s, c).start()

    @pl.loop(0, CHUNKS + lag)
    def _(i):
        @pl.when(i < CHUNKS)
        def _():
            block_states(i)

        @pl.when(i == lag)
        def _():
            for k in range(1, ROW):
                bc_arrival(k, 1).wait_recv()
            maps(1, keep_out)

            @pl.when(last)
            def _():
                decode_inputs()

        @pl.when(i >= lag)
        def _():
            with_carry(i - lag)

    @pl.loop(0, CHUNKS)
    def _(c):
        out_own(c).wait()
        for k in range(1, ROW):
            out_arrival(k, c).wait_recv()
        for q in range(ROW):

            @pl.when(me != 12 + q)
            def _(q=q):
                dout_arrival(q, c).wait_recv()

        @pl.when(last)
        def _():
            dout_own(c).wait()

    for k in range(1, ROW):
        st_copy(k).wait_send()
        for m in range(2):
            bc_copy(k, m).wait_send()

    @pl.loop(0, CHUNKS)
    def _(c):
        for k in range(1, ROW):
            x_copy(k, c).wait_send()
            out_copy(k, c).wait_send()

        @pl.when(z < ROW - 1)
        def _():
            carry_copy(c, me + ROW).wait_send()

        @pl.when(last)
        def _():
            @pl.loop(0, RING)
            def _(s):
                @pl.when(s != me)
                def _():
                    dout_copy(s, c).wait_send()

    @pl.when((y == ROW - 1) & (z < ROW - 1))
    def _():
        for q in range(ROW):
            halo_bc(q, base + ROW + q).wait_send()
            halo_x(q, base + ROW + q).wait_send()

    for q in range(ROW):

        @pl.when(me != 12 + q)
        def _(q=q):
            for copy in dec_copies(q, me):
                copy.wait_send()


def local(
    heads_pre,
    maps_pre,
    step_prompt,
    head_rate,
    skip_gain,
    conv_head_taps,
    conv_head_bias,
    conv_map_taps,
    filter_mapping_offset,
    heads_dec,
    maps_dec,
    step_dec,
):
    tokens, channels = heads_pre.shape
    groups = maps_pre.shape[2] // STATE
    heads = step_prompt.shape[1]

    bc = jnp.concatenate(
        [maps_pre, maps_dec[0], jnp.zeros((8 - STEPS,) + maps_pre.shape[1:], BF16)], axis=0
    )
    bc = bc.reshape(tokens + 8, 2, groups, STATE).transpose(2, 0, 1, 3)
    bc = bc.reshape(groups, tokens + 8, 2 * STATE)
    steps = step_prompt.T.reshape(ROW, HEADS_Q, tokens)

    any_space = pl.BlockSpec(memory_space=pl.ANY)
    vmem = pl.BlockSpec(memory_space=pltpu.VMEM)
    dma = pltpu.SemaphoreType.DMA
    all_rows = (ROW + 1) * BLOCK
    out, dout = pl.pallas_call(
        kernel,
        out_shape=(
            jax.ShapeDtypeStruct((tokens, channels), BF16),
            jax.ShapeDtypeStruct((STEPS, channels), BF16),
        ),
        in_specs=[any_space] * 5 + [vmem] * 6,
        out_specs=(any_space, any_space),
        scratch_shapes=[
            pltpu.VMEM((HALO + ROW * BLOCK, CHAN_Q), BF16),
            pltpu.VMEM((HALO + ROW * BLOCK, 2 * STATE), BF16),
            pltpu.VMEM((ROW + 1, HEADS_Q, BLOCK), F32),
            pltpu.VMEM((RING, STEPS, CHAN_Q), BF16),
            pltpu.VMEM((RING, 8, 2 * STATE), BF16),
            pltpu.VMEM((RING, STEPS, heads), F32),
            pltpu.VMEM((RING, 8, STATE), F32),
            pltpu.VMEM((BLOCK, BLOCK), F32),
            pltpu.VMEM((BLOCK, BLOCK), F32),
            pltpu.VMEM((BLOCK, BLOCK), F32),
            pltpu.VMEM((all_rows, CHAN_Q), BF16),
            pltpu.VMEM((all_rows, 2 * STATE), BF16),
            pltpu.VMEM((ROW + 1, STATE, BLOCK), BF16),
            pltpu.VMEM((ROW + 1, BLOCK, BLOCK), F32),
            pltpu.VMEM((2, BLOCK, BLOCK), F32),
            pltpu.VMEM((2, BLOCK, BLOCK), F32),
            pltpu.VMEM((ROW + 1, HEADS_Q, BLOCK), F32),
            pltpu.VMEM((CHUNKS, ROW + 1, BLOCK, BLOCK), F32),
            pltpu.VMEM((all_rows, CHAN_Q), F32),
            pltpu.VMEM((all_rows, CHAN_Q), F32),
            pltpu.VMEM((all_rows, CHAN_Q), F32),
            pltpu.VMEM((ROW - 1, STATE, CHAN_Q), F32),
            pltpu.VMEM((STATE, CHAN_Q), F32),
            pltpu.VMEM((CHUNKS, STATE, WIDTH), BF16),
            pltpu.VMEM((CHUNKS, STATE, WIDTH), BF16),
            pltpu.VMEM((ROW * BLOCK, CHAN_Q), BF16),
            pltpu.VMEM((RING, STEPS, CHAN_Q), BF16),
            dma((6,)),
            dma((CHUNKS,)),
            dma((CHUNKS,)),
            dma((ROW, CHUNKS)),
            dma((ROW, CHUNKS)),
            dma((ROW, 2)),
            dma((ROW, 2)),
            dma((ROW,)),
            dma((ROW,)),
            dma((2, ROW)),
            dma((2,)),
            dma((3, ROW)),
            dma((3, RING)),
            dma((CHUNKS,)),
            dma((CHUNKS,)),
            dma((ROW, CHUNKS)),
            dma((ROW, CHUNKS)),
            dma((RING, CHUNKS)),
            dma((ROW, CHUNKS)),
        ],
        compiler_params=pltpu.CompilerParams(
            collective_id=0, has_side_effects=True, vmem_limit_bytes=44 << 20
        ),
        name="scan_exchange",
    )(
        heads_pre,
        bc,
        steps,
        heads_dec[0],
        step_dec[0],
        conv_head_taps,
        conv_head_bias[None],
        conv_map_taps,
        filter_mapping_offset,
        head_rate[None],
        skip_gain[None],
    )
    return out, dout[None]


def solution(mesh):
    placed = (
        P(("prompt", "seq"), "head"),
        P(("prompt", "seq"), None, "head"),
        P(("prompt", "seq"), "head"),
        P("head"),
        P("head"),
        P(None, "head"),
        P("head"),
        P(None, None, "head"),
        P(None, "head"),
        P(("prompt", "seq"), None, "head"),
        P(("prompt", "seq"), None, None, "head"),
        P(("prompt", "seq"), None, "head"),
    )
    return jax.shard_map(
        local,
        mesh=mesh,
        in_specs=placed,
        out_specs=(P(("prompt", "seq"), "head"), P(("prompt", "seq"), None, "head")),
        check_vma=False,
    )
```

```python
import functools

import jax
import jax.numpy as jnp
from jax import lax
from jax.experimental import pallas as pl
from jax.experimental.pallas import tpu as pltpu
from jax.sharding import PartitionSpec as P

HEAD_DIM = 64
STATE = 256
CONV = 4
BLOCK = 128
STEPS = 4
ROW = 4
RING = 16
HEADS_Q = 16
CHAN_Q = HEADS_Q * HEAD_DIM
CHUNKS = 8
WIDTH = CHAN_Q // CHUNKS
HALO = 8
HEADS_C = HEADS_Q // CHUNKS
GROUPS = 2
GROUP_CHUNKS = CHUNKS // GROUPS
MESH = pl.DeviceIdType.MESH
F32 = jnp.float32
BF16 = jnp.bfloat16
HIGH = lax.Precision.HIGHEST


def silu(v):
    return v * (1.0 / (1.0 + jnp.exp(-v)))


def iota(shape, dim):
    return lax.broadcasted_iota(jnp.int32, shape, dim)


def conv_rows(xin, taps, bias):
    total = bias + taps[0] * pltpu.roll(xin, 3, 0)[HALO:]
    total = total + taps[1] * pltpu.roll(xin, 2, 0)[HALO:]
    total = total + taps[2] * pltpu.roll(xin, 1, 0)[HALO:]
    total = total + taps[3] * xin[HALO:]
    return silu(total)


def conv_cyclic(xin, taps, bias):
    total = bias + taps[0] * pltpu.roll(xin, 3, 0)
    total = total + taps[1] * pltpu.roll(xin, 2, 0)
    total = total + taps[2] * pltpu.roll(xin, 1, 0)
    total = total + taps[3] * xin
    return silu(total)


def kernel(
    x_ref,
    bc_ref,
    st_ref,
    dec_ref,
    decs_ref,
    taps_ref,
    bias_ref,
    mtaps_ref,
    mbias_ref,
    rate_ref,
    skip_ref,
    out_ref,
    dout_ref,
    xbuf,
    bcbuf,
    st_s,
    decx,
    decm,
    decs,
    rows8,
    rate_s,
    skip_s,
    turn_s,
    xc,
    bcc,
    bt,
    scores,
    tri,
    keep_s,
    cum_t,
    cumcol,
    wexp,
    ecexp,
    yacc,
    local_s,
    total_s,
    cin,
    cout,
    outbuf,
    doutbuf,
    lsem,
    lout_sem,
    ldo_sem,
    sx,
    rx,
    sbc,
    rbc,
    sst,
    rst,
    shalo,
    rhalo,
    sdec,
    rdec,
    scar,
    rcar,
    sout,
    rout,
    sdo,
    rdo,
    carry_ok,
    dec_ok,
):
    me = lax.axis_index("seq")
    z = me // ROW
    y = me % ROW
    group = y // 2
    base = ROW * z
    last = z == ROW - 1
    lag = jnp.where(last, CHUNKS, 2 * z)

    def row_peer(k):
        return lax.rem(y + k, ROW)

    def from_peer(k):
        return lax.rem(y + ROW - k, ROW)

    def rows_of(b):
        return pl.ds(pl.multiple_of(b * BLOCK, BLOCK), BLOCK)

    def in_rows(b):
        return pl.ds(pl.multiple_of(HALO + b * BLOCK, HALO), BLOCK)

    def cols_of(c):
        return pl.ds(pl.multiple_of(c * WIDTH, WIDTH), WIDTH)

    def quarter_cols(q, c):
        return pl.ds(pl.multiple_of(q * CHAN_Q + c * WIDTH, WIDTH), WIDTH)

    def quarter(q):
        return pl.ds(pl.multiple_of(q * CHAN_Q, CHAN_Q), CHAN_Q)

    def half(m):
        return pl.ds(m * STATE, STATE)

    prompt_rows = pl.ds(0, BLOCK)
    end_rows = pl.ds(ROW * BLOCK, HALO)
    dec_rows = pl.ds(BLOCK, 8)
    before = pl.ds(0, HALO)

    def remote(src, dst, send, recv, seq):
        return pltpu.make_async_remote_copy(
            src_ref=src,
            dst_ref=dst,
            send_sem=send,
            recv_sem=recv,
            device_id={"seq": seq},
            device_id_type=MESH,
        )

    def x_copy(k, c):
        q = row_peer(k)
        return remote(
            x_ref.at[:, quarter_cols(q, c)],
            xbuf.at[in_rows(y), cols_of(c)],
            sx.at[k, c],
            rx.at[k, c],
            base + q,
        )

    def x_arrival(k, c):
        src = from_peer(k)
        return remote(
            x_ref.at[:, quarter_cols(y, c)],
            xbuf.at[in_rows(src), cols_of(c)],
            sx.at[k, c],
            rx.at[k, c],
            base + src,
        )

    def bc_copy(k, m):
        q = row_peer(k)
        return remote(
            bc_ref.at[q // 2, prompt_rows, half(m)],
            bcbuf.at[in_rows(y), half(m)],
            sbc.at[k, m],
            rbc.at[k, m],
            base + q,
        )

    def bc_arrival(k, m):
        src = from_peer(k)
        return remote(
            bc_ref.at[group, prompt_rows, half(m)],
            bcbuf.at[in_rows(src), half(m)],
            sbc.at[k, m],
            rbc.at[k, m],
            base + src,
        )

    def st_copy(k):
        q = row_peer(k)
        return remote(st_ref.at[q], st_s.at[y], sst.at[k], rst.at[k], base + q)

    def st_arrival(k):
        src = from_peer(k)
        return remote(st_ref.at[y], st_s.at[src], sst.at[k], rst.at[k], base + src)

    def halo_x(c, seq):
        cols = cols_of(c)
        return remote(
            xbuf.at[end_rows, cols], xbuf.at[before, cols], shalo.at[c], rhalo.at[c], seq
        )

    def halo_bc(m, seq):
        return remote(
            bcbuf.at[end_rows, half(m)],
            bcbuf.at[before, half(m)],
            shalo.at[CHUNKS + m],
            rhalo.at[CHUNKS + m],
            seq,
        )

    def dec_copies(q, sample):
        parts = (
            (dec_ref.at[:, quarter(q)], decx.at[sample]),
            (bc_ref.at[q // 2, dec_rows], decm.at[sample]),
            (decs_ref, decs.at[sample]),
        )
        return [
            remote(src, dst, sdec.at[i, q], rdec.at[i, sample], 12 + q)
            for i, (src, dst) in enumerate(parts)
        ]

    own_dec = [
        pltpu.make_async_copy(dec_ref.at[:, quarter(y)], decx.at[me], lsem.at[3]),
        pltpu.make_async_copy(bc_ref.at[group, dec_rows], decm.at[me], lsem.at[4]),
        pltpu.make_async_copy(decs_ref, decs.at[me], lsem.at[5]),
    ]

    def carry_copy(c, seq):
        return remote(cout.at[c], cin.at[c], scar.at[c], rcar.at[c], seq)

    def out_copy(k, c):
        b = row_peer(k)
        return remote(
            outbuf.at[rows_of(b), cols_of(c)],
            out_ref.at[:, quarter_cols(y, c)],
            sout.at[k, c],
            rout.at[k, c],
            base + b,
        )

    def out_arrival(k, c):
        src = from_peer(k)
        return remote(
            outbuf.at[rows_of(y), cols_of(c)],
            out_ref.at[:, quarter_cols(src, c)],
            sout.at[k, c],
            rout.at[k, c],
            base + src,
        )

    def out_own(c):
        return pltpu.make_async_copy(
            outbuf.at[rows_of(y), cols_of(c)], out_ref.at[:, quarter_cols(y, c)], lout_sem.at[c]
        )

    def group_cols(q, g):
        size = CHAN_Q // GROUPS
        return pl.ds(pl.multiple_of(q * CHAN_Q + g * size, size), size)

    def dout_copy(sample, g):
        return remote(
            doutbuf.at[sample, :, group_cols(0, g)],
            dout_ref.at[:, group_cols(y, g)],
            sdo.at[sample, g],
            rdo.at[y, g],
            sample,
        )

    def dout_arrival(q, g):
        return remote(
            doutbuf.at[me, :, group_cols(0, g)],
            dout_ref.at[:, group_cols(q, g)],
            sdo.at[me, g],
            rdo.at[q, g],
            12 + q,
        )

    def dout_own(g):
        return pltpu.make_async_copy(
            doutbuf.at[me, :, group_cols(0, g)], dout_ref.at[:, group_cols(y, g)], ldo_sem.at[g]
        )

    own_x = pltpu.make_async_copy(x_ref.at[:, quarter(y)], xbuf.at[in_rows(y)], lsem.at[0])
    own_bc = pltpu.make_async_copy(bc_ref.at[group, prompt_rows], bcbuf.at[in_rows(y)], lsem.at[1])
    own_st = pltpu.make_async_copy(st_ref.at[y], st_s.at[y], lsem.at[2])

    def signal(sem, seq):
        pl.semaphore_signal(sem, inc=1, device_id={"seq": seq}, device_id_type=MESH)

    barrier = pltpu.get_barrier_semaphore()
    for k in range(1, ROW):
        signal(barrier, base + row_peer(k))
    own_st.start()
    own_bc.start()
    own_x.start()

    @pl.when(last)
    def _():
        for copy in own_dec:
            copy.start()

    r_i, c_i = iota((BLOCK, BLOCK), 0), iota((BLOCK, BLOCK), 1)
    same = (r_i // 8) == (c_i // 8)
    left = c_i < HEAD_DIM
    tri[0] = jnp.where(r_i <= c_i, 1.0, 0.0).astype(F32)
    tri[1] = jnp.where((r_i <= c_i) & same, 1.0, 0.0).astype(F32)
    keep_s[0] = jnp.where(r_i >= c_i, 1.0, 0.0).astype(F32)
    keep_s[1] = jnp.where((r_i >= c_i) & same, 1.0, 0.0).astype(F32)

    def spread(ref):
        wide = jnp.broadcast_to(ref[...], (BLOCK, ref.shape[1]))
        return jnp.transpose(jnp.concatenate([wide, wide], axis=1))

    rate_s[...] = spread(rate_ref)
    skip_s[...] = spread(skip_ref)

    @pl.when(z == 0)
    def _():
        xbuf[before] = jnp.zeros((HALO, CHAN_Q), BF16)
        bcbuf[before] = jnp.zeros((HALO, 2 * STATE), BF16)
        cin[...] = jnp.zeros_like(cin)

    pl.semaphore_wait(barrier, jnp.where(z == 0, ROW - 1, ROW))

    @pl.when(z < ROW - 1)
    def _():
        signal(barrier, me + ROW)

    for k in range(1, ROW):
        st_copy(k).start()
    for k in range(1, ROW):
        bc_copy(k, 0).start()
    for c in range(CHUNKS):
        for k in range(1, ROW):
            x_copy(k, c).start()
        if c == 1:
            for k in range(1, ROW):
                bc_copy(k, 1).start()

    @pl.when(z > 0)
    def _():
        signal(carry_ok, me - ROW)

    @pl.when(last)
    def _():
        @pl.loop(0, RING)
        def _(s):
            @pl.when(s != me)
            def _():
                signal(dec_ok, s)

    def send_decode():
        pl.semaphore_wait(dec_ok, jnp.where(last, ROW - 1, ROW))

        for q in range(ROW):

            @pl.when(me != 12 + q)
            def _(q=q):
                for copy in dec_copies(q, me):
                    copy.start()

    def steps_of(b, m):
        step = st_s[b]
        drop = -(step * rate_s[pl.ds(pl.multiple_of(y * HEADS_Q, HEADS_Q), HEADS_Q)])
        cum = jnp.dot(drop, tri[m], precision=HIGH, preferred_element_type=F32)
        cum_t[b] = cum
        weight = jnp.exp(cum[:, BLOCK - 1 : BLOCK] - cum) * step
        stack = jnp.concatenate(
            [cum, weight, jnp.exp(cum), jnp.zeros((BLOCK - 3 * HEADS_Q, BLOCK), F32)], axis=0
        )
        turned = jnp.transpose(stack)
        for c in range(CHUNKS):
            shift = (BLOCK - c * HEADS_C) % BLOCK
            cumcol[c, b] = pltpu.roll(turned, shift, 1) if shift else turned
        for j in range(HEADS_Q // 2):
            cols = pl.ds(j * BLOCK, BLOCK)

            def pair(first):
                one = jnp.broadcast_to(turned[:, first : first + 1], (BLOCK, BLOCK))
                two = jnp.broadcast_to(turned[:, first + 1 : first + 2], (BLOCK, BLOCK))
                return jnp.where(left, one, two)

            wexp[rows_of(b), cols] = pair(HEADS_Q + 2 * j)
            ecexp[rows_of(b), cols] = pair(2 * HEADS_Q + 2 * j)

    map_cols = pl.ds(pl.multiple_of(group * STATE, STATE), STATE)

    def map_taps(m):
        return [mtaps_ref[j, pl.ds(m, 1), map_cols] for j in range(CONV)], mbias_ref[
            pl.ds(m, 1), map_cols
        ]

    def keep_in(b, conv):
        bcc[rows_of(b), half(0)] = conv.astype(BF16)
        bt[b] = jnp.transpose(conv).astype(BF16)

    def keep_out(b, conv):
        low = conv.astype(BF16)
        bcc[rows_of(b), half(1)] = low
        score = lax.dot_general(
            low, bcc[rows_of(b), half(0)], (((1,), (1,)), ((), ())), preferred_element_type=F32
        )
        scores[b] = score * keep_s[b // ROW]

    def chan_taps(c):
        cols = quarter_cols(y, c)
        return [taps_ref[pl.ds(j, 1), cols] for j in range(CONV)], bias_ref[:, cols]

    def gain(b, cols):
        return ecexp[pl.ds(b * BLOCK + BLOCK - 1, 1), cols]

    def maps(m, keep):
        taps, bias = map_taps(m)

        @pl.loop(0, ROW)
        def _(b):
            rows = pl.ds(pl.multiple_of(b * BLOCK, BLOCK), BLOCK + HALO)
            keep(b, conv_rows(bcbuf[rows, half(m)].astype(F32), taps, bias))

    own_st.wait()
    for k in range(1, ROW):
        st_arrival(k).wait_recv()

    @pl.loop(0, ROW)
    def _(b):
        steps_of(b, 0)

    own_bc.wait()
    for k in range(1, ROW):
        bc_arrival(k, 0).wait_recv()

    @pl.when(z < ROW - 1)
    def _():
        pl.semaphore_wait(carry_ok, 1)
        halo_bc(0, me + ROW).start()

    @pl.when(z > 0)
    def _():
        halo_bc(0, me).wait_recv()

    maps(0, keep_in)
    own_x.wait()

    def block_states(c):
        for k in range(1, ROW):
            x_arrival(k, c).wait_recv()

        @pl.when(z < ROW - 1)
        def _():
            halo_x(c, me + ROW).start()

        @pl.when(z > 0)
        def _():
            halo_x(c, me).wait_recv()

        cols = cols_of(c)
        taps, bias = chan_taps(c)
        state = None
        for b in range(ROW):
            xin = xbuf[pl.ds(b * BLOCK, BLOCK + HALO), cols].astype(F32)
            low = conv_rows(xin, taps, bias).astype(BF16)
            xc[pl.ds(b * BLOCK, BLOCK), cols] = low
            weighted = (low.astype(F32) * wexp[pl.ds(b * BLOCK, BLOCK), cols]).astype(BF16)
            block_state = jnp.dot(bt[b], weighted, preferred_element_type=F32)
            state = block_state if b == 0 else gain(b, cols) * state + block_state
            if b < ROW - 1:
                local_s[b, :, cols] = state
            else:
                total_s[:, cols] = state

        @pl.when(z == 0)
        def _():
            cout[c] = total_s[:, cols].astype(BF16)
            carry_copy(c, me + ROW).start()

    def with_tail(new, tail):
        width = new.shape[-1]
        rows8[:, 0:STEPS, 0:width] = new
        rows8[:, STEPS:8, 0:width] = jnp.broadcast_to(tail[None], (RING, 8 - STEPS, width))
        return rows8[:, :, 0:width].reshape(BLOCK, width)

    def decode_inputs():
        for copy in own_dec:
            copy.wait()

        @pl.loop(0, RING)
        def _(s):
            @pl.when(s != me)
            def _():
                for copy in dec_copies(y, s):
                    copy.wait_recv()

        rows8[:, :, 0:BLOCK] = jnp.zeros((RING, 8, BLOCK), F32)
        rows8[:, 0:STEPS, 0:64] = decs[...]
        turn_s[...] = jnp.transpose(rows8[:, :, 0:BLOCK].reshape(BLOCK, BLOCK))
        st_s[ROW] = turn_s[pl.ds(pl.multiple_of(y * HEADS_Q, HEADS_Q), HEADS_Q)]
        steps_of(ROW, 1)
        end = pl.ds(ROW * BLOCK, HALO)
        for m, keep in ((0, keep_in), (1, keep_out)):
            taps, bias = map_taps(m)
            new = decm[:, :, m * STATE : (m + 1) * STATE].astype(F32)[:, 0:STEPS]
            tail = bcbuf[end, half(m)].astype(F32)[STEPS:8]
            keep(ROW, conv_cyclic(with_tail(new, tail), taps, bias))

        @pl.loop(0, CHUNKS)
        def _(c):
            cols = cols_of(c)
            taps, bias = chan_taps(c)
            tail = xbuf[end, cols].astype(F32)[STEPS:8]
            conv = conv_cyclic(with_tail(decx[:, :, cols].astype(F32), tail), taps, bias)
            xc[pl.ds(ROW * BLOCK, BLOCK), cols] = conv.astype(BF16)
            inner_part(ROW, c)

    def inner_part(b, c):
        rows = pl.ds(b * BLOCK, BLOCK)
        score = scores[b]
        columns = cumcol[c, b]
        for pair in range(HEADS_C // 2):
            mixes = []
            for j in (2 * pair, 2 * pair + 1):
                head = c * HEADS_C + j
                row = cum_t[b, pl.ds(head, 1)]
                step = st_s[b, pl.ds(head, 1)]
                gap = columns[:, j : j + 1] - row
                mixes.append((score * jnp.exp(gap) * step).astype(BF16))
            mixing = jnp.concatenate(mixes, axis=1)
            cols = pl.ds(pl.multiple_of(c * WIDTH + pair * BLOCK, BLOCK), BLOCK)
            xp = xc[rows, cols].astype(F32)
            blockdiag = jnp.concatenate(
                [jnp.where(left, xp, 0.0).astype(BF16), jnp.where(left, 0.0, xp).astype(BF16)],
                axis=0,
            )
            inner = jnp.dot(mixing, blockdiag, preferred_element_type=F32)
            head = y * HEADS_Q + c * HEADS_C + 2 * pair
            skip = jnp.where(left[0:1], skip_s[pl.ds(head, 1)], skip_s[pl.ds(head + 1, 1)])
            yacc[rows, cols] = inner + skip * xp

    def with_carry(c):
        cols = cols_of(c)

        @pl.when(z > 0)
        def _():
            carry_copy(c, me).wait_recv()

        leads = [gain(0, cols)]
        for b in range(1, ROW):
            leads.append(leads[-1] * gain(b, cols))

        @pl.when((z > 0) & (z < ROW - 1))
        def _():
            cout[c] = (total_s[:, cols] + leads[ROW - 1] * cin[c].astype(F32)).astype(BF16)
            carry_copy(c, me + ROW).start()

        carry = cin[c].astype(F32)
        for b in range(ROW):
            rows = pl.ds(b * BLOCK, BLOCK)
            if b == 0:
                entry = cin[c]
            else:
                entry = (local_s[b - 1, :, cols] + leads[b - 1] * carry).astype(BF16)
            cross = jnp.dot(bcc[rows, half(1)], entry, preferred_element_type=F32)
            outbuf[rows, cols] = (yacc[rows, cols] + ecexp[rows, cols] * cross).astype(BF16)
        out_own(c).start()
        for k in range(1, ROW):
            out_copy(k, c).start()

        @pl.when(last)
        def _():
            final = total_s[:, cols] + leads[ROW - 1] * carry
            high = final.astype(BF16)
            rest = (final - high.astype(F32)).astype(BF16)
            rows = pl.ds(ROW * BLOCK, BLOCK)
            out_map = bcc[rows, half(1)]
            cross = jnp.dot(out_map, high, preferred_element_type=F32) + jnp.dot(
                out_map, rest, preferred_element_type=F32
            )
            result = yacc[rows, cols] + ecexp[rows, cols] * cross
            rows8[:, :, 0:WIDTH] = result.reshape(RING, 8, WIDTH)
            doutbuf[:, :, cols] = rows8[:, 0:STEPS, 0:WIDTH].astype(BF16)

            @pl.when(c % GROUP_CHUNKS == GROUP_CHUNKS - 1)
            def _():
                g = c // GROUP_CHUNKS
                dout_own(g).start()

                @pl.loop(0, RING)
                def _(s):
                    @pl.when(s != me)
                    def _():
                        dout_copy(s, g).start()

    @pl.loop(0, CHUNKS + lag)
    def _(i):
        @pl.when(i < CHUNKS)
        def _():
            block_states(i)

        @pl.when(i == 0)
        def _():
            for k in range(1, ROW):
                bc_arrival(k, 1).wait_recv()

            @pl.when(z < ROW - 1)
            def _():
                halo_bc(1, me + ROW).start()

            @pl.when(z > 0)
            def _():
                halo_bc(1, me).wait_recv()

            maps(1, keep_out)

        @pl.when(i == 2)
        def _():
            send_decode()

        @pl.when(i < CHUNKS)
        def _():
            for b in range(ROW):
                inner_part(b, i)

        @pl.when(last & (i == lag))
        def _():
            decode_inputs()

        @pl.when(i >= lag)
        def _():
            with_carry(i - lag)

    @pl.loop(0, CHUNKS)
    def _(c):
        out_own(c).wait()
        for k in range(1, ROW):
            out_arrival(k, c).wait_recv()

    for g in range(GROUPS):
        for q in range(ROW):

            @pl.when(me != 12 + q)
            def _(q=q, g=g):
                dout_arrival(q, g).wait_recv()

        @pl.when(last)
        def _(g=g):
            dout_own(g).wait()

    for k in range(1, ROW):
        st_copy(k).wait_send()
        for m in range(2):
            bc_copy(k, m).wait_send()

    @pl.loop(0, CHUNKS)
    def _(c):
        for k in range(1, ROW):
            x_copy(k, c).wait_send()
            out_copy(k, c).wait_send()

        @pl.when(z < ROW - 1)
        def _():
            carry_copy(c, me + ROW).wait_send()
            halo_x(c, me + ROW).wait_send()

    @pl.when(last)
    def _():
        @pl.loop(0, RING)
        def _(s):
            @pl.when(s != me)
            def _():
                for g in range(GROUPS):
                    dout_copy(s, g).wait_send()

    @pl.when(z < ROW - 1)
    def _():
        for m in range(2):
            halo_bc(m, me + ROW).wait_send()

    for q in range(ROW):

        @pl.when(me != 12 + q)
        def _(q=q):
            for copy in dec_copies(q, me):
                copy.wait_send()


def local(
    heads_pre,
    maps_pre,
    step_prompt,
    head_rate,
    skip_gain,
    conv_head_taps,
    conv_head_bias,
    conv_map_taps,
    filter_mapping_offset,
    heads_dec,
    maps_dec,
    step_dec,
):
    tokens, channels = heads_pre.shape
    groups = maps_pre.shape[2] // STATE
    heads = step_prompt.shape[1]

    bc = jnp.concatenate(
        [maps_pre, maps_dec[0], jnp.zeros((8 - STEPS,) + maps_pre.shape[1:], BF16)], axis=0
    )
    bc = bc.reshape(tokens + 8, 2, groups, STATE).transpose(2, 0, 1, 3)
    bc = bc.reshape(groups, tokens + 8, 2 * STATE)
    steps = step_prompt.T.reshape(ROW, HEADS_Q, tokens)

    any_space = pl.BlockSpec(memory_space=pl.ANY)
    vmem = pl.BlockSpec(memory_space=pltpu.VMEM)
    dma = pltpu.SemaphoreType.DMA
    all_rows = (ROW + 1) * BLOCK
    out, dout = pl.pallas_call(
        kernel,
        out_shape=(
            jax.ShapeDtypeStruct((tokens, channels), BF16),
            jax.ShapeDtypeStruct((STEPS, channels), BF16),
        ),
        in_specs=[any_space] * 5 + [vmem] * 6,
        out_specs=(any_space, any_space),
        scratch_shapes=[
            pltpu.VMEM((HALO + ROW * BLOCK, CHAN_Q), BF16),
            pltpu.VMEM((HALO + ROW * BLOCK, 2 * STATE), BF16),
            pltpu.VMEM((ROW + 1, HEADS_Q, BLOCK), F32),
            pltpu.VMEM((RING, STEPS, CHAN_Q), BF16),
            pltpu.VMEM((RING, 8, 2 * STATE), BF16),
            pltpu.VMEM((RING, STEPS, heads), F32),
            pltpu.VMEM((RING, 8, STATE), F32),
            pltpu.VMEM((BLOCK, BLOCK), F32),
            pltpu.VMEM((BLOCK, BLOCK), F32),
            pltpu.VMEM((BLOCK, BLOCK), F32),
            pltpu.VMEM((all_rows, CHAN_Q), BF16),
            pltpu.VMEM((all_rows, 2 * STATE), BF16),
            pltpu.VMEM((ROW + 1, STATE, BLOCK), BF16),
            pltpu.VMEM((ROW + 1, BLOCK, BLOCK), F32),
            pltpu.VMEM((2, BLOCK, BLOCK), F32),
            pltpu.VMEM((2, BLOCK, BLOCK), F32),
            pltpu.VMEM((ROW + 1, HEADS_Q, BLOCK), F32),
            pltpu.VMEM((CHUNKS, ROW + 1, BLOCK, BLOCK), F32),
            pltpu.VMEM((all_rows, CHAN_Q), F32),
            pltpu.VMEM((all_rows, CHAN_Q), F32),
            pltpu.VMEM((all_rows, CHAN_Q), F32),
            pltpu.VMEM((ROW - 1, STATE, CHAN_Q), F32),
            pltpu.VMEM((STATE, CHAN_Q), F32),
            pltpu.VMEM((CHUNKS, STATE, WIDTH), BF16),
            pltpu.VMEM((CHUNKS, STATE, WIDTH), BF16),
            pltpu.VMEM((ROW * BLOCK, CHAN_Q), BF16),
            pltpu.VMEM((RING, STEPS, CHAN_Q), BF16),
            dma((6,)),
            dma((CHUNKS,)),
            dma((GROUPS,)),
            dma((ROW, CHUNKS)),
            dma((ROW, CHUNKS)),
            dma((ROW, 2)),
            dma((ROW, 2)),
            dma((ROW,)),
            dma((ROW,)),
            dma((CHUNKS + 2,)),
            dma((CHUNKS + 2,)),
            dma((3, ROW)),
            dma((3, RING)),
            dma((CHUNKS,)),
            dma((CHUNKS,)),
            dma((ROW, CHUNKS)),
            dma((ROW, CHUNKS)),
            dma((RING, GROUPS)),
            dma((ROW, GROUPS)),
            pltpu.SemaphoreType.REGULAR,
            pltpu.SemaphoreType.REGULAR,
        ],
        compiler_params=pltpu.CompilerParams(
            collective_id=0, has_side_effects=True, vmem_limit_bytes=44 << 20
        ),
        name="scan_exchange",
    )(
        heads_pre,
        bc,
        steps,
        heads_dec[0],
        step_dec[0],
        conv_head_taps,
        conv_head_bias[None],
        conv_map_taps,
        filter_mapping_offset,
        head_rate[None],
        skip_gain[None],
    )
    return out, dout[None]


def solution(mesh):
    placed = (
        P(("prompt", "seq"), "head"),
        P(("prompt", "seq"), None, "head"),
        P(("prompt", "seq"), "head"),
        P("head"),
        P("head"),
        P(None, "head"),
        P("head"),
        P(None, None, "head"),
        P(None, "head"),
        P(("prompt", "seq"), None, "head"),
        P(("prompt", "seq"), None, None, "head"),
        P(("prompt", "seq"), None, "head"),
    )
    return jax.shard_map(
        local,
        mesh=mesh,
        in_specs=placed,
        out_specs=(P(("prompt", "seq"), "head"), P(("prompt", "seq"), None, "head")),
        check_vma=False,
    )
```

```python
import functools

import jax
import jax.numpy as jnp
from jax import lax
from jax.experimental import pallas as pl
from jax.experimental.pallas import tpu as pltpu
from jax.sharding import PartitionSpec as P

HEAD_DIM = 64
STATE = 256
CONV = 4
BLOCK = 128
STEPS = 4
ROW = 4
RING = 16
HEADS_Q = 16
CHAN_Q = HEADS_Q * HEAD_DIM
CHUNKS = 8
WIDTH = CHAN_Q // CHUNKS
HALO = 8
HEADS_C = HEADS_Q // CHUNKS
AHEAD = 2
GROUPS = 2
GROUP_CHUNKS = CHUNKS // GROUPS
MESH = pl.DeviceIdType.MESH
F32 = jnp.float32
BF16 = jnp.bfloat16
HIGH = lax.Precision.HIGHEST


def silu(v):
    return v * (1.0 / (1.0 + jnp.exp(-v)))


def iota(shape, dim):
    return lax.broadcasted_iota(jnp.int32, shape, dim)


def conv_rows(xin, taps, bias):
    total = bias + taps[0] * pltpu.roll(xin, 3, 0)[HALO:]
    total = total + taps[1] * pltpu.roll(xin, 2, 0)[HALO:]
    total = total + taps[2] * pltpu.roll(xin, 1, 0)[HALO:]
    total = total + taps[3] * xin[HALO:]
    return silu(total)


def conv_cyclic(xin, taps, bias):
    total = bias + taps[0] * pltpu.roll(xin, 3, 0)
    total = total + taps[1] * pltpu.roll(xin, 2, 0)
    total = total + taps[2] * pltpu.roll(xin, 1, 0)
    total = total + taps[3] * xin
    return silu(total)


def kernel(
    x_ref,
    bc_ref,
    st_ref,
    dec_ref,
    decs_ref,
    taps_ref,
    bias_ref,
    mtaps_ref,
    mbias_ref,
    rate_ref,
    skip_ref,
    out_ref,
    dout_ref,
    xbuf,
    bcbuf,
    st_s,
    decx,
    decm,
    decs,
    rows8,
    rate_s,
    skip_s,
    turn_s,
    xc,
    bcc,
    bt,
    scores,
    tri,
    keep_s,
    cum_t,
    cumcol,
    wexp,
    ecexp,
    yacc,
    local_s,
    total_s,
    cin,
    cout,
    outbuf,
    doutbuf,
    lsem,
    lout_sem,
    ldo_sem,
    sx,
    rx,
    sbc,
    rbc,
    sst,
    rst,
    shalo,
    rhalo,
    sdec,
    rdec,
    scar,
    rcar,
    sout,
    rout,
    sdo,
    rdo,
    carry_ok,
    dec_ok,
    turn_ok,
):
    me = lax.axis_index("seq")
    z = me // ROW
    y = me % ROW
    group = y // 2
    base = ROW * z
    last = z == ROW - 1
    prompt = lax.axis_index("prompt")
    odd = prompt // 2 == 1
    early = odd & ~last
    lag = jnp.where(early, 2 * z, 0)
    first = (z == 0) & ~odd
    wait = jnp.where(odd | first, 0, CHUNKS)

    def row_peer(k):
        return lax.rem(y + k, ROW)

    def from_peer(k):
        return lax.rem(y + ROW - k, ROW)

    def rows_of(b):
        return pl.ds(pl.multiple_of(b * BLOCK, BLOCK), BLOCK)

    def in_rows(b):
        return pl.ds(pl.multiple_of(HALO + b * BLOCK, HALO), BLOCK)

    def cols_of(c):
        return pl.ds(pl.multiple_of(c * WIDTH, WIDTH), WIDTH)

    def quarter_cols(q, c):
        return pl.ds(pl.multiple_of(q * CHAN_Q + c * WIDTH, WIDTH), WIDTH)

    def quarter(q):
        return pl.ds(pl.multiple_of(q * CHAN_Q, CHAN_Q), CHAN_Q)

    def half(m):
        return pl.ds(m * STATE, STATE)

    prompt_rows = pl.ds(0, BLOCK)
    end_rows = pl.ds(ROW * BLOCK, HALO)
    dec_rows = pl.ds(BLOCK, 8)
    before = pl.ds(0, HALO)

    def remote(src, dst, send, recv, seq):
        return pltpu.make_async_remote_copy(
            src_ref=src,
            dst_ref=dst,
            send_sem=send,
            recv_sem=recv,
            device_id={"seq": seq},
            device_id_type=MESH,
        )

    def x_copy(k, c):
        q = row_peer(k)
        return remote(
            x_ref.at[:, quarter_cols(q, c)],
            xbuf.at[in_rows(y), cols_of(c)],
            sx.at[k, c],
            rx.at[k, c],
            base + q,
        )

    def x_arrival(k, c):
        src = from_peer(k)
        return remote(
            x_ref.at[:, quarter_cols(y, c)],
            xbuf.at[in_rows(src), cols_of(c)],
            sx.at[k, c],
            rx.at[k, c],
            base + src,
        )

    def bc_copy(k, m):
        q = row_peer(k)
        return remote(
            bc_ref.at[q // 2, prompt_rows, half(m)],
            bcbuf.at[in_rows(y), half(m)],
            sbc.at[k, m],
            rbc.at[k, m],
            base + q,
        )

    def bc_arrival(k, m):
        src = from_peer(k)
        return remote(
            bc_ref.at[group, prompt_rows, half(m)],
            bcbuf.at[in_rows(src), half(m)],
            sbc.at[k, m],
            rbc.at[k, m],
            base + src,
        )

    def st_copy(k):
        q = row_peer(k)
        return remote(st_ref.at[q], st_s.at[y], sst.at[k], rst.at[k], base + q)

    def st_arrival(k):
        src = from_peer(k)
        return remote(st_ref.at[y], st_s.at[src], sst.at[k], rst.at[k], base + src)

    def halo_x(c, seq):
        cols = cols_of(c)
        return remote(
            xbuf.at[end_rows, cols], xbuf.at[before, cols], shalo.at[c], rhalo.at[c], seq
        )

    def halo_bc(m, seq):
        return remote(
            bcbuf.at[end_rows, half(m)],
            bcbuf.at[before, half(m)],
            shalo.at[CHUNKS + m],
            rhalo.at[CHUNKS + m],
            seq,
        )

    def dec_copies(q, sample):
        parts = (
            (dec_ref.at[:, quarter(q)], decx.at[sample]),
            (bc_ref.at[q // 2, dec_rows], decm.at[sample]),
            (decs_ref, decs.at[sample]),
        )
        return [
            remote(src, dst, sdec.at[i, q], rdec.at[i, sample], 12 + q)
            for i, (src, dst) in enumerate(parts)
        ]

    own_dec = [
        pltpu.make_async_copy(dec_ref.at[:, quarter(y)], decx.at[me], lsem.at[3]),
        pltpu.make_async_copy(bc_ref.at[group, dec_rows], decm.at[me], lsem.at[4]),
        pltpu.make_async_copy(decs_ref, decs.at[me], lsem.at[5]),
    ]

    def carry_copy(c, seq):
        return remote(cout.at[c], cin.at[c], scar.at[c], rcar.at[c], seq)

    def out_copy(k, c):
        b = row_peer(k)
        return remote(
            outbuf.at[rows_of(b), cols_of(c)],
            out_ref.at[:, quarter_cols(y, c)],
            sout.at[k, c],
            rout.at[k, c],
            base + b,
        )

    def out_arrival(k, c):
        src = from_peer(k)
        return remote(
            outbuf.at[rows_of(y), cols_of(c)],
            out_ref.at[:, quarter_cols(src, c)],
            sout.at[k, c],
            rout.at[k, c],
            base + src,
        )

    def out_own(c):
        return pltpu.make_async_copy(
            outbuf.at[rows_of(y), cols_of(c)], out_ref.at[:, quarter_cols(y, c)], lout_sem.at[c]
        )

    def group_cols(q, g):
        size = CHAN_Q // GROUPS
        return pl.ds(pl.multiple_of(q * CHAN_Q + g * size, size), size)

    def dout_copy(sample, g):
        return remote(
            doutbuf.at[sample, :, group_cols(0, g)],
            dout_ref.at[:, group_cols(y, g)],
            sdo.at[sample, g],
            rdo.at[y, g],
            sample,
        )

    def dout_arrival(q, g):
        return remote(
            doutbuf.at[me, :, group_cols(0, g)],
            dout_ref.at[:, group_cols(q, g)],
            sdo.at[me, g],
            rdo.at[q, g],
            12 + q,
        )

    def dout_own(g):
        return pltpu.make_async_copy(
            doutbuf.at[me, :, group_cols(0, g)], dout_ref.at[:, group_cols(y, g)], ldo_sem.at[g]
        )

    own_x = pltpu.make_async_copy(x_ref.at[:, quarter(y)], xbuf.at[in_rows(y)], lsem.at[0])
    own_bc = pltpu.make_async_copy(bc_ref.at[group, prompt_rows], bcbuf.at[in_rows(y)], lsem.at[1])
    own_st = pltpu.make_async_copy(st_ref.at[y], st_s.at[y], lsem.at[2])

    def signal(sem, seq):
        pl.semaphore_signal(sem, inc=1, device_id={"seq": seq}, device_id_type=MESH)

    barrier = pltpu.get_barrier_semaphore()
    for k in range(1, ROW):
        signal(barrier, base + row_peer(k))

    def signal_chip(sem, first):
        for core in range(2):
            pl.semaphore_signal(
                sem, inc=1, device_id={"prompt": first + core}, device_id_type=MESH
            )

    @pl.when((z == 0) & ~odd)
    def _():
        signal_chip(barrier, 2)

    own_st.start()
    own_bc.start()
    own_x.start()

    @pl.when(last)
    def _():
        for copy in own_dec:
            copy.start()

    r_i, c_i = iota((BLOCK, BLOCK), 0), iota((BLOCK, BLOCK), 1)
    same = (r_i // 8) == (c_i // 8)
    left = c_i < HEAD_DIM
    tri[0] = jnp.where(r_i <= c_i, 1.0, 0.0).astype(F32)
    tri[1] = jnp.where((r_i <= c_i) & same, 1.0, 0.0).astype(F32)
    keep_s[0] = jnp.where(r_i >= c_i, 1.0, 0.0).astype(F32)
    keep_s[1] = jnp.where((r_i >= c_i) & same, 1.0, 0.0).astype(F32)

    def spread(ref):
        wide = jnp.broadcast_to(ref[...], (BLOCK, ref.shape[1]))
        return jnp.transpose(jnp.concatenate([wide, wide], axis=1))

    rate_s[...] = spread(rate_ref)
    skip_s[...] = spread(skip_ref)

    @pl.when(z == 0)
    def _():
        xbuf[before] = jnp.zeros((HALO, CHAN_Q), BF16)
        bcbuf[before] = jnp.zeros((HALO, 2 * STATE), BF16)
        cin[...] = jnp.zeros_like(cin)

    pl.semaphore_wait(barrier, jnp.where(z > 0, ROW, jnp.where(odd, ROW + 1, ROW - 1)))

    @pl.when(z < ROW - 1)
    def _():
        signal(barrier, me + ROW)

    for k in range(1, ROW):
        st_copy(k).start()
    for k in range(1, ROW):
        bc_copy(k, 0).start()
    for k in range(1, ROW):
        x_copy(k, 0).start()

    @pl.when(z > 0)
    def _():
        signal(carry_ok, me - ROW)

    @pl.when(last)
    def _():
        @pl.loop(0, RING)
        def _(s):
            @pl.when(s != me)
            def _():
                signal(dec_ok, s)

    def send_decode():
        pl.semaphore_wait(dec_ok, jnp.where(last, ROW - 1, ROW))

        for q in range(ROW):

            @pl.when(me != 12 + q)
            def _(q=q):
                for copy in dec_copies(q, me):
                    copy.start()

    def steps_of(b, m):
        step = st_s[b]
        drop = -(step * rate_s[pl.ds(pl.multiple_of(y * HEADS_Q, HEADS_Q), HEADS_Q)])
        cum = jnp.dot(drop, tri[m], precision=HIGH, preferred_element_type=F32)
        cum_t[b] = cum
        weight = jnp.exp(cum[:, BLOCK - 1 : BLOCK] - cum) * step
        stack = jnp.concatenate(
            [cum, weight, jnp.exp(cum), jnp.zeros((BLOCK - 3 * HEADS_Q, BLOCK), F32)], axis=0
        )
        turned = jnp.transpose(stack)
        for c in range(CHUNKS):
            shift = (BLOCK - c * HEADS_C) % BLOCK
            cumcol[c, b] = pltpu.roll(turned, shift, 1) if shift else turned
        for j in range(HEADS_Q // 2):
            cols = pl.ds(j * BLOCK, BLOCK)

            def pair(first):
                one = jnp.broadcast_to(turned[:, first : first + 1], (BLOCK, BLOCK))
                two = jnp.broadcast_to(turned[:, first + 1 : first + 2], (BLOCK, BLOCK))
                return jnp.where(left, one, two)

            wexp[rows_of(b), cols] = pair(HEADS_Q + 2 * j)
            ecexp[rows_of(b), cols] = pair(2 * HEADS_Q + 2 * j)

    map_cols = pl.ds(pl.multiple_of(group * STATE, STATE), STATE)

    def map_taps(m):
        return [mtaps_ref[j, pl.ds(m, 1), map_cols] for j in range(CONV)], mbias_ref[
            pl.ds(m, 1), map_cols
        ]

    def keep_in(b, conv):
        bcc[rows_of(b), half(0)] = conv.astype(BF16)
        bt[b] = jnp.transpose(conv).astype(BF16)

    def keep_out(b, conv):
        low = conv.astype(BF16)
        bcc[rows_of(b), half(1)] = low
        score = lax.dot_general(
            low, bcc[rows_of(b), half(0)], (((1,), (1,)), ((), ())), preferred_element_type=F32
        )
        scores[b] = score * keep_s[b // ROW]

    def chan_taps(c):
        cols = quarter_cols(y, c)
        return [taps_ref[pl.ds(j, 1), cols] for j in range(CONV)], bias_ref[:, cols]

    def gain(b, cols):
        return ecexp[pl.ds(b * BLOCK + BLOCK - 1, 1), cols]

    def maps(m, keep):
        taps, bias = map_taps(m)

        @pl.loop(0, ROW)
        def _(b):
            rows = pl.ds(pl.multiple_of(b * BLOCK, BLOCK), BLOCK + HALO)
            keep(b, conv_rows(bcbuf[rows, half(m)].astype(F32), taps, bias))

    own_st.wait()
    for k in range(1, ROW):
        st_arrival(k).wait_recv()

    @pl.loop(0, ROW)
    def _(b):
        steps_of(b, 0)

    own_bc.wait()
    for k in range(1, ROW):
        bc_arrival(k, 0).wait_recv()

    for c in range(1, AHEAD):
        for k in range(1, ROW):
            x_copy(k, c).start()

    @pl.when(z < ROW - 1)
    def _():
        pl.semaphore_wait(carry_ok, 1)
        halo_bc(0, me + ROW).start()

    @pl.when(z > 0)
    def _():
        halo_bc(0, me).wait_recv()

    maps(0, keep_in)
    own_x.wait()

    def send_carry(c, state):
        cout[c] = state.astype(BF16)
        carry_copy(c, me + ROW).start()

    def block_states(c):
        for k in range(1, ROW):
            x_arrival(k, c).wait_recv()

        @pl.when(c < CHUNKS - AHEAD)
        def _():
            for k in range(1, ROW):
                x_copy(k, c + AHEAD).start()

        @pl.when(z < ROW - 1)
        def _():
            halo_x(c, me + ROW).start()

        @pl.when(z > 0)
        def _():
            halo_x(c, me).wait_recv()

        cols = cols_of(c)
        taps, bias = chan_taps(c)
        state = None
        for b in range(ROW):
            xin = xbuf[pl.ds(b * BLOCK, BLOCK + HALO), cols].astype(F32)
            low = conv_rows(xin, taps, bias).astype(BF16)
            xc[pl.ds(b * BLOCK, BLOCK), cols] = low
            weighted = (low.astype(F32) * wexp[pl.ds(b * BLOCK, BLOCK), cols]).astype(BF16)
            block_state = jnp.dot(bt[b], weighted, preferred_element_type=F32)
            state = block_state if b == 0 else gain(b, cols) * state + block_state
            if b < ROW - 1:
                local_s[b, :, cols] = state
            else:
                total_s[:, cols] = state

    def with_tail(new, tail):
        width = new.shape[-1]
        rows8[:, 0:STEPS, 0:width] = new
        rows8[:, STEPS:8, 0:width] = jnp.broadcast_to(tail[None], (RING, 8 - STEPS, width))
        return rows8[:, :, 0:width].reshape(BLOCK, width)

    def decode_inputs():
        for copy in own_dec:
            copy.wait()

        @pl.loop(0, RING)
        def _(s):
            @pl.when(s != me)
            def _():
                for copy in dec_copies(y, s):
                    copy.wait_recv()

        rows8[:, :, 0:BLOCK] = jnp.zeros((RING, 8, BLOCK), F32)
        rows8[:, 0:STEPS, 0:64] = decs[...]
        turn_s[...] = jnp.transpose(rows8[:, :, 0:BLOCK].reshape(BLOCK, BLOCK))
        st_s[ROW] = turn_s[pl.ds(pl.multiple_of(y * HEADS_Q, HEADS_Q), HEADS_Q)]
        steps_of(ROW, 1)
        end = pl.ds(ROW * BLOCK, HALO)
        for m, keep in ((0, keep_in), (1, keep_out)):
            taps, bias = map_taps(m)
            new = decm[:, :, m * STATE : (m + 1) * STATE].astype(F32)[:, 0:STEPS]
            tail = bcbuf[end, half(m)].astype(F32)[STEPS:8]
            keep(ROW, conv_cyclic(with_tail(new, tail), taps, bias))

        @pl.loop(0, CHUNKS)
        def _(c):
            cols = cols_of(c)
            taps, bias = chan_taps(c)
            tail = xbuf[end, cols].astype(F32)[STEPS:8]
            conv = conv_cyclic(with_tail(decx[:, :, cols].astype(F32), tail), taps, bias)
            xc[pl.ds(ROW * BLOCK, BLOCK), cols] = conv.astype(BF16)
            inner_part(ROW, c)

    def inner_part(b, c):
        rows = pl.ds(b * BLOCK, BLOCK)
        score = scores[b]
        columns = cumcol[c, b]
        for pair in range(HEADS_C // 2):
            mixes = []
            for j in (2 * pair, 2 * pair + 1):
                head = c * HEADS_C + j
                row = cum_t[b, pl.ds(head, 1)]
                step = st_s[b, pl.ds(head, 1)]
                gap = columns[:, j : j + 1] - row
                mixes.append((score * jnp.exp(gap) * step).astype(BF16))
            mixing = jnp.concatenate(mixes, axis=1)
            cols = pl.ds(pl.multiple_of(c * WIDTH + pair * BLOCK, BLOCK), BLOCK)
            xp = xc[rows, cols].astype(F32)
            blockdiag = jnp.concatenate(
                [jnp.where(left, xp, 0.0).astype(BF16), jnp.where(left, 0.0, xp).astype(BF16)],
                axis=0,
            )
            inner = jnp.dot(mixing, blockdiag, preferred_element_type=F32)
            head = y * HEADS_Q + c * HEADS_C + 2 * pair
            skip = jnp.where(left[0:1], skip_s[pl.ds(head, 1)], skip_s[pl.ds(head + 1, 1)])
            yacc[rows, cols] = inner + skip * xp

    def leads_of(cols):
        leads = [gain(0, cols)]
        for b in range(1, ROW):
            leads.append(leads[-1] * gain(b, cols))
        return leads

    def forward(c):
        @pl.when(z > 0)
        def _():
            carry_copy(c, me).wait_recv()

        @pl.when(z < ROW - 1)
        def _():
            cols = cols_of(c)
            lead = leads_of(cols)[ROW - 1]
            send_carry(c, total_s[:, cols] + lead * cin[c].astype(F32))

    def outputs(c):
        cols = cols_of(c)
        leads = leads_of(cols)
        carry = cin[c].astype(F32)
        @pl.when(last)
        def _():
            final = total_s[:, cols] + leads[ROW - 1] * carry
            high = final.astype(BF16)
            rest = (final - high.astype(F32)).astype(BF16)
            rows = pl.ds(ROW * BLOCK, BLOCK)
            out_map = bcc[rows, half(1)]
            cross = jnp.dot(out_map, high, preferred_element_type=F32) + jnp.dot(
                out_map, rest, preferred_element_type=F32
            )
            result = yacc[rows, cols] + ecexp[rows, cols] * cross
            rows8[:, :, 0:WIDTH] = result.reshape(RING, 8, WIDTH)
            doutbuf[:, :, cols] = rows8[:, 0:STEPS, 0:WIDTH].astype(BF16)

            @pl.when(c % GROUP_CHUNKS == GROUP_CHUNKS - 1)
            def _():
                g = c // GROUP_CHUNKS
                dout_own(g).start()

                @pl.loop(0, RING)
                def _(s):
                    @pl.when(s != me)
                    def _():
                        dout_copy(s, g).start()

        for b in range(ROW):
            rows = pl.ds(b * BLOCK, BLOCK)
            if b == 0:
                entry = cin[c]
            else:
                entry = (local_s[b - 1, :, cols] + leads[b - 1] * carry).astype(BF16)
            cross = jnp.dot(bcc[rows, half(1)], entry, preferred_element_type=F32)
            outbuf[rows, cols] = (yacc[rows, cols] + ecexp[rows, cols] * cross).astype(BF16)
        out_own(c).start()
        for k in range(1, ROW):
            out_copy(k, c).start()

    send_decode()

    @pl.loop(0, CHUNKS + lag)
    def _(i):
        @pl.when(i < CHUNKS)
        def _():
            block_states(i)

        @pl.when(i == 4)
        def _():
            for k in range(1, ROW):
                bc_copy(k, 1).start()

        @pl.when(early & (i >= lag))
        def _():
            forward(i - lag)

    @pl.when((z == 0) & odd)
    def _():
        for c in range(CHUNKS):
            carry_copy(c, me + ROW).wait_send()
        signal_chip(turn_ok, 0)

    for k in range(1, ROW):
        bc_arrival(k, 1).wait_recv()

    @pl.when(z < ROW - 1)
    def _():
        halo_bc(1, me + ROW).start()

    @pl.when(z > 0)
    def _():
        halo_bc(1, me).wait_recv()

    maps(1, keep_out)

    @pl.loop(0, CHUNKS + wait)
    def _(i):
        @pl.when(i < CHUNKS)
        def _():
            for b in range(ROW):
                inner_part(b, i)

        @pl.when(last & (i == wait))
        def _():
            decode_inputs()

        @pl.when(~early & ~first & (i >= wait))
        def _():
            forward(i - wait)

        @pl.when(first & (i == 3))
        def _():
            pl.semaphore_wait(turn_ok, 2)

            @pl.loop(0, CHUNKS)
            def _(c):
                forward(c)

        @pl.when(i >= wait)
        def _():
            outputs(i - wait)

    @pl.loop(0, CHUNKS)
    def _(c):
        out_own(c).wait()
        for k in range(1, ROW):
            out_arrival(k, c).wait_recv()

    for g in range(GROUPS):
        for q in range(ROW):

            @pl.when(me != 12 + q)
            def _(q=q, g=g):
                dout_arrival(q, g).wait_recv()

        @pl.when(last)
        def _(g=g):
            dout_own(g).wait()

    for k in range(1, ROW):
        st_copy(k).wait_send()
        for m in range(2):
            bc_copy(k, m).wait_send()

    @pl.loop(0, CHUNKS)
    def _(c):
        for k in range(1, ROW):
            x_copy(k, c).wait_send()
            out_copy(k, c).wait_send()

        @pl.when(z < ROW - 1)
        def _():
            @pl.when((z > 0) | ~odd)
            def _():
                carry_copy(c, me + ROW).wait_send()

            halo_x(c, me + ROW).wait_send()

    @pl.when(last)
    def _():
        @pl.loop(0, RING)
        def _(s):
            @pl.when(s != me)
            def _():
                for g in range(GROUPS):
                    dout_copy(s, g).wait_send()

    @pl.when(z < ROW - 1)
    def _():
        for m in range(2):
            halo_bc(m, me + ROW).wait_send()

    for q in range(ROW):

        @pl.when(me != 12 + q)
        def _(q=q):
            for copy in dec_copies(q, me):
                copy.wait_send()


def local(
    heads_pre,
    maps_pre,
    step_prompt,
    head_rate,
    skip_gain,
    conv_head_taps,
    conv_head_bias,
    conv_map_taps,
    filter_mapping_offset,
    heads_dec,
    maps_dec,
    step_dec,
):
    tokens, channels = heads_pre.shape
    groups = maps_pre.shape[2] // STATE
    heads = step_prompt.shape[1]

    bc = jnp.concatenate(
        [maps_pre, maps_dec[0], jnp.zeros((8 - STEPS,) + maps_pre.shape[1:], BF16)], axis=0
    )
    bc = bc.reshape(tokens + 8, 2, groups, STATE).transpose(2, 0, 1, 3)
    bc = bc.reshape(groups, tokens + 8, 2 * STATE)
    steps = step_prompt.T.reshape(ROW, HEADS_Q, tokens)

    any_space = pl.BlockSpec(memory_space=pl.ANY)
    vmem = pl.BlockSpec(memory_space=pltpu.VMEM)
    dma = pltpu.SemaphoreType.DMA
    all_rows = (ROW + 1) * BLOCK
    out, dout = pl.pallas_call(
        kernel,
        out_shape=(
            jax.ShapeDtypeStruct((tokens, channels), BF16),
            jax.ShapeDtypeStruct((STEPS, channels), BF16),
        ),
        in_specs=[any_space] * 5 + [vmem] * 6,
        out_specs=(any_space, any_space),
        scratch_shapes=[
            pltpu.VMEM((HALO + ROW * BLOCK, CHAN_Q), BF16),
            pltpu.VMEM((HALO + ROW * BLOCK, 2 * STATE), BF16),
            pltpu.VMEM((ROW + 1, HEADS_Q, BLOCK), F32),
            pltpu.VMEM((RING, STEPS, CHAN_Q), BF16),
            pltpu.VMEM((RING, 8, 2 * STATE), BF16),
            pltpu.VMEM((RING, STEPS, heads), F32),
            pltpu.VMEM((RING, 8, STATE), F32),
            pltpu.VMEM((BLOCK, BLOCK), F32),
            pltpu.VMEM((BLOCK, BLOCK), F32),
            pltpu.VMEM((BLOCK, BLOCK), F32),
            pltpu.VMEM((all_rows, CHAN_Q), BF16),
            pltpu.VMEM((all_rows, 2 * STATE), BF16),
            pltpu.VMEM((ROW + 1, STATE, BLOCK), BF16),
            pltpu.VMEM((ROW + 1, BLOCK, BLOCK), F32),
            pltpu.VMEM((2, BLOCK, BLOCK), F32),
            pltpu.VMEM((2, BLOCK, BLOCK), F32),
            pltpu.VMEM((ROW + 1, HEADS_Q, BLOCK), F32),
            pltpu.VMEM((CHUNKS, ROW + 1, BLOCK, BLOCK), F32),
            pltpu.VMEM((all_rows, CHAN_Q), F32),
            pltpu.VMEM((all_rows, CHAN_Q), F32),
            pltpu.VMEM((all_rows, CHAN_Q), F32),
            pltpu.VMEM((ROW - 1, STATE, CHAN_Q), F32),
            pltpu.VMEM((STATE, CHAN_Q), F32),
            pltpu.VMEM((CHUNKS, STATE, WIDTH), BF16),
            pltpu.VMEM((CHUNKS, STATE, WIDTH), BF16),
            pltpu.VMEM((ROW * BLOCK, CHAN_Q), BF16),
            pltpu.VMEM((RING, STEPS, CHAN_Q), BF16),
            dma((6,)),
            dma((CHUNKS,)),
            dma((GROUPS,)),
            dma((ROW, CHUNKS)),
            dma((ROW, CHUNKS)),
            dma((ROW, 2)),
            dma((ROW, 2)),
            dma((ROW,)),
            dma((ROW,)),
            dma((CHUNKS + 2,)),
            dma((CHUNKS + 2,)),
            dma((3, ROW)),
            dma((3, RING)),
            dma((CHUNKS,)),
            dma((CHUNKS,)),
            dma((ROW, CHUNKS)),
            dma((ROW, CHUNKS)),
            dma((RING, GROUPS)),
            dma((ROW, GROUPS)),
            pltpu.SemaphoreType.REGULAR,
            pltpu.SemaphoreType.REGULAR,
            pltpu.SemaphoreType.REGULAR,
        ],
        compiler_params=pltpu.CompilerParams(
            collective_id=0, has_side_effects=True, vmem_limit_bytes=44 << 20
        ),
        name="scan_exchange",
    )(
        heads_pre,
        bc,
        steps,
        heads_dec[0],
        step_dec[0],
        conv_head_taps,
        conv_head_bias[None],
        conv_map_taps,
        filter_mapping_offset,
        head_rate[None],
        skip_gain[None],
    )
    return out, dout[None]


def solution(mesh):
    placed = (
        P(("prompt", "seq"), "head"),
        P(("prompt", "seq"), None, "head"),
        P(("prompt", "seq"), "head"),
        P("head"),
        P("head"),
        P(None, "head"),
        P("head"),
        P(None, None, "head"),
        P(None, "head"),
        P(("prompt", "seq"), None, "head"),
        P(("prompt", "seq"), None, None, "head"),
        P(("prompt", "seq"), None, "head"),
    )
    return jax.shard_map(
        local,
        mesh=mesh,
        in_specs=placed,
        out_specs=(P(("prompt", "seq"), "head"), P(("prompt", "seq"), None, "head")),
        check_vma=False,
    )
```

```python
import functools

import jax
import jax.numpy as jnp
from jax import lax
from jax.experimental import pallas as pl
from jax.experimental.pallas import tpu as pltpu
from jax.sharding import PartitionSpec as P

HEAD_DIM = 64
STATE = 256
CONV = 4
BLOCK = 128
STEPS = 4
ROW = 4
RING = 16
HEADS_Q = 16
CHAN_Q = HEADS_Q * HEAD_DIM
CHUNKS = 8
WIDTH = CHAN_Q // CHUNKS
HALO = 8
HEADS_C = HEADS_Q // CHUNKS
AHEAD = 3
GROUPS = 2
GROUP_CHUNKS = CHUNKS // GROUPS
MESH = pl.DeviceIdType.MESH
F32 = jnp.float32
BF16 = jnp.bfloat16
HIGH = lax.Precision.HIGHEST


def silu(v):
    return v * (1.0 / (1.0 + jnp.exp(-v)))


def iota(shape, dim):
    return lax.broadcasted_iota(jnp.int32, shape, dim)


def conv_rows(xin, taps, bias):
    total = bias + taps[0] * pltpu.roll(xin, 3, 0)[HALO:]
    total = total + taps[1] * pltpu.roll(xin, 2, 0)[HALO:]
    total = total + taps[2] * pltpu.roll(xin, 1, 0)[HALO:]
    total = total + taps[3] * xin[HALO:]
    return silu(total)


def conv_cyclic(xin, taps, bias):
    total = bias + taps[0] * pltpu.roll(xin, 3, 0)
    total = total + taps[1] * pltpu.roll(xin, 2, 0)
    total = total + taps[2] * pltpu.roll(xin, 1, 0)
    total = total + taps[3] * xin
    return silu(total)


def kernel(
    x_ref,
    bc_ref,
    st_ref,
    dec_ref,
    decs_ref,
    taps_ref,
    bias_ref,
    mtaps_ref,
    mbias_ref,
    rate_ref,
    skip_ref,
    out_ref,
    dout_ref,
    xbuf,
    bcbuf,
    st_s,
    decx,
    decm,
    decs,
    rows8,
    rate_s,
    skip_s,
    turn_s,
    xc,
    bcc,
    bt,
    scores,
    tri,
    keep_s,
    cum_t,
    cumcol,
    wexp,
    ecexp,
    yacc,
    local_s,
    total_s,
    cin,
    cout,
    outbuf,
    doutbuf,
    lsem,
    lout_sem,
    ldo_sem,
    sx,
    rx,
    sbc,
    rbc,
    sst,
    rst,
    shalo,
    rhalo,
    sdec,
    rdec,
    scar,
    rcar,
    sout,
    rout,
    sdo,
    rdo,
    carry_ok,
    dec_ok,
    turn_ok,
):
    me = lax.axis_index("seq")
    z = me // ROW
    y = me % ROW
    group = y // 2
    base = ROW * z
    last = z == ROW - 1
    prompt = lax.axis_index("prompt")
    odd = prompt // 2 == 1
    early = odd & ~last
    lag = jnp.where(early, 2 * z, 0)
    first = (z == 0) & ~odd
    wait = jnp.where(odd | first, 0, CHUNKS)

    def row_peer(k):
        return lax.rem(y + k, ROW)

    def from_peer(k):
        return lax.rem(y + ROW - k, ROW)

    def rows_of(b):
        return pl.ds(pl.multiple_of(b * BLOCK, BLOCK), BLOCK)

    def in_rows(b):
        return pl.ds(pl.multiple_of(HALO + b * BLOCK, HALO), BLOCK)

    def cols_of(c):
        return pl.ds(pl.multiple_of(c * WIDTH, WIDTH), WIDTH)

    def quarter_cols(q, c):
        return pl.ds(pl.multiple_of(q * CHAN_Q + c * WIDTH, WIDTH), WIDTH)

    def quarter(q):
        return pl.ds(pl.multiple_of(q * CHAN_Q, CHAN_Q), CHAN_Q)

    def half(m):
        return pl.ds(m * STATE, STATE)

    prompt_rows = pl.ds(0, BLOCK)
    end_rows = pl.ds(ROW * BLOCK, HALO)
    dec_rows = pl.ds(BLOCK, STEPS)
    before = pl.ds(0, HALO)

    def remote(src, dst, send, recv, seq):
        return pltpu.make_async_remote_copy(
            src_ref=src,
            dst_ref=dst,
            send_sem=send,
            recv_sem=recv,
            device_id={"seq": seq},
            device_id_type=MESH,
        )

    def x_copy(k, c):
        q = row_peer(k)
        return remote(
            x_ref.at[:, quarter_cols(q, c)],
            xbuf.at[in_rows(y), cols_of(c)],
            sx.at[k, c],
            rx.at[k, c],
            base + q,
        )

    def x_arrival(k, c):
        src = from_peer(k)
        return remote(
            x_ref.at[:, quarter_cols(y, c)],
            xbuf.at[in_rows(src), cols_of(c)],
            sx.at[k, c],
            rx.at[k, c],
            base + src,
        )

    def bc_copy(k, m):
        q = row_peer(k)
        return remote(
            bc_ref.at[q // 2, prompt_rows, half(m)],
            bcbuf.at[in_rows(y), half(m)],
            sbc.at[k, m],
            rbc.at[k, m],
            base + q,
        )

    def bc_arrival(k, m):
        src = from_peer(k)
        return remote(
            bc_ref.at[group, prompt_rows, half(m)],
            bcbuf.at[in_rows(src), half(m)],
            sbc.at[k, m],
            rbc.at[k, m],
            base + src,
        )

    def st_copy(k):
        q = row_peer(k)
        return remote(st_ref.at[q], st_s.at[y], sst.at[k], rst.at[k], base + q)

    def st_arrival(k):
        src = from_peer(k)
        return remote(st_ref.at[y], st_s.at[src], sst.at[k], rst.at[k], base + src)

    def halo_x(c, seq):
        cols = cols_of(c)
        return remote(
            xbuf.at[end_rows, cols], xbuf.at[before, cols], shalo.at[c], rhalo.at[c], seq
        )

    def halo_bc(m, seq):
        return remote(
            bcbuf.at[end_rows, half(m)],
            bcbuf.at[before, half(m)],
            shalo.at[CHUNKS + m],
            rhalo.at[CHUNKS + m],
            seq,
        )

    def dec_copies(q, sample):
        parts = (
            (dec_ref.at[:, quarter(q)], decx.at[sample]),
            (bc_ref.at[q // 2, dec_rows], decm.at[sample]),
            (decs_ref, decs.at[sample]),
        )
        return [
            remote(src, dst, sdec.at[i, q], rdec.at[i, sample], 12 + q)
            for i, (src, dst) in enumerate(parts)
        ]

    own_dec = [
        pltpu.make_async_copy(dec_ref.at[:, quarter(y)], decx.at[me], lsem.at[3]),
        pltpu.make_async_copy(bc_ref.at[group, dec_rows], decm.at[me], lsem.at[4]),
        pltpu.make_async_copy(decs_ref, decs.at[me], lsem.at[5]),
    ]

    def carry_copy(c, seq):
        return remote(cout.at[c], cin.at[c], scar.at[c], rcar.at[c], seq)

    def out_copy(k, c):
        b = row_peer(k)
        return remote(
            outbuf.at[rows_of(b), cols_of(c)],
            out_ref.at[:, quarter_cols(y, c)],
            sout.at[k, c],
            rout.at[k, c],
            base + b,
        )

    def out_arrival(k, c):
        src = from_peer(k)
        return remote(
            outbuf.at[rows_of(y), cols_of(c)],
            out_ref.at[:, quarter_cols(src, c)],
            sout.at[k, c],
            rout.at[k, c],
            base + src,
        )

    def out_own(c):
        return pltpu.make_async_copy(
            outbuf.at[rows_of(y), cols_of(c)], out_ref.at[:, quarter_cols(y, c)], lout_sem.at[c]
        )

    def group_cols(q, g):
        size = CHAN_Q // GROUPS
        return pl.ds(pl.multiple_of(q * CHAN_Q + g * size, size), size)

    def dout_copy(sample, g):
        return remote(
            doutbuf.at[sample, :, group_cols(0, g)],
            dout_ref.at[:, group_cols(y, g)],
            sdo.at[sample, g],
            rdo.at[y, g],
            sample,
        )

    def dout_arrival(q, g):
        return remote(
            doutbuf.at[me, :, group_cols(0, g)],
            dout_ref.at[:, group_cols(q, g)],
            sdo.at[me, g],
            rdo.at[q, g],
            12 + q,
        )

    def dout_own(g):
        return pltpu.make_async_copy(
            doutbuf.at[me, :, group_cols(0, g)], dout_ref.at[:, group_cols(y, g)], ldo_sem.at[g]
        )

    own_x = pltpu.make_async_copy(x_ref.at[:, quarter(y)], xbuf.at[in_rows(y)], lsem.at[0])
    own_bc = pltpu.make_async_copy(bc_ref.at[group, prompt_rows], bcbuf.at[in_rows(y)], lsem.at[1])
    own_st = pltpu.make_async_copy(st_ref.at[y], st_s.at[y], lsem.at[2])

    def signal(sem, seq):
        pl.semaphore_signal(sem, inc=1, device_id={"seq": seq}, device_id_type=MESH)

    barrier = pltpu.get_barrier_semaphore()
    for k in range(1, ROW):
        signal(barrier, base + row_peer(k))

    def signal_chip(sem, first):
        for core in range(2):
            pl.semaphore_signal(
                sem, inc=1, device_id={"prompt": first + core}, device_id_type=MESH
            )

    @pl.when((z == 0) & ~odd)
    def _():
        signal_chip(barrier, 2)

    own_st.start()
    own_bc.start()
    own_x.start()

    @pl.when(last)
    def _():
        for copy in own_dec:
            copy.start()

    r_i, c_i = iota((BLOCK, BLOCK), 0), iota((BLOCK, BLOCK), 1)
    same = (r_i // 8) == (c_i // 8)
    left = c_i < HEAD_DIM
    tri[0] = jnp.where(r_i <= c_i, 1.0, 0.0).astype(F32)
    tri[1] = jnp.where((r_i <= c_i) & same, 1.0, 0.0).astype(F32)
    keep_s[0] = jnp.where(r_i >= c_i, 1.0, 0.0).astype(F32)
    keep_s[1] = jnp.where((r_i >= c_i) & same, 1.0, 0.0).astype(F32)

    def spread(ref):
        wide = jnp.broadcast_to(ref[...], (BLOCK, ref.shape[1]))
        return jnp.transpose(jnp.concatenate([wide, wide], axis=1))

    rate_s[...] = spread(rate_ref)
    skip_s[...] = spread(skip_ref)

    @pl.when(z == 0)
    def _():
        xbuf[before] = jnp.zeros((HALO, CHAN_Q), BF16)
        bcbuf[before] = jnp.zeros((HALO, 2 * STATE), BF16)
        cin[...] = jnp.zeros_like(cin)

    pl.semaphore_wait(barrier, jnp.where(z > 0, ROW, jnp.where(odd, ROW + 1, ROW - 1)))

    @pl.when(z < ROW - 1)
    def _():
        signal(barrier, me + ROW)

    for k in range(1, ROW):
        st_copy(k).start()
    for k in range(1, ROW):
        bc_copy(k, 0).start()
    for k in range(1, ROW):
        x_copy(k, 0).start()

    @pl.when(z > 0)
    def _():
        signal(carry_ok, me - ROW)

    @pl.when(last)
    def _():
        @pl.loop(0, RING)
        def _(s):
            @pl.when(s != me)
            def _():
                signal(dec_ok, s)

    def send_decode():
        pl.semaphore_wait(dec_ok, jnp.where(last, ROW - 1, ROW))

        for q in range(ROW):

            @pl.when(me != 12 + q)
            def _(q=q):
                for copy in dec_copies(q, me):
                    copy.start()

    def steps_of(b, m):
        step = st_s[b]
        drop = -(step * rate_s[pl.ds(pl.multiple_of(y * HEADS_Q, HEADS_Q), HEADS_Q)])
        cum = jnp.dot(drop, tri[m], precision=HIGH, preferred_element_type=F32)
        cum_t[b] = cum
        weight = jnp.exp(cum[:, BLOCK - 1 : BLOCK] - cum) * step
        stack = jnp.concatenate(
            [cum, weight, jnp.exp(cum), jnp.zeros((BLOCK - 3 * HEADS_Q, BLOCK), F32)], axis=0
        )
        turned = jnp.transpose(stack)
        for c in range(CHUNKS):
            shift = (BLOCK - c * HEADS_C) % BLOCK
            cumcol[c, b] = pltpu.roll(turned, shift, 1) if shift else turned
        for j in range(HEADS_Q // 2):
            cols = pl.ds(j * BLOCK, BLOCK)

            def pair(first):
                one = jnp.broadcast_to(turned[:, first : first + 1], (BLOCK, BLOCK))
                two = jnp.broadcast_to(turned[:, first + 1 : first + 2], (BLOCK, BLOCK))
                return jnp.where(left, one, two)

            wexp[rows_of(b), cols] = pair(HEADS_Q + 2 * j)
            ecexp[rows_of(b), cols] = pair(2 * HEADS_Q + 2 * j)

    map_cols = pl.ds(pl.multiple_of(group * STATE, STATE), STATE)

    def map_taps(m):
        return [mtaps_ref[j, pl.ds(m, 1), map_cols] for j in range(CONV)], mbias_ref[
            pl.ds(m, 1), map_cols
        ]

    def keep_in(b, conv):
        bcc[rows_of(b), half(0)] = conv.astype(BF16)
        bt[b] = jnp.transpose(conv).astype(BF16)

    def keep_out(b, conv):
        low = conv.astype(BF16)
        bcc[rows_of(b), half(1)] = low
        score = lax.dot_general(
            low, bcc[rows_of(b), half(0)], (((1,), (1,)), ((), ())), preferred_element_type=F32
        )
        scores[b] = score * keep_s[b // ROW]

    def chan_taps(c):
        cols = quarter_cols(y, c)
        return [taps_ref[pl.ds(j, 1), cols] for j in range(CONV)], bias_ref[:, cols]

    def gain(b, cols):
        return ecexp[pl.ds(b * BLOCK + BLOCK - 1, 1), cols]

    def maps(m, keep):
        taps, bias = map_taps(m)

        @pl.loop(0, ROW)
        def _(b):
            rows = pl.ds(pl.multiple_of(b * BLOCK, BLOCK), BLOCK + HALO)
            keep(b, conv_rows(bcbuf[rows, half(m)].astype(F32), taps, bias))

    own_st.wait()
    for k in range(1, ROW):
        st_arrival(k).wait_recv()

    @pl.loop(0, ROW)
    def _(b):
        steps_of(b, 0)

    own_bc.wait()
    for k in range(1, ROW):
        bc_arrival(k, 0).wait_recv()

    for c in range(1, AHEAD):
        for k in range(1, ROW):
            x_copy(k, c).start()

    @pl.when(z < ROW - 1)
    def _():
        pl.semaphore_wait(carry_ok, 1)
        halo_bc(0, me + ROW).start()

    @pl.when(z > 0)
    def _():
        halo_bc(0, me).wait_recv()

    maps(0, keep_in)
    own_x.wait()

    def send_carry(c, state):
        cout[c] = state.astype(BF16)
        carry_copy(c, me + ROW).start()

    def block_states(c):
        for k in range(1, ROW):
            x_arrival(k, c).wait_recv()

        @pl.when(c < CHUNKS - AHEAD)
        def _():
            for k in range(1, ROW):
                x_copy(k, c + AHEAD).start()

        @pl.when(z < ROW - 1)
        def _():
            halo_x(c, me + ROW).start()

        @pl.when(z > 0)
        def _():
            halo_x(c, me).wait_recv()

        cols = cols_of(c)
        taps, bias = chan_taps(c)
        state = None
        for b in range(ROW):
            xin = xbuf[pl.ds(b * BLOCK, BLOCK + HALO), cols].astype(F32)
            low = conv_rows(xin, taps, bias).astype(BF16)
            xc[pl.ds(b * BLOCK, BLOCK), cols] = low
            weighted = (low.astype(F32) * wexp[pl.ds(b * BLOCK, BLOCK), cols]).astype(BF16)
            block_state = jnp.dot(bt[b], weighted, preferred_element_type=F32)
            state = block_state if b == 0 else gain(b, cols) * state + block_state
            if b < ROW - 1:
                local_s[b, :, cols] = state
            else:
                total_s[:, cols] = state

    def with_tail(new, tail):
        width = new.shape[-1]
        rows8[:, 0:STEPS, 0:width] = new
        rows8[:, STEPS:8, 0:width] = jnp.broadcast_to(tail[None], (RING, 8 - STEPS, width))
        return rows8[:, :, 0:width].reshape(BLOCK, width)

    def decode_inputs():
        for copy in own_dec:
            copy.wait()

        @pl.loop(0, RING)
        def _(s):
            @pl.when(s != me)
            def _():
                for copy in dec_copies(y, s):
                    copy.wait_recv()

        rows8[:, :, 0:BLOCK] = jnp.zeros((RING, 8, BLOCK), F32)
        rows8[:, 0:STEPS, 0:64] = decs[...]
        turn_s[...] = jnp.transpose(rows8[:, :, 0:BLOCK].reshape(BLOCK, BLOCK))
        st_s[ROW] = turn_s[pl.ds(pl.multiple_of(y * HEADS_Q, HEADS_Q), HEADS_Q)]
        steps_of(ROW, 1)
        end = pl.ds(ROW * BLOCK, HALO)
        for m, keep in ((0, keep_in), (1, keep_out)):
            taps, bias = map_taps(m)
            new = decm[:, :, m * STATE : (m + 1) * STATE].astype(F32)
            tail = bcbuf[end, half(m)].astype(F32)[STEPS:8]
            keep(ROW, conv_cyclic(with_tail(new, tail), taps, bias))

        @pl.loop(0, CHUNKS)
        def _(c):
            cols = cols_of(c)
            taps, bias = chan_taps(c)
            tail = xbuf[end, cols].astype(F32)[STEPS:8]
            conv = conv_cyclic(with_tail(decx[:, :, cols].astype(F32), tail), taps, bias)
            xc[pl.ds(ROW * BLOCK, BLOCK), cols] = conv.astype(BF16)
            inner_part(ROW, c)

    def inner_part(b, c):
        rows = pl.ds(b * BLOCK, BLOCK)
        score = scores[b]
        columns = cumcol[c, b]
        for pair in range(HEADS_C // 2):
            mixes = []
            for j in (2 * pair, 2 * pair + 1):
                head = c * HEADS_C + j
                row = cum_t[b, pl.ds(head, 1)]
                step = st_s[b, pl.ds(head, 1)]
                gap = columns[:, j : j + 1] - row
                mixes.append((score * jnp.exp(gap) * step).astype(BF16))
            mixing = jnp.concatenate(mixes, axis=1)
            cols = pl.ds(pl.multiple_of(c * WIDTH + pair * BLOCK, BLOCK), BLOCK)
            xp = xc[rows, cols].astype(F32)
            blockdiag = jnp.concatenate(
                [jnp.where(left, xp, 0.0).astype(BF16), jnp.where(left, 0.0, xp).astype(BF16)],
                axis=0,
            )
            inner = jnp.dot(mixing, blockdiag, preferred_element_type=F32)
            head = y * HEADS_Q + c * HEADS_C + 2 * pair
            skip = jnp.where(left[0:1], skip_s[pl.ds(head, 1)], skip_s[pl.ds(head + 1, 1)])
            yacc[rows, cols] = inner + skip * xp

    def leads_of(cols):
        leads = [gain(0, cols)]
        for b in range(1, ROW):
            leads.append(leads[-1] * gain(b, cols))
        return leads

    def forward(c):
        @pl.when(z > 0)
        def _():
            carry_copy(c, me).wait_recv()

        @pl.when(z < ROW - 1)
        def _():
            cols = cols_of(c)
            lead = leads_of(cols)[ROW - 1]
            send_carry(c, total_s[:, cols] + lead * cin[c].astype(F32))

    def outputs(c):
        cols = cols_of(c)
        leads = leads_of(cols)
        carry = cin[c].astype(F32)
        @pl.when(last)
        def _():
            final = total_s[:, cols] + leads[ROW - 1] * carry
            high = final.astype(BF16)
            rest = (final - high.astype(F32)).astype(BF16)
            rows = pl.ds(ROW * BLOCK, BLOCK)
            out_map = bcc[rows, half(1)]
            cross = jnp.dot(out_map, high, preferred_element_type=F32) + jnp.dot(
                out_map, rest, preferred_element_type=F32
            )
            result = yacc[rows, cols] + ecexp[rows, cols] * cross
            rows8[:, :, 0:WIDTH] = result.reshape(RING, 8, WIDTH)
            doutbuf[:, :, cols] = rows8[:, 0:STEPS, 0:WIDTH].astype(BF16)

            @pl.when(c % GROUP_CHUNKS == GROUP_CHUNKS - 1)
            def _():
                g = c // GROUP_CHUNKS
                dout_own(g).start()

                @pl.loop(0, RING)
                def _(s):
                    @pl.when(s != me)
                    def _():
                        dout_copy(s, g).start()

        for b in range(ROW):
            rows = pl.ds(b * BLOCK, BLOCK)
            if b == 0:
                entry = cin[c]
            else:
                entry = (local_s[b - 1, :, cols] + leads[b - 1] * carry).astype(BF16)
            cross = jnp.dot(bcc[rows, half(1)], entry, preferred_element_type=F32)
            outbuf[rows, cols] = (yacc[rows, cols] + ecexp[rows, cols] * cross).astype(BF16)
        out_own(c).start()
        for k in range(1, ROW):
            out_copy(k, c).start()

    send_decode()

    @pl.loop(0, CHUNKS + lag)
    def _(i):
        @pl.when(i < CHUNKS)
        def _():
            block_states(i)

        @pl.when(i == 4)
        def _():
            for k in range(1, ROW):
                bc_copy(k, 1).start()

        @pl.when(early & (i >= lag))
        def _():
            forward(i - lag)

    @pl.when((z == 0) & odd)
    def _():
        for c in range(CHUNKS):
            carry_copy(c, me + ROW).wait_send()
        signal_chip(turn_ok, 0)

    for k in range(1, ROW):
        bc_arrival(k, 1).wait_recv()

    @pl.when(z < ROW - 1)
    def _():
        halo_bc(1, me + ROW).start()

    @pl.when(z > 0)
    def _():
        halo_bc(1, me).wait_recv()

    maps(1, keep_out)

    @pl.loop(0, CHUNKS + wait)
    def _(i):
        @pl.when(i < CHUNKS)
        def _():
            for b in range(ROW):
                inner_part(b, i)

        @pl.when(last & (i == wait))
        def _():
            decode_inputs()

        @pl.when(~early & ~first & (i >= wait))
        def _():
            forward(i - wait)

        @pl.when(first & (i == 3))
        def _():
            pl.semaphore_wait(turn_ok, 2)

            @pl.loop(0, CHUNKS)
            def _(c):
                forward(c)

        @pl.when(i >= wait)
        def _():
            outputs(i - wait)

    @pl.loop(0, CHUNKS)
    def _(c):
        out_own(c).wait()
        for k in range(1, ROW):
            out_arrival(k, c).wait_recv()

    for g in range(GROUPS):
        for q in range(ROW):

            @pl.when(me != 12 + q)
            def _(q=q, g=g):
                dout_arrival(q, g).wait_recv()

        @pl.when(last)
        def _(g=g):
            dout_own(g).wait()

    for k in range(1, ROW):
        st_copy(k).wait_send()
        for m in range(2):
            bc_copy(k, m).wait_send()

    @pl.loop(0, CHUNKS)
    def _(c):
        for k in range(1, ROW):
            x_copy(k, c).wait_send()
            out_copy(k, c).wait_send()

        @pl.when(z < ROW - 1)
        def _():
            @pl.when((z > 0) | ~odd)
            def _():
                carry_copy(c, me + ROW).wait_send()

            halo_x(c, me + ROW).wait_send()

    @pl.when(last)
    def _():
        @pl.loop(0, RING)
        def _(s):
            @pl.when(s != me)
            def _():
                for g in range(GROUPS):
                    dout_copy(s, g).wait_send()

    @pl.when(z < ROW - 1)
    def _():
        for m in range(2):
            halo_bc(m, me + ROW).wait_send()

    for q in range(ROW):

        @pl.when(me != 12 + q)
        def _(q=q):
            for copy in dec_copies(q, me):
                copy.wait_send()


def local(
    heads_pre,
    maps_pre,
    step_prompt,
    head_rate,
    skip_gain,
    conv_head_taps,
    conv_head_bias,
    conv_map_taps,
    filter_mapping_offset,
    heads_dec,
    maps_dec,
    step_dec,
):
    tokens, channels = heads_pre.shape
    groups = maps_pre.shape[2] // STATE
    heads = step_prompt.shape[1]

    bc = jnp.concatenate(
        [maps_pre, maps_dec[0], jnp.zeros((8 - STEPS,) + maps_pre.shape[1:], BF16)], axis=0
    )
    bc = bc.reshape(tokens + 8, 2, groups, STATE).transpose(2, 0, 1, 3)
    bc = bc.reshape(groups, tokens + 8, 2 * STATE)
    steps = step_prompt.T.reshape(ROW, HEADS_Q, tokens)

    any_space = pl.BlockSpec(memory_space=pl.ANY)
    vmem = pl.BlockSpec(memory_space=pltpu.VMEM)
    dma = pltpu.SemaphoreType.DMA
    all_rows = (ROW + 1) * BLOCK
    out, dout = pl.pallas_call(
        kernel,
        out_shape=(
            jax.ShapeDtypeStruct((tokens, channels), BF16),
            jax.ShapeDtypeStruct((STEPS, channels), BF16),
        ),
        in_specs=[any_space] * 5 + [vmem] * 6,
        out_specs=(any_space, any_space),
        scratch_shapes=[
            pltpu.VMEM((HALO + ROW * BLOCK, CHAN_Q), BF16),
            pltpu.VMEM((HALO + ROW * BLOCK, 2 * STATE), BF16),
            pltpu.VMEM((ROW + 1, HEADS_Q, BLOCK), F32),
            pltpu.VMEM((RING, STEPS, CHAN_Q), BF16),
            pltpu.VMEM((RING, STEPS, 2 * STATE), BF16),
            pltpu.VMEM((RING, STEPS, heads), F32),
            pltpu.VMEM((RING, 8, STATE), F32),
            pltpu.VMEM((BLOCK, BLOCK), F32),
            pltpu.VMEM((BLOCK, BLOCK), F32),
            pltpu.VMEM((BLOCK, BLOCK), F32),
            pltpu.VMEM((all_rows, CHAN_Q), BF16),
            pltpu.VMEM((all_rows, 2 * STATE), BF16),
            pltpu.VMEM((ROW + 1, STATE, BLOCK), BF16),
            pltpu.VMEM((ROW + 1, BLOCK, BLOCK), F32),
            pltpu.VMEM((2, BLOCK, BLOCK), F32),
            pltpu.VMEM((2, BLOCK, BLOCK), F32),
            pltpu.VMEM((ROW + 1, HEADS_Q, BLOCK), F32),
            pltpu.VMEM((CHUNKS, ROW + 1, BLOCK, BLOCK), F32),
            pltpu.VMEM((all_rows, CHAN_Q), F32),
            pltpu.VMEM((all_rows, CHAN_Q), F32),
            pltpu.VMEM((all_rows, CHAN_Q), F32),
            pltpu.VMEM((ROW - 1, STATE, CHAN_Q), F32),
            pltpu.VMEM((STATE, CHAN_Q), F32),
            pltpu.VMEM((CHUNKS, STATE, WIDTH), BF16),
            pltpu.VMEM((CHUNKS, STATE, WIDTH), BF16),
            pltpu.VMEM((ROW * BLOCK, CHAN_Q), BF16),
            pltpu.VMEM((RING, STEPS, CHAN_Q), BF16),
            dma((6,)),
            dma((CHUNKS,)),
            dma((GROUPS,)),
            dma((ROW, CHUNKS)),
            dma((ROW, CHUNKS)),
            dma((ROW, 2)),
            dma((ROW, 2)),
            dma((ROW,)),
            dma((ROW,)),
            dma((CHUNKS + 2,)),
            dma((CHUNKS + 2,)),
            dma((3, ROW)),
            dma((3, RING)),
            dma((CHUNKS,)),
            dma((CHUNKS,)),
            dma((ROW, CHUNKS)),
            dma((ROW, CHUNKS)),
            dma((RING, GROUPS)),
            dma((ROW, GROUPS)),
            pltpu.SemaphoreType.REGULAR,
            pltpu.SemaphoreType.REGULAR,
            pltpu.SemaphoreType.REGULAR,
        ],
        compiler_params=pltpu.CompilerParams(
            collective_id=0, has_side_effects=True, vmem_limit_bytes=44 << 20
        ),
        name="scan_exchange",
    )(
        heads_pre,
        bc,
        steps,
        heads_dec[0],
        step_dec[0],
        conv_head_taps,
        conv_head_bias[None],
        conv_map_taps,
        filter_mapping_offset,
        head_rate[None],
        skip_gain[None],
    )
    return out, dout[None]


def solution(mesh):
    placed = (
        P(("prompt", "seq"), "head"),
        P(("prompt", "seq"), None, "head"),
        P(("prompt", "seq"), "head"),
        P("head"),
        P("head"),
        P(None, "head"),
        P("head"),
        P(None, None, "head"),
        P(None, "head"),
        P(("prompt", "seq"), None, "head"),
        P(("prompt", "seq"), None, None, "head"),
        P(("prompt", "seq"), None, "head"),
    )
    return jax.shard_map(
        local,
        mesh=mesh,
        in_specs=placed,
        out_specs=(P(("prompt", "seq"), "head"), P(("prompt", "seq"), None, "head")),
        check_vma=False,
    )
```

```python
import functools

import jax
import jax.numpy as jnp
from jax import lax
from jax.experimental import pallas as pl
from jax.experimental.pallas import tpu as pltpu
from jax.sharding import PartitionSpec as P

HEAD_DIM = 64
STATE = 256
CONV = 4
BLOCK = 128
STEPS = 4
ROW = 4
RING = 16
HEADS_Q = 16
CHAN_Q = HEADS_Q * HEAD_DIM
CHUNKS = 8
WIDTH = CHAN_Q // CHUNKS
HALO = 8
HEADS_C = HEADS_Q // CHUNKS
AHEAD = 3
GROUPS = 2
GROUP_CHUNKS = CHUNKS // GROUPS
MESH = pl.DeviceIdType.MESH
F32 = jnp.float32
BF16 = jnp.bfloat16
HIGH = lax.Precision.HIGHEST


def silu(v):
    return v * (1.0 / (1.0 + jnp.exp(-v)))


def iota(shape, dim):
    return lax.broadcasted_iota(jnp.int32, shape, dim)


def conv_rows(xin, taps, bias):
    total = bias + taps[0] * pltpu.roll(xin, 3, 0)[HALO:]
    total = total + taps[1] * pltpu.roll(xin, 2, 0)[HALO:]
    total = total + taps[2] * pltpu.roll(xin, 1, 0)[HALO:]
    total = total + taps[3] * xin[HALO:]
    return silu(total)


def conv_cyclic(xin, taps, bias):
    total = bias + taps[0] * pltpu.roll(xin, 3, 0)
    total = total + taps[1] * pltpu.roll(xin, 2, 0)
    total = total + taps[2] * pltpu.roll(xin, 1, 0)
    total = total + taps[3] * xin
    return silu(total)


def kernel(
    x_ref,
    bc_ref,
    st_ref,
    dec_ref,
    decs_ref,
    taps_ref,
    bias_ref,
    mtaps_ref,
    mbias_ref,
    rate_ref,
    skip_ref,
    out_ref,
    dout_ref,
    xbuf,
    bcbuf,
    st_s,
    decx,
    decm,
    decs,
    rows8,
    rate_s,
    skip_s,
    turn_s,
    xc,
    bcc,
    bt,
    scores,
    tri,
    keep_s,
    cum_t,
    cumcol,
    wexp,
    ecexp,
    yacc,
    local_s,
    total_s,
    cin,
    cout,
    outbuf,
    doutbuf,
    lsem,
    lout_sem,
    ldo_sem,
    sx,
    rx,
    sbc,
    rbc,
    sst,
    rst,
    shalo,
    rhalo,
    sdec,
    rdec,
    scar,
    rcar,
    sout,
    rout,
    sdo,
    rdo,
    carry_ok,
    dec_ok,
    turn_ok,
):
    me = lax.axis_index("seq")
    z = me // ROW
    y = me % ROW
    group = y // 2
    base = ROW * z
    last = z == ROW - 1
    prompt = lax.axis_index("prompt")
    odd = prompt // 2 == 1
    early = odd & ~last
    lag = jnp.where(early, z, 0)
    first = (z == 0) & ~odd
    wait = jnp.where(odd | first, 0, CHUNKS)

    def row_peer(k):
        return lax.rem(y + k, ROW)

    def from_peer(k):
        return lax.rem(y + ROW - k, ROW)

    def rows_of(b):
        return pl.ds(pl.multiple_of(b * BLOCK, BLOCK), BLOCK)

    def in_rows(b):
        return pl.ds(pl.multiple_of(HALO + b * BLOCK, HALO), BLOCK)

    def cols_of(c):
        return pl.ds(pl.multiple_of(c * WIDTH, WIDTH), WIDTH)

    def quarter_cols(q, c):
        return pl.ds(pl.multiple_of(q * CHAN_Q + c * WIDTH, WIDTH), WIDTH)

    def quarter(q):
        return pl.ds(pl.multiple_of(q * CHAN_Q, CHAN_Q), CHAN_Q)

    def half(m):
        return pl.ds(m * STATE, STATE)

    prompt_rows = pl.ds(0, BLOCK)
    end_rows = pl.ds(ROW * BLOCK, HALO)
    dec_rows = pl.ds(BLOCK, STEPS)
    before = pl.ds(0, HALO)

    def remote(src, dst, send, recv, seq):
        return pltpu.make_async_remote_copy(
            src_ref=src,
            dst_ref=dst,
            send_sem=send,
            recv_sem=recv,
            device_id={"seq": seq},
            device_id_type=MESH,
        )

    def x_copy(k, c):
        q = row_peer(k)
        return remote(
            x_ref.at[:, quarter_cols(q, c)],
            xbuf.at[in_rows(y), cols_of(c)],
            sx.at[k, c],
            rx.at[k, c],
            base + q,
        )

    def x_arrival(k, c):
        src = from_peer(k)
        return remote(
            x_ref.at[:, quarter_cols(y, c)],
            xbuf.at[in_rows(src), cols_of(c)],
            sx.at[k, c],
            rx.at[k, c],
            base + src,
        )

    def bc_copy(k, m):
        q = row_peer(k)
        return remote(
            bc_ref.at[q // 2, prompt_rows, half(m)],
            bcbuf.at[in_rows(y), half(m)],
            sbc.at[k, m],
            rbc.at[k, m],
            base + q,
        )

    def bc_arrival(k, m):
        src = from_peer(k)
        return remote(
            bc_ref.at[group, prompt_rows, half(m)],
            bcbuf.at[in_rows(src), half(m)],
            sbc.at[k, m],
            rbc.at[k, m],
            base + src,
        )

    def st_copy(k):
        q = row_peer(k)
        return remote(st_ref.at[q], st_s.at[y], sst.at[k], rst.at[k], base + q)

    def st_arrival(k):
        src = from_peer(k)
        return remote(st_ref.at[y], st_s.at[src], sst.at[k], rst.at[k], base + src)

    def halo_x(c, seq):
        cols = cols_of(c)
        return remote(
            xbuf.at[end_rows, cols], xbuf.at[before, cols], shalo.at[c], rhalo.at[c], seq
        )

    def halo_bc(m, seq):
        return remote(
            bcbuf.at[end_rows, half(m)],
            bcbuf.at[before, half(m)],
            shalo.at[CHUNKS + m],
            rhalo.at[CHUNKS + m],
            seq,
        )

    def dec_copies(q, sample):
        parts = (
            (dec_ref.at[:, quarter(q)], decx.at[sample]),
            (bc_ref.at[q // 2, dec_rows], decm.at[sample]),
            (decs_ref, decs.at[sample]),
        )
        return [
            remote(src, dst, sdec.at[i, q], rdec.at[i, sample], 12 + q)
            for i, (src, dst) in enumerate(parts)
        ]

    own_dec = [
        pltpu.make_async_copy(dec_ref.at[:, quarter(y)], decx.at[me], lsem.at[3]),
        pltpu.make_async_copy(bc_ref.at[group, dec_rows], decm.at[me], lsem.at[4]),
        pltpu.make_async_copy(decs_ref, decs.at[me], lsem.at[5]),
    ]

    def carry_copy(c, seq):
        return remote(cout.at[c], cin.at[c], scar.at[c], rcar.at[c], seq)

    def out_copy(k, c):
        b = row_peer(k)
        return remote(
            outbuf.at[rows_of(b), cols_of(c)],
            out_ref.at[:, quarter_cols(y, c)],
            sout.at[k, c],
            rout.at[k, c],
            base + b,
        )

    def out_arrival(k, c):
        src = from_peer(k)
        return remote(
            outbuf.at[rows_of(y), cols_of(c)],
            out_ref.at[:, quarter_cols(src, c)],
            sout.at[k, c],
            rout.at[k, c],
            base + src,
        )

    def out_own(c):
        return pltpu.make_async_copy(
            outbuf.at[rows_of(y), cols_of(c)], out_ref.at[:, quarter_cols(y, c)], lout_sem.at[c]
        )

    def group_cols(q, g):
        size = CHAN_Q // GROUPS
        return pl.ds(pl.multiple_of(q * CHAN_Q + g * size, size), size)

    def dout_copy(sample, g):
        return remote(
            doutbuf.at[sample, :, group_cols(0, g)],
            dout_ref.at[:, group_cols(y, g)],
            sdo.at[sample, g],
            rdo.at[y, g],
            sample,
        )

    def dout_arrival(q, g):
        return remote(
            doutbuf.at[me, :, group_cols(0, g)],
            dout_ref.at[:, group_cols(q, g)],
            sdo.at[me, g],
            rdo.at[q, g],
            12 + q,
        )

    def dout_own(g):
        return pltpu.make_async_copy(
            doutbuf.at[me, :, group_cols(0, g)], dout_ref.at[:, group_cols(y, g)], ldo_sem.at[g]
        )

    own_x = pltpu.make_async_copy(x_ref.at[:, quarter(y)], xbuf.at[in_rows(y)], lsem.at[0])
    own_bc = pltpu.make_async_copy(bc_ref.at[group, prompt_rows], bcbuf.at[in_rows(y)], lsem.at[1])
    own_st = pltpu.make_async_copy(st_ref.at[y], st_s.at[y], lsem.at[2])

    def signal(sem, seq):
        pl.semaphore_signal(sem, inc=1, device_id={"seq": seq}, device_id_type=MESH)

    barrier = pltpu.get_barrier_semaphore()
    for k in range(1, ROW):
        signal(barrier, base + row_peer(k))

    def signal_chip(sem, first):
        for core in range(2):
            pl.semaphore_signal(
                sem, inc=1, device_id={"prompt": first + core}, device_id_type=MESH
            )

    @pl.when((z == 0) & ~odd)
    def _():
        signal_chip(barrier, 2)

    own_st.start()
    own_bc.start()
    own_x.start()

    @pl.when(last)
    def _():
        for copy in own_dec:
            copy.start()

    r_i, c_i = iota((BLOCK, BLOCK), 0), iota((BLOCK, BLOCK), 1)
    same = (r_i // 8) == (c_i // 8)
    left = c_i < HEAD_DIM
    tri[0] = jnp.where(r_i <= c_i, 1.0, 0.0).astype(F32)
    tri[1] = jnp.where((r_i <= c_i) & same, 1.0, 0.0).astype(F32)
    keep_s[0] = jnp.where(r_i >= c_i, 1.0, 0.0).astype(F32)
    keep_s[1] = jnp.where((r_i >= c_i) & same, 1.0, 0.0).astype(F32)

    def spread(ref):
        wide = jnp.broadcast_to(ref[...], (BLOCK, ref.shape[1]))
        return jnp.transpose(jnp.concatenate([wide, wide], axis=1))

    rate_s[...] = spread(rate_ref)
    skip_s[...] = spread(skip_ref)

    @pl.when(z == 0)
    def _():
        xbuf[before] = jnp.zeros((HALO, CHAN_Q), BF16)
        bcbuf[before] = jnp.zeros((HALO, 2 * STATE), BF16)
        cin[...] = jnp.zeros_like(cin)

    pl.semaphore_wait(barrier, jnp.where(z > 0, ROW, jnp.where(odd, ROW + 1, ROW - 1)))

    @pl.when(z < ROW - 1)
    def _():
        signal(barrier, me + ROW)

    for k in range(1, ROW):
        st_copy(k).start()
    for k in range(1, ROW):
        bc_copy(k, 0).start()
    for k in range(1, ROW):
        x_copy(k, 0).start()

    @pl.when(z > 0)
    def _():
        signal(carry_ok, me - ROW)

    @pl.when(last)
    def _():
        @pl.loop(0, RING)
        def _(s):
            @pl.when(s != me)
            def _():
                signal(dec_ok, s)

    def send_decode():
        pl.semaphore_wait(dec_ok, jnp.where(last, ROW - 1, ROW))

        for q in range(ROW):

            @pl.when(me != 12 + q)
            def _(q=q):
                for copy in dec_copies(q, me):
                    copy.start()

    def steps_of(b, m):
        step = st_s[b]
        drop = -(step * rate_s[pl.ds(pl.multiple_of(y * HEADS_Q, HEADS_Q), HEADS_Q)])
        cum = jnp.dot(drop, tri[m], precision=HIGH, preferred_element_type=F32)
        cum_t[b] = cum
        weight = jnp.exp(cum[:, BLOCK - 1 : BLOCK] - cum) * step
        stack = jnp.concatenate(
            [cum, weight, jnp.exp(cum), jnp.zeros((BLOCK - 3 * HEADS_Q, BLOCK), F32)], axis=0
        )
        turned = jnp.transpose(stack)
        for c in range(CHUNKS):
            shift = (BLOCK - c * HEADS_C) % BLOCK
            cumcol[c, b] = pltpu.roll(turned, shift, 1) if shift else turned
        for j in range(HEADS_Q // 2):
            cols = pl.ds(j * BLOCK, BLOCK)

            def pair(first):
                one = jnp.broadcast_to(turned[:, first : first + 1], (BLOCK, BLOCK))
                two = jnp.broadcast_to(turned[:, first + 1 : first + 2], (BLOCK, BLOCK))
                return jnp.where(left, one, two)

            wexp[rows_of(b), cols] = pair(HEADS_Q + 2 * j)
            ecexp[rows_of(b), cols] = pair(2 * HEADS_Q + 2 * j)

    map_cols = pl.ds(pl.multiple_of(group * STATE, STATE), STATE)

    def map_taps(m):
        return [mtaps_ref[j, pl.ds(m, 1), map_cols] for j in range(CONV)], mbias_ref[
            pl.ds(m, 1), map_cols
        ]

    def keep_in(b, conv):
        bcc[rows_of(b), half(0)] = conv.astype(BF16)
        bt[b] = jnp.transpose(conv).astype(BF16)

    def keep_out(b, conv):
        low = conv.astype(BF16)
        bcc[rows_of(b), half(1)] = low
        score = lax.dot_general(
            low, bcc[rows_of(b), half(0)], (((1,), (1,)), ((), ())), preferred_element_type=F32
        )
        scores[b] = score * keep_s[b // ROW]

    def chan_taps(c):
        cols = quarter_cols(y, c)
        return [taps_ref[pl.ds(j, 1), cols] for j in range(CONV)], bias_ref[:, cols]

    def gain(b, cols):
        return ecexp[pl.ds(b * BLOCK + BLOCK - 1, 1), cols]

    def maps(m, keep):
        taps, bias = map_taps(m)

        @pl.loop(0, ROW)
        def _(b):
            rows = pl.ds(pl.multiple_of(b * BLOCK, BLOCK), BLOCK + HALO)
            keep(b, conv_rows(bcbuf[rows, half(m)].astype(F32), taps, bias))

    own_st.wait()
    for k in range(1, ROW):
        st_arrival(k).wait_recv()

    @pl.loop(0, ROW)
    def _(b):
        steps_of(b, 0)

    own_bc.wait()
    for k in range(1, ROW):
        bc_arrival(k, 0).wait_recv()

    for c in range(1, AHEAD):
        for k in range(1, ROW):
            x_copy(k, c).start()

    @pl.when(z < ROW - 1)
    def _():
        pl.semaphore_wait(carry_ok, 1)
        halo_bc(0, me + ROW).start()

    @pl.when(z > 0)
    def _():
        halo_bc(0, me).wait_recv()

    maps(0, keep_in)
    own_x.wait()

    def send_carry(c, state):
        cout[c] = state.astype(BF16)
        carry_copy(c, me + ROW).start()

    def block_states(c):
        for k in range(1, ROW):
            x_arrival(k, c).wait_recv()

        @pl.when(c < CHUNKS - AHEAD)
        def _():
            for k in range(1, ROW):
                x_copy(k, c + AHEAD).start()

        @pl.when(z < ROW - 1)
        def _():
            halo_x(c, me + ROW).start()

        @pl.when(z > 0)
        def _():
            halo_x(c, me).wait_recv()

        cols = cols_of(c)
        taps, bias = chan_taps(c)
        state = None
        for b in range(ROW):
            xin = xbuf[pl.ds(b * BLOCK, BLOCK + HALO), cols].astype(F32)
            low = conv_rows(xin, taps, bias).astype(BF16)
            xc[pl.ds(b * BLOCK, BLOCK), cols] = low
            weighted = (low.astype(F32) * wexp[pl.ds(b * BLOCK, BLOCK), cols]).astype(BF16)
            block_state = jnp.dot(bt[b], weighted, preferred_element_type=F32)
            state = block_state if b == 0 else gain(b, cols) * state + block_state
            if b < ROW - 1:
                local_s[b, :, cols] = state
            else:
                total_s[:, cols] = state

    def with_tail(new, tail):
        width = new.shape[-1]
        rows8[:, 0:STEPS, 0:width] = new
        rows8[:, STEPS:8, 0:width] = jnp.broadcast_to(tail[None], (RING, 8 - STEPS, width))
        return rows8[:, :, 0:width].reshape(BLOCK, width)

    def decode_inputs():
        for copy in own_dec:
            copy.wait()

        @pl.loop(0, RING)
        def _(s):
            @pl.when(s != me)
            def _():
                for copy in dec_copies(y, s):
                    copy.wait_recv()

        rows8[:, :, 0:BLOCK] = jnp.zeros((RING, 8, BLOCK), F32)
        rows8[:, 0:STEPS, 0:64] = decs[...]
        turn_s[...] = jnp.transpose(rows8[:, :, 0:BLOCK].reshape(BLOCK, BLOCK))
        st_s[ROW] = turn_s[pl.ds(pl.multiple_of(y * HEADS_Q, HEADS_Q), HEADS_Q)]
        steps_of(ROW, 1)
        end = pl.ds(ROW * BLOCK, HALO)
        for m, keep in ((0, keep_in), (1, keep_out)):
            taps, bias = map_taps(m)
            new = decm[:, :, m * STATE : (m + 1) * STATE].astype(F32)
            tail = bcbuf[end, half(m)].astype(F32)[STEPS:8]
            keep(ROW, conv_cyclic(with_tail(new, tail), taps, bias))

        @pl.loop(0, CHUNKS)
        def _(c):
            cols = cols_of(c)
            taps, bias = chan_taps(c)
            tail = xbuf[end, cols].astype(F32)[STEPS:8]
            conv = conv_cyclic(with_tail(decx[:, :, cols].astype(F32), tail), taps, bias)
            xc[pl.ds(ROW * BLOCK, BLOCK), cols] = conv.astype(BF16)
            inner_part(ROW, c)

    def inner_part(b, c):
        rows = pl.ds(b * BLOCK, BLOCK)
        score = scores[b]
        columns = cumcol[c, b]
        for pair in range(HEADS_C // 2):
            mixes = []
            for j in (2 * pair, 2 * pair + 1):
                head = c * HEADS_C + j
                row = cum_t[b, pl.ds(head, 1)]
                step = st_s[b, pl.ds(head, 1)]
                gap = columns[:, j : j + 1] - row
                mixes.append((score * jnp.exp(gap) * step).astype(BF16))
            mixing = jnp.concatenate(mixes, axis=1)
            cols = pl.ds(pl.multiple_of(c * WIDTH + pair * BLOCK, BLOCK), BLOCK)
            xp = xc[rows, cols].astype(F32)
            blockdiag = jnp.concatenate(
                [jnp.where(left, xp, 0.0).astype(BF16), jnp.where(left, 0.0, xp).astype(BF16)],
                axis=0,
            )
            inner = jnp.dot(mixing, blockdiag, preferred_element_type=F32)
            head = y * HEADS_Q + c * HEADS_C + 2 * pair
            skip = jnp.where(left[0:1], skip_s[pl.ds(head, 1)], skip_s[pl.ds(head + 1, 1)])
            yacc[rows, cols] = inner + skip * xp

    def leads_of(cols):
        leads = [gain(0, cols)]
        for b in range(1, ROW):
            leads.append(leads[-1] * gain(b, cols))
        return leads

    def forward(c):
        @pl.when(z > 0)
        def _():
            carry_copy(c, me).wait_recv()

        @pl.when(z < ROW - 1)
        def _():
            cols = cols_of(c)
            lead = leads_of(cols)[ROW - 1]
            send_carry(c, total_s[:, cols] + lead * cin[c].astype(F32))

    def outputs(c):
        cols = cols_of(c)
        leads = leads_of(cols)
        carry = cin[c].astype(F32)
        @pl.when(last)
        def _():
            final = total_s[:, cols] + leads[ROW - 1] * carry
            high = final.astype(BF16)
            rest = (final - high.astype(F32)).astype(BF16)
            rows = pl.ds(ROW * BLOCK, BLOCK)
            out_map = bcc[rows, half(1)]
            cross = jnp.dot(out_map, high, preferred_element_type=F32) + jnp.dot(
                out_map, rest, preferred_element_type=F32
            )
            result = yacc[rows, cols] + ecexp[rows, cols] * cross
            rows8[:, :, 0:WIDTH] = result.reshape(RING, 8, WIDTH)
            doutbuf[:, :, cols] = rows8[:, 0:STEPS, 0:WIDTH].astype(BF16)

            @pl.when(c % GROUP_CHUNKS == GROUP_CHUNKS - 1)
            def _():
                g = c // GROUP_CHUNKS
                dout_own(g).start()

                @pl.loop(0, RING)
                def _(s):
                    @pl.when(s != me)
                    def _():
                        dout_copy(s, g).start()

        for b in range(ROW):
            rows = pl.ds(b * BLOCK, BLOCK)
            if b == 0:
                entry = cin[c]
            else:
                entry = (local_s[b - 1, :, cols] + leads[b - 1] * carry).astype(BF16)
            cross = jnp.dot(bcc[rows, half(1)], entry, preferred_element_type=F32)
            outbuf[rows, cols] = (yacc[rows, cols] + ecexp[rows, cols] * cross).astype(BF16)
        out_own(c).start()
        for k in range(1, ROW):
            out_copy(k, c).start()

    send_decode()

    @pl.loop(0, CHUNKS + lag)
    def _(i):
        @pl.when(i < CHUNKS)
        def _():
            block_states(i)

        @pl.when(i == 4)
        def _():
            for k in range(1, ROW):
                bc_copy(k, 1).start()

        @pl.when(early & (i >= lag))
        def _():
            forward(i - lag)

    @pl.when((z == 0) & odd)
    def _():
        for c in range(CHUNKS):
            carry_copy(c, me + ROW).wait_send()
        signal_chip(turn_ok, 0)

    for k in range(1, ROW):
        bc_arrival(k, 1).wait_recv()

    @pl.when(z < ROW - 1)
    def _():
        halo_bc(1, me + ROW).start()

    @pl.when(z > 0)
    def _():
        halo_bc(1, me).wait_recv()

    maps(1, keep_out)

    @pl.loop(0, CHUNKS + wait)
    def _(i):
        @pl.when(i < CHUNKS)
        def _():
            for b in range(ROW):
                inner_part(b, i)

        @pl.when(last & (i == wait))
        def _():
            decode_inputs()

        @pl.when(~early & ~first & (i >= wait))
        def _():
            forward(i - wait)

        @pl.when(first & (i == 3))
        def _():
            pl.semaphore_wait(turn_ok, 2)

            @pl.loop(0, CHUNKS)
            def _(c):
                forward(c)

        @pl.when(i >= wait)
        def _():
            outputs(i - wait)

    @pl.loop(0, CHUNKS)
    def _(c):
        out_own(c).wait()
        for k in range(1, ROW):
            out_arrival(k, c).wait_recv()

    for g in range(GROUPS):
        for q in range(ROW):

            @pl.when(me != 12 + q)
            def _(q=q, g=g):
                dout_arrival(q, g).wait_recv()

        @pl.when(last)
        def _(g=g):
            dout_own(g).wait()

    for k in range(1, ROW):
        st_copy(k).wait_send()
        for m in range(2):
            bc_copy(k, m).wait_send()

    @pl.loop(0, CHUNKS)
    def _(c):
        for k in range(1, ROW):
            x_copy(k, c).wait_send()
            out_copy(k, c).wait_send()

        @pl.when(z < ROW - 1)
        def _():
            @pl.when((z > 0) | ~odd)
            def _():
                carry_copy(c, me + ROW).wait_send()

            halo_x(c, me + ROW).wait_send()

    @pl.when(last)
    def _():
        @pl.loop(0, RING)
        def _(s):
            @pl.when(s != me)
            def _():
                for g in range(GROUPS):
                    dout_copy(s, g).wait_send()

    @pl.when(z < ROW - 1)
    def _():
        for m in range(2):
            halo_bc(m, me + ROW).wait_send()

    for q in range(ROW):

        @pl.when(me != 12 + q)
        def _(q=q):
            for copy in dec_copies(q, me):
                copy.wait_send()


def local(
    heads_pre,
    maps_pre,
    step_prompt,
    head_rate,
    skip_gain,
    conv_head_taps,
    conv_head_bias,
    conv_map_taps,
    filter_mapping_offset,
    heads_dec,
    maps_dec,
    step_dec,
):
    tokens, channels = heads_pre.shape
    groups = maps_pre.shape[2] // STATE
    heads = step_prompt.shape[1]

    bc = jnp.concatenate(
        [maps_pre, maps_dec[0], jnp.zeros((8 - STEPS,) + maps_pre.shape[1:], BF16)], axis=0
    )
    bc = bc.reshape(tokens + 8, 2, groups, STATE).transpose(2, 0, 1, 3)
    bc = bc.reshape(groups, tokens + 8, 2 * STATE)
    steps = step_prompt.T.reshape(ROW, HEADS_Q, tokens)

    any_space = pl.BlockSpec(memory_space=pl.ANY)
    vmem = pl.BlockSpec(memory_space=pltpu.VMEM)
    dma = pltpu.SemaphoreType.DMA
    all_rows = (ROW + 1) * BLOCK
    out, dout = pl.pallas_call(
        kernel,
        out_shape=(
            jax.ShapeDtypeStruct((tokens, channels), BF16),
            jax.ShapeDtypeStruct((STEPS, channels), BF16),
        ),
        in_specs=[any_space] * 5 + [vmem] * 6,
        out_specs=(any_space, any_space),
        scratch_shapes=[
            pltpu.VMEM((HALO + ROW * BLOCK, CHAN_Q), BF16),
            pltpu.VMEM((HALO + ROW * BLOCK, 2 * STATE), BF16),
            pltpu.VMEM((ROW + 1, HEADS_Q, BLOCK), F32),
            pltpu.VMEM((RING, STEPS, CHAN_Q), BF16),
            pltpu.VMEM((RING, STEPS, 2 * STATE), BF16),
            pltpu.VMEM((RING, STEPS, heads), F32),
            pltpu.VMEM((RING, 8, STATE), F32),
            pltpu.VMEM((BLOCK, BLOCK), F32),
            pltpu.VMEM((BLOCK, BLOCK), F32),
            pltpu.VMEM((BLOCK, BLOCK), F32),
            pltpu.VMEM((all_rows, CHAN_Q), BF16),
            pltpu.VMEM((all_rows, 2 * STATE), BF16),
            pltpu.VMEM((ROW + 1, STATE, BLOCK), BF16),
            pltpu.VMEM((ROW + 1, BLOCK, BLOCK), F32),
            pltpu.VMEM((2, BLOCK, BLOCK), F32),
            pltpu.VMEM((2, BLOCK, BLOCK), F32),
            pltpu.VMEM((ROW + 1, HEADS_Q, BLOCK), F32),
            pltpu.VMEM((CHUNKS, ROW + 1, BLOCK, BLOCK), F32),
            pltpu.VMEM((all_rows, CHAN_Q), F32),
            pltpu.VMEM((all_rows, CHAN_Q), F32),
            pltpu.VMEM((all_rows, CHAN_Q), F32),
            pltpu.VMEM((ROW - 1, STATE, CHAN_Q), F32),
            pltpu.VMEM((STATE, CHAN_Q), F32),
            pltpu.VMEM((CHUNKS, STATE, WIDTH), BF16),
            pltpu.VMEM((CHUNKS, STATE, WIDTH), BF16),
            pltpu.VMEM((ROW * BLOCK, CHAN_Q), BF16),
            pltpu.VMEM((RING, STEPS, CHAN_Q), BF16),
            dma((6,)),
            dma((CHUNKS,)),
            dma((GROUPS,)),
            dma((ROW, CHUNKS)),
            dma((ROW, CHUNKS)),
            dma((ROW, 2)),
            dma((ROW, 2)),
            dma((ROW,)),
            dma((ROW,)),
            dma((CHUNKS + 2,)),
            dma((CHUNKS + 2,)),
            dma((3, ROW)),
            dma((3, RING)),
            dma((CHUNKS,)),
            dma((CHUNKS,)),
            dma((ROW, CHUNKS)),
            dma((ROW, CHUNKS)),
            dma((RING, GROUPS)),
            dma((ROW, GROUPS)),
            pltpu.SemaphoreType.REGULAR,
            pltpu.SemaphoreType.REGULAR,
            pltpu.SemaphoreType.REGULAR,
        ],
        compiler_params=pltpu.CompilerParams(
            collective_id=0, has_side_effects=True, vmem_limit_bytes=44 << 20
        ),
        name="scan_exchange",
    )(
        heads_pre,
        bc,
        steps,
        heads_dec[0],
        step_dec[0],
        conv_head_taps,
        conv_head_bias[None],
        conv_map_taps,
        filter_mapping_offset,
        head_rate[None],
        skip_gain[None],
    )
    return out, dout[None]


def solution(mesh):
    placed = (
        P(("prompt", "seq"), "head"),
        P(("prompt", "seq"), None, "head"),
        P(("prompt", "seq"), "head"),
        P("head"),
        P("head"),
        P(None, "head"),
        P("head"),
        P(None, None, "head"),
        P(None, "head"),
        P(("prompt", "seq"), None, "head"),
        P(("prompt", "seq"), None, None, "head"),
        P(("prompt", "seq"), None, "head"),
    )
    return jax.shard_map(
        local,
        mesh=mesh,
        in_specs=placed,
        out_specs=(P(("prompt", "seq"), "head"), P(("prompt", "seq"), None, "head")),
        check_vma=False,
    )
```

```python
import functools

import jax
import jax.numpy as jnp
from jax import lax
from jax.experimental import pallas as pl
from jax.experimental.pallas import tpu as pltpu
from jax.sharding import PartitionSpec as P

HEAD_DIM = 64
STATE = 256
CONV = 4
BLOCK = 128
STEPS = 4
ROW = 4
RING = 16
HEADS_Q = 16
CHAN_Q = HEADS_Q * HEAD_DIM
CHUNKS = 8
WIDTH = CHAN_Q // CHUNKS
HALO = 8
HEADS_C = HEADS_Q // CHUNKS
AHEAD = 3
GROUPS = 2
GROUP_CHUNKS = CHUNKS // GROUPS
MESH = pl.DeviceIdType.MESH
F32 = jnp.float32
BF16 = jnp.bfloat16
HIGH = lax.Precision.HIGHEST


def silu(v):
    return v * (1.0 / (1.0 + jnp.exp(-v)))


def iota(shape, dim):
    return lax.broadcasted_iota(jnp.int32, shape, dim)


def conv_rows(xin, taps, bias):
    total = bias + taps[0] * pltpu.roll(xin, 3, 0)[HALO:]
    total = total + taps[1] * pltpu.roll(xin, 2, 0)[HALO:]
    total = total + taps[2] * pltpu.roll(xin, 1, 0)[HALO:]
    total = total + taps[3] * xin[HALO:]
    return silu(total)


def conv_cyclic(xin, taps, bias):
    total = bias + taps[0] * pltpu.roll(xin, 3, 0)
    total = total + taps[1] * pltpu.roll(xin, 2, 0)
    total = total + taps[2] * pltpu.roll(xin, 1, 0)
    total = total + taps[3] * xin
    return silu(total)


def kernel(
    x_ref,
    bc_ref,
    st_ref,
    dec_ref,
    decs_ref,
    taps_ref,
    bias_ref,
    mtaps_ref,
    mbias_ref,
    rate_ref,
    skip_ref,
    out_ref,
    dout_ref,
    xbuf,
    bcbuf,
    st_s,
    decx,
    decm,
    decs,
    rows8,
    rate_s,
    skip_s,
    turn_s,
    xc,
    bcc,
    bt,
    scores,
    tri,
    keep_s,
    cum_t,
    cumcol,
    wexp,
    ecexp,
    yacc,
    local_s,
    total_s,
    cin,
    cout,
    outbuf,
    doutbuf,
    lsem,
    lout_sem,
    ldo_sem,
    sx,
    rx,
    sbc,
    rbc,
    sst,
    rst,
    shalo,
    rhalo,
    sdec,
    rdec,
    scar,
    rcar,
    sout,
    rout,
    sdo,
    rdo,
    carry_ok,
    dec_ok,
    turn_ok,
):
    me = lax.axis_index("seq")
    z = me // ROW
    y = me % ROW
    group = y // 2
    base = ROW * z
    last = z == ROW - 1
    prompt = lax.axis_index("prompt")
    odd = prompt // 2 == 1
    early = odd & ~last
    lag = jnp.where(early, z, 0)
    first = (z == 0) & ~odd
    wait = jnp.where(odd | first, 0, CHUNKS)

    def row_peer(k):
        return lax.rem(y + k, ROW)

    def from_peer(k):
        return lax.rem(y + ROW - k, ROW)

    def rows_of(b):
        return pl.ds(pl.multiple_of(b * BLOCK, BLOCK), BLOCK)

    def in_rows(b):
        return pl.ds(pl.multiple_of(HALO + b * BLOCK, HALO), BLOCK)

    def cols_of(c):
        return pl.ds(pl.multiple_of(c * WIDTH, WIDTH), WIDTH)

    def quarter_cols(q, c):
        return pl.ds(pl.multiple_of(q * CHAN_Q + c * WIDTH, WIDTH), WIDTH)

    def quarter(q):
        return pl.ds(pl.multiple_of(q * CHAN_Q, CHAN_Q), CHAN_Q)

    def half(m):
        return pl.ds(m * STATE, STATE)

    prompt_rows = pl.ds(0, BLOCK)
    end_rows = pl.ds(ROW * BLOCK, HALO)
    dec_rows = pl.ds(BLOCK, STEPS)
    before = pl.ds(0, HALO)

    def remote(src, dst, send, recv, seq):
        return pltpu.make_async_remote_copy(
            src_ref=src,
            dst_ref=dst,
            send_sem=send,
            recv_sem=recv,
            device_id={"seq": seq},
            device_id_type=MESH,
        )

    def x_copy(k, c):
        q = row_peer(k)
        return remote(
            x_ref.at[:, quarter_cols(q, c)],
            xbuf.at[in_rows(y), cols_of(c)],
            sx.at[k, c],
            rx.at[k, c],
            base + q,
        )

    def x_arrival(k, c):
        src = from_peer(k)
        return remote(
            x_ref.at[:, quarter_cols(y, c)],
            xbuf.at[in_rows(src), cols_of(c)],
            sx.at[k, c],
            rx.at[k, c],
            base + src,
        )

    def bc_copy(k, m):
        q = row_peer(k)
        return remote(
            bc_ref.at[q // 2, prompt_rows, half(m)],
            bcbuf.at[in_rows(y), half(m)],
            sbc.at[k, m],
            rbc.at[k, m],
            base + q,
        )

    def bc_arrival(k, m):
        src = from_peer(k)
        return remote(
            bc_ref.at[group, prompt_rows, half(m)],
            bcbuf.at[in_rows(src), half(m)],
            sbc.at[k, m],
            rbc.at[k, m],
            base + src,
        )

    def st_copy(k):
        q = row_peer(k)
        return remote(st_ref.at[q], st_s.at[y], sst.at[k], rst.at[k], base + q)

    def st_arrival(k):
        src = from_peer(k)
        return remote(st_ref.at[y], st_s.at[src], sst.at[k], rst.at[k], base + src)

    def halo_x(c, seq):
        cols = cols_of(c)
        return remote(
            xbuf.at[end_rows, cols], xbuf.at[before, cols], shalo.at[c], rhalo.at[c], seq
        )

    def halo_bc(m, seq):
        return remote(
            bcbuf.at[end_rows, half(m)],
            bcbuf.at[before, half(m)],
            shalo.at[CHUNKS + m],
            rhalo.at[CHUNKS + m],
            seq,
        )

    def dec_copies(q, sample):
        parts = (
            (dec_ref.at[:, quarter(q)], decx.at[sample]),
            (bc_ref.at[q // 2, dec_rows], decm.at[sample]),
            (decs_ref, decs.at[sample]),
        )
        return [
            remote(src, dst, sdec.at[i, q], rdec.at[i, sample], 12 + q)
            for i, (src, dst) in enumerate(parts)
        ]

    own_dec = [
        pltpu.make_async_copy(dec_ref.at[:, quarter(y)], decx.at[me], lsem.at[3]),
        pltpu.make_async_copy(bc_ref.at[group, dec_rows], decm.at[me], lsem.at[4]),
        pltpu.make_async_copy(decs_ref, decs.at[me], lsem.at[5]),
    ]

    def carry_copy(c, seq):
        return remote(cout.at[c], cin.at[c], scar.at[c], rcar.at[c], seq)

    def out_copy(k, c):
        b = row_peer(k)
        return remote(
            outbuf.at[rows_of(b), cols_of(c)],
            out_ref.at[:, quarter_cols(y, c)],
            sout.at[k, c],
            rout.at[k, c],
            base + b,
        )

    def out_arrival(k, c):
        src = from_peer(k)
        return remote(
            outbuf.at[rows_of(y), cols_of(c)],
            out_ref.at[:, quarter_cols(src, c)],
            sout.at[k, c],
            rout.at[k, c],
            base + src,
        )

    def out_own(c):
        return pltpu.make_async_copy(
            outbuf.at[rows_of(y), cols_of(c)], out_ref.at[:, quarter_cols(y, c)], lout_sem.at[c]
        )

    def group_cols(q, g):
        size = CHAN_Q // GROUPS
        return pl.ds(pl.multiple_of(q * CHAN_Q + g * size, size), size)

    def dout_copy(sample, g):
        return remote(
            doutbuf.at[sample, :, group_cols(0, g)],
            dout_ref.at[:, group_cols(y, g)],
            sdo.at[sample, g],
            rdo.at[y, g],
            sample,
        )

    def dout_arrival(q, g):
        return remote(
            doutbuf.at[me, :, group_cols(0, g)],
            dout_ref.at[:, group_cols(q, g)],
            sdo.at[me, g],
            rdo.at[q, g],
            12 + q,
        )

    def dout_own(g):
        return pltpu.make_async_copy(
            doutbuf.at[me, :, group_cols(0, g)], dout_ref.at[:, group_cols(y, g)], ldo_sem.at[g]
        )

    own_x = pltpu.make_async_copy(x_ref.at[:, quarter(y)], xbuf.at[in_rows(y)], lsem.at[0])
    own_bc = pltpu.make_async_copy(bc_ref.at[group, prompt_rows], bcbuf.at[in_rows(y)], lsem.at[1])
    own_st = pltpu.make_async_copy(st_ref.at[y], st_s.at[y], lsem.at[2])

    def signal(sem, seq):
        pl.semaphore_signal(sem, inc=1, device_id={"seq": seq}, device_id_type=MESH)

    barrier = pltpu.get_barrier_semaphore()
    for k in range(1, ROW):
        signal(barrier, base + row_peer(k))

    def signal_chip(sem, first):
        for core in range(2):
            pl.semaphore_signal(
                sem, inc=1, device_id={"prompt": first + core}, device_id_type=MESH
            )

    @pl.when((z == 0) & ~odd)
    def _():
        signal_chip(barrier, 2)

    own_st.start()
    own_bc.start()
    own_x.start()

    @pl.when(last)
    def _():
        for copy in own_dec:
            copy.start()

    r_i, c_i = iota((BLOCK, BLOCK), 0), iota((BLOCK, BLOCK), 1)
    same = (r_i // 8) == (c_i // 8)
    left = c_i < HEAD_DIM
    tri[0] = jnp.where(r_i <= c_i, 1.0, 0.0).astype(F32)
    tri[1] = jnp.where((r_i <= c_i) & same, 1.0, 0.0).astype(F32)
    keep_s[0] = jnp.where(r_i >= c_i, 1.0, 0.0).astype(F32)
    keep_s[1] = jnp.where((r_i >= c_i) & same, 1.0, 0.0).astype(F32)

    def spread(ref):
        wide = jnp.broadcast_to(ref[...], (BLOCK, ref.shape[1]))
        return jnp.transpose(jnp.concatenate([wide, wide], axis=1))

    rate_s[...] = spread(rate_ref)
    skip_s[...] = spread(skip_ref)

    @pl.when(z == 0)
    def _():
        xbuf[before] = jnp.zeros((HALO, CHAN_Q), BF16)
        bcbuf[before] = jnp.zeros((HALO, 2 * STATE), BF16)
        cin[...] = jnp.zeros_like(cin)

    pl.semaphore_wait(barrier, jnp.where(z > 0, ROW, jnp.where(odd, ROW + 1, ROW - 1)))

    @pl.when(z < ROW - 1)
    def _():
        signal(barrier, me + ROW)

    for k in range(1, ROW):
        st_copy(k).start()
    for k in range(1, ROW):
        bc_copy(k, 0).start()
    for k in range(1, ROW):
        x_copy(k, 0).start()

    @pl.when(z > 0)
    def _():
        signal(carry_ok, me - ROW)

    @pl.when(last)
    def _():
        @pl.loop(0, RING)
        def _(s):
            @pl.when(s != me)
            def _():
                signal(dec_ok, s)

    def send_decode():
        pl.semaphore_wait(dec_ok, jnp.where(last, ROW - 1, ROW))

        for q in range(ROW):

            @pl.when(me != 12 + q)
            def _(q=q):
                for copy in dec_copies(q, me):
                    copy.start()

    def steps_of(b, m):
        step = st_s[b]
        drop = -(step * rate_s[pl.ds(pl.multiple_of(y * HEADS_Q, HEADS_Q), HEADS_Q)])
        cum = jnp.dot(drop, tri[m], precision=HIGH, preferred_element_type=F32)
        cum_t[b] = cum
        weight = jnp.exp(cum[:, BLOCK - 1 : BLOCK] - cum) * step
        stack = jnp.concatenate(
            [cum, weight, jnp.exp(cum), jnp.zeros((BLOCK - 3 * HEADS_Q, BLOCK), F32)], axis=0
        )
        turned = jnp.transpose(stack)
        for c in range(CHUNKS):
            shift = (BLOCK - c * HEADS_C) % BLOCK
            cumcol[c, b] = pltpu.roll(turned, shift, 1) if shift else turned
        for j in range(HEADS_Q // 2):
            cols = pl.ds(j * BLOCK, BLOCK)

            def pair(first):
                one = jnp.broadcast_to(turned[:, first : first + 1], (BLOCK, BLOCK))
                two = jnp.broadcast_to(turned[:, first + 1 : first + 2], (BLOCK, BLOCK))
                return jnp.where(left, one, two)

            wexp[rows_of(b), cols] = pair(HEADS_Q + 2 * j)
            ecexp[rows_of(b), cols] = pair(2 * HEADS_Q + 2 * j)

    map_cols = pl.ds(pl.multiple_of(group * STATE, STATE), STATE)

    def map_taps(m):
        return [mtaps_ref[j, pl.ds(m, 1), map_cols] for j in range(CONV)], mbias_ref[
            pl.ds(m, 1), map_cols
        ]

    def keep_in(b, conv):
        bcc[rows_of(b), half(0)] = conv.astype(BF16)
        bt[b] = jnp.transpose(conv).astype(BF16)

    def keep_out(b, conv):
        low = conv.astype(BF16)
        bcc[rows_of(b), half(1)] = low
        score = lax.dot_general(
            low, bcc[rows_of(b), half(0)], (((1,), (1,)), ((), ())), preferred_element_type=F32
        )
        scores[b] = score * keep_s[b // ROW]

    def chan_taps(c):
        cols = quarter_cols(y, c)
        return [taps_ref[pl.ds(j, 1), cols] for j in range(CONV)], bias_ref[:, cols]

    def gain(b, cols):
        return ecexp[pl.ds(b * BLOCK + BLOCK - 1, 1), cols]

    def maps(m, keep):
        taps, bias = map_taps(m)

        @pl.loop(0, ROW)
        def _(b):
            rows = pl.ds(pl.multiple_of(b * BLOCK, BLOCK), BLOCK + HALO)
            keep(b, conv_rows(bcbuf[rows, half(m)].astype(F32), taps, bias))

    own_st.wait()
    for k in range(1, ROW):
        st_arrival(k).wait_recv()

    @pl.loop(0, ROW)
    def _(b):
        steps_of(b, 0)

    own_bc.wait()
    for k in range(1, ROW):
        bc_arrival(k, 0).wait_recv()

    for c in range(1, AHEAD):
        for k in range(1, ROW):
            x_copy(k, c).start()

    @pl.when(z < ROW - 1)
    def _():
        pl.semaphore_wait(carry_ok, 1)
        halo_bc(0, me + ROW).start()

    @pl.when(z > 0)
    def _():
        halo_bc(0, me).wait_recv()

    maps(0, keep_in)
    own_x.wait()

    def send_carry(c, state):
        cout[c] = state.astype(BF16)
        carry_copy(c, me + ROW).start()

    def block_states(c):
        for k in range(1, ROW):
            x_arrival(k, c).wait_recv()

        @pl.when(c < CHUNKS - AHEAD)
        def _():
            for k in range(1, ROW):
                x_copy(k, c + AHEAD).start()

        @pl.when(z < ROW - 1)
        def _():
            halo_x(c, me + ROW).start()

        @pl.when(z > 0)
        def _():
            halo_x(c, me).wait_recv()

        cols = cols_of(c)
        taps, bias = chan_taps(c)
        state = None
        for b in range(ROW):
            xin = xbuf[pl.ds(b * BLOCK, BLOCK + HALO), cols].astype(F32)
            low = conv_rows(xin, taps, bias).astype(BF16)
            xc[pl.ds(b * BLOCK, BLOCK), cols] = low
            weighted = (low.astype(F32) * wexp[pl.ds(b * BLOCK, BLOCK), cols]).astype(BF16)
            block_state = jnp.dot(bt[b], weighted, preferred_element_type=F32)
            state = block_state if b == 0 else gain(b, cols) * state + block_state
            if b < ROW - 1:
                local_s[b, :, cols] = state
            else:
                total_s[:, cols] = state

    def with_tail(new, tail):
        width = new.shape[-1]
        rows8[:, 0:STEPS, 0:width] = new
        rows8[:, STEPS:8, 0:width] = jnp.broadcast_to(tail[None], (RING, 8 - STEPS, width))
        return rows8[:, :, 0:width].reshape(BLOCK, width)

    def decode_inputs():
        for copy in own_dec:
            copy.wait()

        @pl.loop(0, RING)
        def _(s):
            @pl.when(s != me)
            def _():
                for copy in dec_copies(y, s):
                    copy.wait_recv()

        rows8[:, :, 0:BLOCK] = jnp.zeros((RING, 8, BLOCK), F32)
        rows8[:, 0:STEPS, 0:64] = decs[...]
        turn_s[...] = jnp.transpose(rows8[:, :, 0:BLOCK].reshape(BLOCK, BLOCK))
        st_s[ROW] = turn_s[pl.ds(pl.multiple_of(y * HEADS_Q, HEADS_Q), HEADS_Q)]
        steps_of(ROW, 1)
        end = pl.ds(ROW * BLOCK, HALO)
        for m, keep in ((0, keep_in), (1, keep_out)):
            taps, bias = map_taps(m)
            new = decm[:, :, m * STATE : (m + 1) * STATE].astype(F32)
            tail = bcbuf[end, half(m)].astype(F32)[STEPS:8]
            keep(ROW, conv_cyclic(with_tail(new, tail), taps, bias))

        @pl.loop(0, CHUNKS)
        def _(c):
            cols = cols_of(c)
            taps, bias = chan_taps(c)
            tail = xbuf[end, cols].astype(F32)[STEPS:8]
            conv = conv_cyclic(with_tail(decx[:, :, cols].astype(F32), tail), taps, bias)
            xc[pl.ds(ROW * BLOCK, BLOCK), cols] = conv.astype(BF16)
            inner_part(ROW, c)

    def inner_part(b, c):
        rows = pl.ds(b * BLOCK, BLOCK)
        score = scores[b]
        columns = cumcol[c, b]
        for pair in range(HEADS_C // 2):
            mixes = []
            for j in (2 * pair, 2 * pair + 1):
                head = c * HEADS_C + j
                row = cum_t[b, pl.ds(head, 1)]
                step = st_s[b, pl.ds(head, 1)]
                gap = columns[:, j : j + 1] - row
                mixes.append((score * jnp.exp(gap) * step).astype(BF16))
            mixing = jnp.concatenate(mixes, axis=1)
            cols = pl.ds(pl.multiple_of(c * WIDTH + pair * BLOCK, BLOCK), BLOCK)
            xp = xc[rows, cols].astype(F32)
            blockdiag = jnp.concatenate(
                [jnp.where(left, xp, 0.0).astype(BF16), jnp.where(left, 0.0, xp).astype(BF16)],
                axis=0,
            )
            inner = jnp.dot(mixing, blockdiag, preferred_element_type=F32)
            head = y * HEADS_Q + c * HEADS_C + 2 * pair
            skip = jnp.where(left[0:1], skip_s[pl.ds(head, 1)], skip_s[pl.ds(head + 1, 1)])
            yacc[rows, cols] = inner + skip * xp

    def leads_of(cols):
        leads = [gain(0, cols)]
        for b in range(1, ROW):
            leads.append(leads[-1] * gain(b, cols))
        return leads

    def forward(c):
        @pl.when(z > 0)
        def _():
            carry_copy(c, me).wait_recv()

        @pl.when(z < ROW - 1)
        def _():
            cols = cols_of(c)
            lead = leads_of(cols)[ROW - 1]
            send_carry(c, total_s[:, cols] + lead * cin[c].astype(F32))

    def outputs(c):
        cols = cols_of(c)
        leads = leads_of(cols)
        carry = cin[c].astype(F32)
        @pl.when(last)
        def _():
            final = total_s[:, cols] + leads[ROW - 1] * carry
            high = final.astype(BF16)
            rest = (final - high.astype(F32)).astype(BF16)
            rows = pl.ds(ROW * BLOCK, BLOCK)
            out_map = bcc[rows, half(1)]
            cross = jnp.dot(out_map, high, preferred_element_type=F32) + jnp.dot(
                out_map, rest, preferred_element_type=F32
            )
            result = yacc[rows, cols] + ecexp[rows, cols] * cross
            rows8[:, :, 0:WIDTH] = result.reshape(RING, 8, WIDTH)
            doutbuf[:, :, cols] = rows8[:, 0:STEPS, 0:WIDTH].astype(BF16)

            @pl.when(c % GROUP_CHUNKS == GROUP_CHUNKS - 1)
            def _():
                g = c // GROUP_CHUNKS
                dout_own(g).start()

                @pl.loop(0, RING)
                def _(s):
                    @pl.when(s != me)
                    def _():
                        dout_copy(s, g).start()

        for b in range(ROW):
            rows = pl.ds(b * BLOCK, BLOCK)
            if b == 0:
                entry = cin[c]
            else:
                entry = (local_s[b - 1, :, cols] + leads[b - 1] * carry).astype(BF16)
            cross = jnp.dot(bcc[rows, half(1)], entry, preferred_element_type=F32)
            outbuf[rows, cols] = (yacc[rows, cols] + ecexp[rows, cols] * cross).astype(BF16)
        out_own(c).start()
        for k in range(1, ROW):
            out_copy(k, c).start()

    send_decode()

    @pl.loop(0, CHUNKS + lag)
    def _(i):
        @pl.when(i < CHUNKS)
        def _():
            block_states(i)

        @pl.when(i == 5)
        def _():
            for k in range(1, ROW):
                bc_copy(k, 1).start()

        @pl.when(early & (i >= lag))
        def _():
            forward(i - lag)

    @pl.when((z == 0) & odd)
    def _():
        for c in range(CHUNKS):
            carry_copy(c, me + ROW).wait_send()
        signal_chip(turn_ok, 0)

    for k in range(1, ROW):
        bc_arrival(k, 1).wait_recv()

    @pl.when(z < ROW - 1)
    def _():
        halo_bc(1, me + ROW).start()

    @pl.when(z > 0)
    def _():
        halo_bc(1, me).wait_recv()

    maps(1, keep_out)

    @pl.loop(0, CHUNKS + wait)
    def _(i):
        @pl.when(i < CHUNKS)
        def _():
            for b in range(ROW):
                inner_part(b, i)

        @pl.when(last & (i == wait))
        def _():
            decode_inputs()

        @pl.when(~early & ~first & (i >= wait))
        def _():
            forward(i - wait)

        @pl.when(first & (i == 3))
        def _():
            pl.semaphore_wait(turn_ok, 2)

            @pl.loop(0, CHUNKS)
            def _(c):
                forward(c)

        @pl.when(i >= wait)
        def _():
            outputs(i - wait)

    @pl.loop(0, CHUNKS)
    def _(c):
        out_own(c).wait()
        for k in range(1, ROW):
            out_arrival(k, c).wait_recv()

    for g in range(GROUPS):
        for q in range(ROW):

            @pl.when(me != 12 + q)
            def _(q=q, g=g):
                dout_arrival(q, g).wait_recv()

        @pl.when(last)
        def _(g=g):
            dout_own(g).wait()

    for k in range(1, ROW):
        st_copy(k).wait_send()
        for m in range(2):
            bc_copy(k, m).wait_send()

    @pl.loop(0, CHUNKS)
    def _(c):
        for k in range(1, ROW):
            x_copy(k, c).wait_send()
            out_copy(k, c).wait_send()

        @pl.when(z < ROW - 1)
        def _():
            @pl.when((z > 0) | ~odd)
            def _():
                carry_copy(c, me + ROW).wait_send()

            halo_x(c, me + ROW).wait_send()

    @pl.when(last)
    def _():
        @pl.loop(0, RING)
        def _(s):
            @pl.when(s != me)
            def _():
                for g in range(GROUPS):
                    dout_copy(s, g).wait_send()

    @pl.when(z < ROW - 1)
    def _():
        for m in range(2):
            halo_bc(m, me + ROW).wait_send()

    for q in range(ROW):

        @pl.when(me != 12 + q)
        def _(q=q):
            for copy in dec_copies(q, me):
                copy.wait_send()


def local(
    heads_pre,
    maps_pre,
    step_prompt,
    head_rate,
    skip_gain,
    conv_head_taps,
    conv_head_bias,
    conv_map_taps,
    filter_mapping_offset,
    heads_dec,
    maps_dec,
    step_dec,
):
    tokens, channels = heads_pre.shape
    groups = maps_pre.shape[2] // STATE
    heads = step_prompt.shape[1]

    bc = jnp.concatenate(
        [maps_pre, maps_dec[0], jnp.zeros((8 - STEPS,) + maps_pre.shape[1:], BF16)], axis=0
    )
    bc = bc.reshape(tokens + 8, 2, groups, STATE).transpose(2, 0, 1, 3)
    bc = bc.reshape(groups, tokens + 8, 2 * STATE)
    steps = step_prompt.T.reshape(ROW, HEADS_Q, tokens)

    any_space = pl.BlockSpec(memory_space=pl.ANY)
    vmem = pl.BlockSpec(memory_space=pltpu.VMEM)
    dma = pltpu.SemaphoreType.DMA
    all_rows = (ROW + 1) * BLOCK
    out, dout = pl.pallas_call(
        kernel,
        out_shape=(
            jax.ShapeDtypeStruct((tokens, channels), BF16),
            jax.ShapeDtypeStruct((STEPS, channels), BF16),
        ),
        in_specs=[any_space] * 5 + [vmem] * 6,
        out_specs=(any_space, any_space),
        scratch_shapes=[
            pltpu.VMEM((HALO + ROW * BLOCK, CHAN_Q), BF16),
            pltpu.VMEM((HALO + ROW * BLOCK, 2 * STATE), BF16),
            pltpu.VMEM((ROW + 1, HEADS_Q, BLOCK), F32),
            pltpu.VMEM((RING, STEPS, CHAN_Q), BF16),
            pltpu.VMEM((RING, STEPS, 2 * STATE), BF16),
            pltpu.VMEM((RING, STEPS, heads), F32),
            pltpu.VMEM((RING, 8, STATE), F32),
            pltpu.VMEM((BLOCK, BLOCK), F32),
            pltpu.VMEM((BLOCK, BLOCK), F32),
            pltpu.VMEM((BLOCK, BLOCK), F32),
            pltpu.VMEM((all_rows, CHAN_Q), BF16),
            pltpu.VMEM((all_rows, 2 * STATE), BF16),
            pltpu.VMEM((ROW + 1, STATE, BLOCK), BF16),
            pltpu.VMEM((ROW + 1, BLOCK, BLOCK), F32),
            pltpu.VMEM((2, BLOCK, BLOCK), F32),
            pltpu.VMEM((2, BLOCK, BLOCK), F32),
            pltpu.VMEM((ROW + 1, HEADS_Q, BLOCK), F32),
            pltpu.VMEM((CHUNKS, ROW + 1, BLOCK, BLOCK), F32),
            pltpu.VMEM((all_rows, CHAN_Q), F32),
            pltpu.VMEM((all_rows, CHAN_Q), F32),
            pltpu.VMEM((all_rows, CHAN_Q), F32),
            pltpu.VMEM((ROW - 1, STATE, CHAN_Q), F32),
            pltpu.VMEM((STATE, CHAN_Q), F32),
            pltpu.VMEM((CHUNKS, STATE, WIDTH), BF16),
            pltpu.VMEM((CHUNKS, STATE, WIDTH), BF16),
            pltpu.VMEM((ROW * BLOCK, CHAN_Q), BF16),
            pltpu.VMEM((RING, STEPS, CHAN_Q), BF16),
            dma((6,)),
            dma((CHUNKS,)),
            dma((GROUPS,)),
            dma((ROW, CHUNKS)),
            dma((ROW, CHUNKS)),
            dma((ROW, 2)),
            dma((ROW, 2)),
            dma((ROW,)),
            dma((ROW,)),
            dma((CHUNKS + 2,)),
            dma((CHUNKS + 2,)),
            dma((3, ROW)),
            dma((3, RING)),
            dma((CHUNKS,)),
            dma((CHUNKS,)),
            dma((ROW, CHUNKS)),
            dma((ROW, CHUNKS)),
            dma((RING, GROUPS)),
            dma((ROW, GROUPS)),
            pltpu.SemaphoreType.REGULAR,
            pltpu.SemaphoreType.REGULAR,
            pltpu.SemaphoreType.REGULAR,
        ],
        compiler_params=pltpu.CompilerParams(
            collective_id=0, has_side_effects=True, vmem_limit_bytes=44 << 20
        ),
        name="scan_exchange",
    )(
        heads_pre,
        bc,
        steps,
        heads_dec[0],
        step_dec[0],
        conv_head_taps,
        conv_head_bias[None],
        conv_map_taps,
        filter_mapping_offset,
        head_rate[None],
        skip_gain[None],
    )
    return out, dout[None]


def solution(mesh):
    placed = (
        P(("prompt", "seq"), "head"),
        P(("prompt", "seq"), None, "head"),
        P(("prompt", "seq"), "head"),
        P("head"),
        P("head"),
        P(None, "head"),
        P("head"),
        P(None, None, "head"),
        P(None, "head"),
        P(("prompt", "seq"), None, "head"),
        P(("prompt", "seq"), None, None, "head"),
        P(("prompt", "seq"), None, "head"),
    )
    return jax.shard_map(
        local,
        mesh=mesh,
        in_specs=placed,
        out_specs=(P(("prompt", "seq"), "head"), P(("prompt", "seq"), None, "head")),
        check_vma=False,
    )
```
